32 devices in a mesh: fsdp: 4 (over y, x), ctx: 4 (over z), tp: 2 (over core).
Axes of the slice: x: 2, y: 2, z: 4, core: 2. Of those that a mesh axis runs over, the one named last changes fastest.
Arguments:
- tokens: bfloat16 [8, 1024, 2048], P('fsdp', 'ctx'), may hold values from -6 to 6
- cotangent: bfloat16 [8, 1024, 2048], P('fsdp', 'ctx'), may hold values from -6 to 6
- prefix_len: int32 [8], P('fsdp'), may hold values from 102 to 512
- group_order: int32 [8], replicated, may hold values from 0 to 7, each once
- ln_gain: bfloat16 [2048], replicated, may hold values from 0.25 to 1.75
- ln_bias: bfloat16 [2048], replicated, may hold values from -4 to 4
- query_weight: bfloat16 [2048, 2048], P('fsdp', 'tp'), may hold values from -0.125 to 0.125
- query_bias: bfloat16 [2048], P('tp'), may hold values from -4 to 4
- key_weight: bfloat16 [2048, 2048], P('fsdp', 'tp'), may hold values from -0.125 to 0.125
- key_bias: bfloat16 [2048], P('tp'), may hold values from -4 to 4
- value_weight: bfloat16 [2048, 2048], P('fsdp', 'tp'), may hold values from -0.125 to 0.125
- value_bias: bfloat16 [2048], P('tp'), may hold values from -4 to 4
- out_weight: bfloat16 [2048, 2048], P('fsdp', 'tp'), may hold values from -1 to 1
- out_bias: bfloat16 [2048], replicated, may hold values from -4 to 4
- up_weight: bfloat16 [2048, 8192], P('fsdp', 'tp'), may hold values from -0.125 to 0.125
- up_bias: bfloat16 [8192], P('tp'), may hold values from -4 to 4
- down_weight: bfloat16 [2048, 8192], P('fsdp', 'tp'), may hold values from -0.0625 to 0.0625
- down_bias: bfloat16 [2048], replicated, may hold values from -4 to 4
Outputs:
- output: bfloat16 [8, 1024, 2048], P('fsdp', 'ctx')
- input_grad: bfloat16 [8, 1024, 2048], P('fsdp', 'ctx')
- ln_gain_grad: float32 [2048], replicated
- ln_bias_grad: float32 [2048], replicated
- query_weight_grad: float32 [2048, 2048], P('fsdp', 'tp')
- query_bias_grad: float32 [2048], P('tp')
- key_weight_grad: float32 [2048, 2048], P('fsdp', 'tp')
- key_bias_grad: float32 [2048], P('tp')
- value_weight_grad: float32 [2048, 2048], P('fsdp', 'tp')
- value_bias_grad: float32 [2048], P('tp')
- out_weight_grad: float32 [2048, 2048], P('fsdp', 'tp')
- up_weight_grad: float32 [2048, 8192], P('fsdp', 'tp')
- up_bias_grad: float32 [8192], P('tp')
- down_weight_grad: float32 [2048, 8192], P('fsdp', 'tp')
- out_biases_grad: float32 [2048], replicated
The draws below stay inside these ranges and needn't reach their ends.
Inputs may be any that keep to these rules, and one draw needn't show every extreme that they name: Each number of 0 to 7 appears once; storage rows k * 128 to k * 128 + 127 of every sequence hold positions group_order[k] * 128 onwards.
All inputs are finite; a program needn't handle non-finite values.
Results may differ from the reference program's by a relative error of at most 0.012.
Values may be sent and summed in bfloat16 or wider, within the bound.
No kernel may reach another device: no remote copies, remote signals or barrier semaphores. Data moves between devices by JAX's collectives and lax.ppermute only.
A program may use at most 448 MiB of HBM per device.

```python
import jax
import jax.numpy as jnp
from jax import lax

D = 2048
FF = 8192
HEADS = 32
HD = 64
ROT = 32
SEQ_LEN = 1024
GROUPS = 8
GROUP = 128
SEQS = 8


def plant(array, stream_key, low, top_value):
    longest = array.shape.index(max(array.shape))
    spots = []
    for shift in (0, 1):
        where = [jax.random.randint(jax.random.fold_in(stream_key, axis), (), 0, length) for axis, length in enumerate(array.shape)]
        where[longest] = (where[longest] + shift) % array.shape[longest]
        spots.append(tuple(where))
    return array.at[spots[0]].set(low).at[spots[1]].set(top_value)


def levels(rng, extent, cuts, smallest, top_value):
    level, own = 1.0, jax.random.fold_in(rng, 6)
    for axis_at, parts in cuts:
        draws = jnp.exp(jax.random.uniform(jax.random.fold_in(own, axis_at), (parts,), jnp.float32, smallest / len(cuts), top_value / len(cuts)))
        level = level * jnp.repeat(draws, extent[axis_at] // parts).reshape([-1 if axis == axis_at else 1 for axis in range(len(extent))])
    return level


def bell_draw(rng, dims, spread, reach, shards=(), kind=jnp.bfloat16):
    values = spread * jax.random.normal(rng, dims, jnp.float32)
    if shards:
        values = values * levels(rng, dims, shards, -0.22, 0.18)
    return jnp.clip(values, -reach, reach).astype(kind)


def setup_inputs(seed: int = 0) -> dict:
    streams_of = jax.random.split(jax.random.key(seed), 19)
    tokens = bell_draw(streams_of[0], (SEQS, SEQ_LEN, D), 1.0, 6.0, ((0, 4), (1, 4)))
    cotangent = bell_draw(streams_of[1], (SEQS, SEQ_LEN, D), 1.0, 6.0, ((0, 4), (1, 4)))
    prefix_len = plant(jax.random.randint(streams_of[2], (SEQS,), SEQ_LEN // 10, SEQ_LEN // 2 + 1), jax.random.fold_in(streams_of[2], 1), SEQ_LEN // 10, (SEQ_LEN // 2 + 1) - 1).astype(jnp.int32)
    group_order = jax.random.permutation(streams_of[3], GROUPS).astype(jnp.int32)
    ln_gain = jnp.clip(1.0 + 0.15 * jax.random.normal(streams_of[4], (D,), jnp.float32), 0.25, 1.75).astype(jnp.bfloat16)
    ln_bias = bell_draw(streams_of[5], (D,), 0.3, 4.0)
    query_weight = bell_draw(streams_of[6], (D, D), D ** -0.5, 0.125, ((0, 4), (1, 2)))
    query_bias = bell_draw(streams_of[7], (D,), 0.3, 4.0, ((0, 2),))
    key_weight = bell_draw(streams_of[8], (D, D), D ** -0.5, 0.125, ((0, 4), (1, 2)))
    key_bias = bell_draw(streams_of[9], (D,), 0.3, 4.0, ((0, 2),))
    value_weight = bell_draw(streams_of[10], (D, D), D ** -0.5, 0.125, ((0, 4), (1, 2)))
    value_bias = bell_draw(streams_of[11], (D,), 0.3, 4.0, ((0, 2),))
    out_weight = bell_draw(streams_of[12], (D, D), (D // 64) ** -0.5, 1.0, ((0, 4), (1, 2)))
    out_bias = bell_draw(streams_of[13], (D,), 0.3, 4.0)
    up_weight = bell_draw(streams_of[14], (D, FF), D ** -0.5, 0.125, ((0, 4), (1, 2)))
    up_bias = bell_draw(streams_of[15], (FF,), 0.3, 4.0, ((0, 2),))
    down_weight = bell_draw(streams_of[16], (D, FF), FF ** -0.5, 0.0625, ((0, 4), (1, 2)))
    down_bias = bell_draw(streams_of[17], (D,), 0.3, 4.0)
    return dict(tokens=tokens, cotangent=cotangent, prefix_len=prefix_len, group_order=group_order, ln_gain=ln_gain, ln_bias=ln_bias, query_weight=query_weight, query_bias=query_bias, key_weight=key_weight, key_bias=key_bias, value_weight=value_weight, value_bias=value_bias, out_weight=out_weight, out_bias=out_bias, up_weight=up_weight, up_bias=up_bias, down_weight=down_weight, down_bias=down_bias)


@jax.custom_vjp
def low(v):
    return lax.optimization_barrier(v.astype(jnp.bfloat16)).astype(jnp.float32)

@jax.custom_vjp
def low_back(v):
    return v

def low_keep(v):
    return (low(v), None)

def low_pass(kept, grad):
    return (grad,)

def back_keep(v):
    return (v, None)

def back_low(kept, grad):
    return (low(grad),)
low.defvjp(low_keep, low_pass)
low_back.defvjp(back_keep, back_low)
masked_fill = -1e+30
norm_eps = 1e-05

def positions(group_order, row_start, row_count, group_len):
    row_index = row_start + jnp.arange(row_count, dtype=jnp.int32)
    slot_index = row_index // group_len
    offset = row_index - slot_index * group_len
    matches = slot_index[:, None] == jnp.arange(group_order.shape[0], dtype=jnp.int32)[None, :]
    anchor = lax.optimization_barrier(jnp.sum(jnp.where(matches, group_order[None, :], 0), axis=1)).astype(jnp.int32)
    return (anchor * group_len + offset).astype(jnp.int32)

def rotary_tables(places):
    half_rot = ROT // 2
    frequency = jnp.power(10000.0, -2.0 * jnp.arange(half_rot, dtype=jnp.float32) / ROT)
    angles = places.astype(jnp.float32)[:, None] * frequency[None, :]
    return (jnp.cos(angles), jnp.sin(angles))

def rotate(tensor, cosine, sine_vals):
    half_rot = cosine.shape[-1]
    front_part = tensor[..., :half_rot]
    back_part = tensor[..., half_rot:2 * half_rot]
    rest_part = tensor[..., 2 * half_rot:]
    cosine_rows = cosine[:, None, :]
    sine_rows = sine_vals[:, None, :]
    return jnp.concatenate([front_part * cosine_rows - back_part * sine_rows, back_part * cosine_rows + front_part * sine_rows, rest_part], axis=-1)

def matmul(left, right):
    return jnp.dot(left, right, precision=lax.Precision.HIGHEST)

def sequence_layer(inputs, prefix, key_place, params):
    norm_gain, norm_shift, w_query, b_query, w_key, b_key, w_value, b_value, w_out, b_out, w_up, b_up, w_down, b_down = params
    length = inputs.shape[0]
    centre = lax.optimization_barrier(jnp.mean(inputs, axis=-1, keepdims=True))
    centred = inputs - centre
    variance = lax.optimization_barrier(jnp.mean(centred * centred, axis=-1, keepdims=True))
    normed = centred * lax.rsqrt(variance + norm_eps)
    hidden = low(normed * norm_gain + norm_shift)
    cosine, sine_vals = rotary_tables(key_place)
    queries = low_back(matmul(hidden, w_query) + b_query).reshape(length, HEADS, HD)
    queries = low(rotate(queries, cosine, sine_vals))
    key_rows = low_back(matmul(hidden, w_key) + b_key).reshape(length, HEADS, HD)
    key_rows = low(rotate(key_rows, cosine, sine_vals))
    value_rows = low(low_back(matmul(hidden, w_value) + b_value)).reshape(length, HEADS, HD)
    scores = low_back(jnp.einsum('qhd,khd->hqk', queries, key_rows, precision=lax.Precision.HIGHEST) * HD ** (-0.5))
    allowed = (key_place[None, :] <= key_place[:, None]) | (key_place[None, :] < prefix)
    masked = jnp.where(allowed[None], scores, masked_fill)
    attn_probs = low(jax.nn.softmax(masked, axis=-1))
    context = jnp.einsum('hqk,khd->qhd', attn_probs, value_rows, precision=lax.Precision.HIGHEST)
    context = low(low_back(context)).reshape(length, D)
    attended = matmul(context, w_out.T) + b_out
    up_proj = low_back(matmul(hidden, w_up) + b_up)
    activated = low(jax.nn.gelu(up_proj, approximate=True))
    mlp_out = matmul(activated, w_down.T) + b_down
    return inputs + attended + mlp_out

def reference(tokens, cotangent, prefix_len, group_order, ln_gain, ln_bias, query_weight, query_bias, key_weight, key_bias, value_weight, value_bias, out_weight, out_bias, up_weight, up_bias, down_weight, down_bias):
    key_place = positions(group_order, 0, SEQ_LEN, GROUP)
    floats = tuple((entry_item.astype(jnp.float32) for entry_item in (tokens, ln_gain, ln_bias, query_weight, query_bias, key_weight, key_bias, value_weight, value_bias, out_weight, out_bias, up_weight, up_bias, down_weight, down_bias)))

    def forward(inputs, *params):

        def one_sequence(item_pair):
            return sequence_layer(item_pair[0], item_pair[1], key_place, params)
        return lax.map(jax.checkpoint(one_sequence), (inputs, prefix_len))
    output, pullback = jax.vjp(forward, *floats)
    gradients = pullback(cotangent.astype(jnp.float32))
    return (output.astype(jnp.bfloat16), gradients[0].astype(jnp.bfloat16), gradients[1], gradients[2], gradients[3], gradients[4], gradients[5], gradients[6], gradients[7], gradients[8], gradients[9], gradients[11], gradients[12], gradients[13], gradients[10])
```

```python
import functools

import jax
import jax.numpy as jnp
from jax import lax
from jax.experimental import pallas as pl
from jax.experimental.pallas import tpu as pltpu
from jax.sharding import PartitionSpec as P

HD = 64
ROT = 32
HALF = ROT // 2
PAIR = 2 * HD
NEG = -1e30
EPS = 1e-05
LOG2E = 1.4426950408889634
GELU_C = 0.7978845608028654
GELU_A = 0.044715
F32 = jnp.float32
BF16 = jnp.bfloat16


def xor_swap(value, axis, size, step):
    return lax.ppermute(value, axis, [(j, j ^ step) for j in range(size)])


def line_gather(mine, axis, size):
    left, right = [mine], [mine]
    for step in range(1, size):
        left.append(lax.ppermute(left[-1], axis, [(j, j + 1) for j in range(step - 1, size - 1)]))
        right.append(lax.ppermute(right[-1], axis, [(j, j - 1) for j in range(1, size - step + 1)]))
    return left, right


def by_distance(left, right, here):
    size = len(left)
    return [left[0]] + [
        jnp.where(here >= m, left[m], right[size - m]) for m in range(1, size)
    ]


def line_scatter_sum(parts, axis, size):
    add = lambda a, b: (a.astype(F32) + b.astype(F32)).astype(BF16)
    toward_right, toward_left = None, None
    for step in range(1, size):
        out_r = parts[step] if toward_right is None else add(toward_right, parts[step])
        out_l = parts[size - step] if toward_left is None else add(toward_left, parts[size - step])
        toward_right = lax.ppermute(out_r, axis, [(j, j + 1) for j in range(min(step, size - 1))])
        toward_left = lax.ppermute(
            out_l, axis, [(j, j - 1) for j in range(max(size - step, 1), size)]
        )
    return parts[0].astype(F32) + toward_right.astype(F32) + toward_left.astype(F32)


def rotate(x, cos, sa, sb):
    return (
        x * cos + pltpu.roll(x, PAIR - HALF, axis=1) * sa + pltpu.roll(x, HALF, axis=1) * sb
    )


def attention_kernel(
    glen, qblock, most,
    offs_ref, prefix_ref,
    qkv_ref, do_ref, cos_ref, sa_ref, sb_ref,
    ctx_ref, dqkv_ref,
    qm, qtm, k_s, kt_s, v_s, vt_s, dom, dotm, ot, dqt, dk_acc, dv_acc,
):
    length = cos_ref.shape[0]
    blocks = length // glen
    lane = lax.broadcasted_iota(jnp.int32, (glen, PAIR), 1)
    for p in range(blocks):
        rows = pl.ds(pl.multiple_of(offs_ref[p], glen), glen)
        to = slice(p * glen, (p + 1) * glen)
        cos, sa, sb = cos_ref[to, :], sa_ref[to, :], sb_ref[to, :]
        q = rotate(qkv_ref[0, rows, 0:PAIR], cos, sa, sb).astype(BF16).astype(F32) * (HD**-0.5)
        do = do_ref[0, rows, :].astype(F32)
        k_s[to, :] = rotate(qkv_ref[0, rows, PAIR : 2 * PAIR], cos, sa, sb).astype(BF16)
        v_s[to, :] = qkv_ref[0, rows, 2 * PAIR : 3 * PAIR].astype(BF16)
        for h in range(2):
            keep = (lane >= h * HD) & (lane < (h + 1) * HD)
            qm[h, to, :] = jnp.where(keep, q, 0.0).astype(BF16)
            dom[h, to, :] = jnp.where(keep, do, 0.0).astype(BF16)
    for h in range(2):
        qtm[h] = qm[h].T
        dotm[h] = dom[h].T
    kt_s[...] = k_s[...].T.reshape(2, HD, length)
    vt_s[...] = v_s[...].T.reshape(2, HD, length)
    dk_acc[...] = jnp.zeros_like(dk_acc)
    dv_acc[...] = jnp.zeros_like(dv_acc)
    prefix = prefix_ref[pl.program_id(0)]

    dot = functools.partial(jnp.dot, preferred_element_type=F32)
    for b in range(length // qblock):
        first = b * qblock
        reach = max(first + qblock, most)
        cols = slice(first, first + qblock)
        clear = first if first >= most else 0

        def head(h, _):
            s = dot(k_s[0:reach, :], qtm[h, :, cols]) * LOG2E
            kpos = clear + lax.broadcasted_iota(jnp.int32, (reach - clear, qblock), 0)
            qpos = first + lax.broadcasted_iota(jnp.int32, (1, qblock), 1)
            limit = jnp.maximum(qpos + 1, prefix)
            tail = jnp.where(kpos < limit, s[clear:reach], NEG)
            s = jnp.concatenate([s[:clear], tail], axis=0) if clear else tail
            e = jnp.exp2(s - jnp.max(s, axis=0, keepdims=True))
            prob = e * (1.0 / jnp.sum(e, axis=0, keepdims=True))
            low = prob.astype(BF16)
            ot[h, :, cols] = dot(vt_s[h, :, 0:reach], low)
            dv_acc[0:reach, :] += dot(low, dom[h, cols, :])
            dp = dot(v_s[0:reach, :], dotm[h, :, cols])
            delta = jnp.sum(prob * dp, axis=0, keepdims=True)
            ds = (prob * (dp - delta)).astype(BF16)
            dqt[h, :, cols] = dot(kt_s[h, :, 0:reach], ds)
            dk_acc[0:reach, :] += dot(ds, qm[h, cols, :])
            return 0

        lax.fori_loop(0, 2, head, 0)

    for p in range(blocks):
        rows = pl.ds(pl.multiple_of(offs_ref[p], glen), glen)
        to = slice(p * glen, (p + 1) * glen)
        cos, sa, sb = cos_ref[to, :], -sa_ref[to, :], -sb_ref[to, :]
        ctx_ref[0, rows, :] = ot[:, :, to].reshape(PAIR, glen).T.astype(BF16)
        dq = dqt[:, :, to].reshape(PAIR, glen).T * (HD**-0.5)
        dqkv_ref[0, rows, 0:PAIR] = rotate(dq, cos, sa, sb).astype(BF16)
        dqkv_ref[0, rows, PAIR : 2 * PAIR] = rotate(dk_acc[to, :], cos, sa, sb).astype(BF16)
        dqkv_ref[0, rows, 2 * PAIR : 3 * PAIR] = dv_acc[to, :].astype(BF16)


def attention(qkv, grad_context, offs, prefix, tables):
    seqs, length, _ = qkv.shape
    pairs = grad_context.shape[-1] // PAIR
    glen = length // offs.shape[0]
    qblock = min(256, length)
    most = length // 2
    whole = pl.BlockSpec((length, PAIR), lambda s, p, *_: (0, 0))
    wide = pl.BlockSpec((1, length, 3 * PAIR), lambda s, p, *_: (s, 0, p))
    narrow = pl.BlockSpec((1, length, PAIR), lambda s, p, *_: (s, 0, p))
    vm = pltpu.VMEM
    return pl.pallas_call(
        functools.partial(attention_kernel, glen, qblock, most),
        out_shape=(
            jax.ShapeDtypeStruct((seqs, length, pairs * PAIR), BF16),
            jax.ShapeDtypeStruct((seqs, length, pairs * 3 * PAIR), BF16),
        ),
        grid_spec=pltpu.PrefetchScalarGridSpec(
            num_scalar_prefetch=2,
            grid=(seqs, pairs),
            in_specs=[wide, narrow, whole, whole, whole],
            out_specs=(narrow, wide),
            scratch_shapes=[
                vm((2, length, PAIR), BF16),
                vm((2, PAIR, length), BF16),
                vm((length, PAIR), BF16),
                vm((2, HD, length), BF16),
                vm((length, PAIR), BF16),
                vm((2, HD, length), BF16),
                vm((2, length, PAIR), BF16),
                vm((2, PAIR, length), BF16),
                vm((2, HD, length), F32),
                vm((2, HD, length), F32),
                vm((length, PAIR), F32),
                vm((length, PAIR), F32),
            ],
        ),
        compiler_params=pltpu.CompilerParams(vmem_limit_bytes=40 << 20),
        name="attention",
    )(offs, prefix, qkv, grad_context, *tables)


def place_kernel(size, n_out, width, here_ref, *refs):
    blocks = refs[: 2 * size - 1]
    outs = refs[-n_out:]
    here = here_ref[0]
    m = pl.program_id(0)

    def put(value):
        for o in range(n_out):
            pieces = [
                value[:, c : c + width]
                for c in range(o * width, value.shape[1], n_out * width)
            ]
            whole = pieces[0] if len(pieces) == 1 else jnp.concatenate(pieces, axis=1)
            outs[o][...] = whole.astype(F32)

    @pl.when(m == 0)
    def _():
        put(blocks[0][...])

    for k in range(1, size):

        @pl.when((m == k) & (here >= k))
        def _():
            put(blocks[k][...])

        @pl.when((m == k) & (here < k))
        def _():
            put(blocks[2 * size - 1 - k][...])


def place(left, right, here, columns, out=None, n_out=1, width=None, part=0, parts=1):
    size = len(left)
    rows, span = left[0].shape
    width = width or span
    block = span // n_out
    blocks = left + right[1:]
    ops = list(blocks) + ([] if out is None else list(out))
    spec = pl.BlockSpec((rows, span), lambda m, h: (0, 0))
    out_spec = pl.BlockSpec(
        (rows, block), lambda m, h: (0, lax.rem(h[0] - m + size, size) * parts + part)
    )
    return pl.pallas_call(
        functools.partial(place_kernel, size, n_out, width),
        out_shape=tuple(jax.ShapeDtypeStruct((rows, columns), F32) for _ in range(n_out)),
        grid_spec=pltpu.PrefetchScalarGridSpec(
            num_scalar_prefetch=1,
            grid=(size,),
            in_specs=[spec] * len(blocks)
            + ([] if out is None else [pl.BlockSpec(memory_space=pl.ANY)] * n_out),
            out_specs=tuple(out_spec for _ in range(n_out)),
        ),
        input_output_aliases={} if out is None else {1 + len(blocks) + o: o for o in range(n_out)},
        compiler_params=pltpu.CompilerParams(vmem_limit_bytes=40 << 20),
        name="place",
    )(here.reshape(1), *ops)


def gelu_parts(up):
    inner = GELU_C * (up + GELU_A * up * up * up)
    t = jnp.tanh(inner)
    act = 0.5 * up * (1.0 + t)
    slope = 0.5 * (1.0 + t) + 0.5 * up * (1.0 - t * t) * GELU_C * (1.0 + 3.0 * GELU_A * up * up)
    return act, slope


def local(
    tokens, cotangent, prefix_len, group_order, ln_gain, ln_bias,
    query_weight, query_bias, key_weight, key_bias, value_weight, value_bias,
    out_weight, out_bias, up_weight, up_bias, down_weight, down_bias,
):
    nf, nc, nt = lax.axis_size("fsdp"), lax.axis_size("ctx"), lax.axis_size("tp")
    fi, ci, ti = lax.axis_index("fsdp"), lax.axis_index("ctx"), lax.axis_index("tp")
    seqs, rows, width = tokens.shape
    own_seqs = seqs // nt
    length = rows * nc
    own = own_seqs * rows
    db = width // nf
    inner = query_weight.shape[1] // nc
    units = up_weight.shape[1] // nc
    pairs = inner // PAIR

    def relative(x):
        return jnp.concatenate(
            [lax.dynamic_slice_in_dim(x, (fi ^ k) * db, db, axis=-1) for k in range(nf)], axis=-1
        )

    def columns(w):
        return lax.dynamic_slice_in_dim(w, ci * (w.shape[1] // nc), w.shape[1] // nc, axis=1)

    def by_pairs(arrays):
        return jnp.concatenate(
            [a[..., p * PAIR : (p + 1) * PAIR] for p in range(pairs) for a in arrays], axis=-1
        )

    def gather_rows(w):
        return jnp.concatenate(
            [w] + [xor_swap(w, "fsdp", nf, k) for k in range(1, nf)], axis=0
        )

    w_qkv = gather_rows(by_pairs([columns(query_weight), columns(key_weight), columns(value_weight)]))
    w_up = gather_rows(columns(up_weight))
    w_out = gather_rows(columns(out_weight))
    w_down = gather_rows(columns(down_weight))
    bias_cols = lambda b: lax.dynamic_slice_in_dim(b, ci * (b.shape[0] // nc), b.shape[0] // nc)
    b_qkv = by_pairs([bias_cols(query_bias), bias_cols(key_bias), bias_cols(value_bias)]).astype(F32)
    b_up = bias_cols(up_bias).astype(F32)

    x = lax.dynamic_slice_in_dim(tokens, ti * own_seqs, own_seqs, axis=0).reshape(own, width)
    g_own = lax.dynamic_slice_in_dim(cotangent, ti * own_seqs, own_seqs, axis=0).reshape(own, width)
    x = relative(x).astype(F32)
    g_own = relative(g_own)
    gain, shift = relative(ln_gain).astype(F32), relative(ln_bias).astype(F32)
    centred = x - jnp.mean(x, axis=-1, keepdims=True)
    inv_std = lax.rsqrt(jnp.mean(centred * centred, axis=-1, keepdims=True) + EPS)
    normed = centred * inv_std
    h_own = (normed * gain + shift).astype(BF16)

    def gather_tokens(mine):
        chunks = by_distance(*line_gather(mine, "ctx", nc), ci)
        others = []
        for k in range(1, nt):
            others += [xor_swap(c, "tp", nt, k) for c in chunks]
        out = jnp.stack(chunks + others).reshape(nt, nc, own_seqs, rows, width)
        return jnp.transpose(out, (0, 2, 1, 3, 4)).reshape(seqs * length, width)

    hidden = gather_tokens(h_own)
    grad = gather_tokens(g_own)

    def mm(a, b):
        return jnp.dot(a, b, preferred_element_type=F32)

    def mm_nt(a, b):
        return lax.dot_general(a, b, (((1,), (1,)), ((), ())), preferred_element_type=F32)

    def mm_tn(a, b):
        return lax.dot_general(a, b, (((0,), (0,)), ((), ())), preferred_element_type=F32)

    lane = jnp.arange(PAIR, dtype=jnp.int32)[None, :] % HD
    freq = jnp.power(10000.0, -2.0 * (lane % HALF).astype(F32) / ROT)
    angle = jnp.arange(length, dtype=jnp.int32).astype(F32)[:, None] * freq
    cos = jnp.where(lane < ROT, jnp.cos(angle), 1.0)
    sin = jnp.sin(angle)
    sa = jnp.where(lane < HALF, -sin, 0.0)
    sb = jnp.where((lane >= HALF) & (lane < ROT), sin, 0.0)
    groups = group_order.shape[0]
    glen = length // groups
    places = jnp.arange(groups, dtype=jnp.int32)
    slot = jnp.sum(
        jnp.where(group_order[None, :] == places[:, None], places[None, :], 0), axis=1
    ) * glen
    offs = ((ci - slot // rows + nc) % nc) * rows + slot % rows
    seq_ids = jnp.arange(seqs, dtype=jnp.int32)
    seq_of = ((seq_ids // own_seqs) ^ ti) * own_seqs + seq_ids % own_seqs
    prefix = jnp.sum(
        jnp.where(seq_of[:, None] == seq_ids[None, :], prefix_len[None, :], 0), axis=1
    )

    qkv = (mm(hidden, w_qkv) + b_qkv).reshape(seqs, length, 3 * inner)
    grad_context = mm(grad, w_out).astype(BF16).reshape(seqs, length, inner)
    context, dqkv = attention(
        qkv, grad_context, offs.astype(jnp.int32), prefix.astype(jnp.int32), (cos, sa, sb)
    )
    context = context.reshape(seqs * length, inner)
    dqkv = dqkv.reshape(seqs * length, 3 * inner)

    up = mm(hidden, w_up) + b_up
    act, slope = gelu_parts(up)
    act = act.astype(BF16)
    dup = (mm(grad, w_down) * slope).astype(BF16)

    def scatter_tokens(partial):
        part = partial.astype(BF16).reshape(nt, own_seqs, nc, rows, width)
        parts = []
        for m in range(nc):
            total = part[0, :, m].reshape(own, width).astype(F32)
            for k in range(1, nt):
                total = total + xor_swap(part[k, :, m].reshape(own, width), "tp", nt, k).astype(F32)
            parts.append(total.astype(BF16))
        return line_scatter_sum(parts, "ctx", nc)

    branches = scatter_tokens(mm_nt(act, w_down) + mm_nt(context, w_out))
    out_own = x + branches + relative(out_bias).astype(F32) + relative(down_bias).astype(F32)

    grad_hidden = scatter_tokens(mm_nt(dup, w_up) + mm_nt(dqkv, w_qkv))
    gs = grad_hidden * gain
    grad_normed = inv_std * (
        gs - jnp.mean(gs, axis=-1, keepdims=True)
        - normed * jnp.mean(gs * normed, axis=-1, keepdims=True)
    )
    in_own = g_own.astype(F32) + grad_normed

    def whole_tokens(own_rows):
        mine = relative(own_rows.astype(BF16)).reshape(1, own_seqs, rows, width)
        parts = [mine] + [xor_swap(mine, "tp", nt, k) for k in range(1, nt)]
        full = jnp.zeros((nt, own_seqs, rows, width), BF16)
        for k in range(nt):
            full = lax.dynamic_update_slice_in_dim(full, parts[k], ti ^ k, axis=0)
        return full.reshape(seqs, rows, width)

    output = whole_tokens(out_own)
    input_grad = whole_tokens(in_own)

    def weight_grad(left_act, right_act):
        full = mm_tn(left_act, right_act).astype(BF16)
        total = full[0:db].astype(F32)
        for k in range(1, nf):
            total = total + xor_swap(full[k * db : (k + 1) * db], "fsdp", nf, k).astype(F32)
        return line_gather(total.astype(BF16), "ctx", nc)

    chunk = min(512, units)
    parts = units // chunk
    here = ci.astype(jnp.int32)
    dw_down, dw_up = None, None
    for q in range(parts):
        cut = slice(q * chunk, (q + 1) * chunk)
        dw_down = place(*weight_grad(grad, act[:, cut]), here, units * nc, dw_down, part=q, parts=parts)
    for q in range(parts):
        cut = slice(q * chunk, (q + 1) * chunk)
        dw_up = place(*weight_grad(hidden, dup[:, cut]), here, units * nc, dw_up, part=q, parts=parts)
    dw_out = place(*weight_grad(grad, context), here, inner * nc)
    dw_qkv = place(*weight_grad(hidden, dqkv), here, inner * nc, n_out=3, width=PAIR)

    def over_line(v):
        full = jnp.zeros((nc,) + v.shape, v.dtype)
        for k in range(nc):
            got = v if k == 0 else lax.ppermute(v, "ctx", [(j, (j + k) % nc) for j in range(nc)])
            full = lax.dynamic_update_slice_in_dim(full, got[None], (ci - k + nc) % nc, axis=0)
        return full

    def over_fsdp(v):
        return v + sum(xor_swap(v, "fsdp", nf, k) for k in range(1, nf))

    col_sum = lambda a: jnp.sum(a.astype(F32), axis=0)
    bias_sums = over_fsdp(jnp.concatenate([col_sum(dqkv), col_sum(dup)]))
    wide = over_line(bias_sums)
    qkv_sums = wide[:, : 3 * inner].reshape(nc, pairs, 3, PAIR)
    qb, kb, vb = (qkv_sums[:, :, n].reshape(nc * inner) for n in range(3))
    ub = wide[:, 3 * inner :].reshape(nc * units)
    obias = over_fsdp(relative(col_sum(grad)))

    norm_sums = relative(jnp.stack([col_sum(grad_hidden * normed), col_sum(grad_hidden)]))
    for k in range(1, nt):
        norm_sums = norm_sums + xor_swap(norm_sums, "tp", nt, k)
    norm_sums = over_fsdp(norm_sums)
    norm_sums = jnp.sum(over_line(norm_sums), axis=0)

    return (
        output, input_grad, norm_sums[0], norm_sums[1],
        dw_qkv[0], qb, dw_qkv[1], kb, dw_qkv[2], vb,
        dw_out[0], dw_up[0], ub, dw_down[0], obias,
    )


def solution(mesh):
    rows, flat, cols, one = P("fsdp", "ctx", None), P("fsdp", "tp"), P("tp"), P()
    return jax.shard_map(
        local,
        mesh=mesh,
        in_specs=(
            rows, rows, P("fsdp"), one, one, one,
            flat, cols, flat, cols, flat, cols, flat, one, flat, cols, flat, one,
        ),
        out_specs=(
            rows, rows, one, one, flat, cols, flat, cols, flat, cols, flat, flat, cols, flat, one,
        ),
        check_vma=False,
    )
```

```python
import functools

import jax
import jax.numpy as jnp
from jax import lax
from jax.experimental import pallas as pl
from jax.experimental.pallas import tpu as pltpu
from jax.sharding import PartitionSpec as P

HD = 64
ROT = 32
HALF = ROT // 2
PAIR = 2 * HD
NEG = -1e30
EPS = 1e-05
LOG2E = 1.4426950408889634
GELU_C = 0.7978845608028654
GELU_A = 0.044715
F32 = jnp.float32
BF16 = jnp.bfloat16


def meet(tree):
    return lax.optimization_barrier(tree)


def total(addends):
    out = addends[0].astype(F32)
    for one in addends[1:]:
        out = out + one.astype(F32)
    return out


def xor_swap(value, axis, size, step):
    return lax.ppermute(value, axis, [(j, j ^ step) for j in range(size)])


def to_all(value, axis, size):
    return lax.all_to_all(jnp.broadcast_to(value[None], (size,) + value.shape), axis, 0, 0, tiled=True)


def gather_step(sides, step, size, axis="ctx"):
    left, right = sides
    return (
        lax.ppermute(left, axis, [(j, j + 1) for j in range(step - 1, size - 1)]),
        lax.ppermute(right, axis, [(j, j - 1) for j in range(1, size - step + 1)]),
    )


def sum_step(sides, parts, step, size, axis="ctx"):
    a, b = parts(step), parts(size - step)
    if sides is not None:
        a, b = a + [sides[0]], b + [sides[1]]
    return (
        lax.ppermute(
            total(a).astype(BF16), axis, [(j, j + 1) for j in range(min(step, size - 1))]
        ),
        lax.ppermute(
            total(b).astype(BF16), axis, [(j, j - 1) for j in range(max(size - step, 1), size)]
        ),
    )


def by_distance(blocks, here):
    n = len(blocks)
    return [blocks[0]] + [
        jnp.where(here >= m, blocks[m][0], blocks[n - m][1]) for m in range(1, n)
    ]


FREE = pl.CostEstimate(flops=1, transcendentals=0, bytes_accessed=1)


def rotate(x, cos, sa, sb):
    return (
        x * cos + pltpu.roll(x, PAIR - HALF, axis=1) * sa + pltpu.roll(x, HALF, axis=1) * sb
    )


def masked_scores(k_s, qt, prefix, first, reach, clear):
    s = jnp.dot(k_s[0:reach, :], qt, preferred_element_type=F32) * LOG2E
    count = qt.shape[1]
    kpos = clear + lax.broadcasted_iota(jnp.int32, (reach - clear, count), 0)
    qpos = first + lax.broadcasted_iota(jnp.int32, (1, count), 1)
    tail = jnp.where(kpos < jnp.maximum(qpos + 1, prefix), s[clear:reach], NEG)
    return jnp.concatenate([s[:clear], tail], axis=0) if clear else tail


def spans(length, qblock, most):
    for first in range(0, length, qblock):
        yield first, max(first + qblock, most), first if first >= most else 0


def keep_head(x, h):
    lane = lax.broadcasted_iota(jnp.int32, x.shape, 1)
    return jnp.where((lane >= h * HD) & (lane < (h + 1) * HD), x, 0.0)


def attend_kernel(
    glen, qblock, most,
    offs_ref, prefix_ref,
    qkv_ref, cos_ref, sa_ref, sb_ref,
    ctx_ref, sorted_ref, stat_ref,
    qtm, k_s, vt_s, ot,
):
    length = cos_ref.shape[0]
    for p in range(length // glen):
        rows = pl.ds(pl.multiple_of(offs_ref[p], glen), glen)
        to = slice(p * glen, (p + 1) * glen)
        cos, sa, sb = cos_ref[to, :], sa_ref[to, :], sb_ref[to, :]
        q = rotate(qkv_ref[rows, 0:PAIR], cos, sa, sb).astype(BF16).astype(F32) * (HD**-0.5)
        sorted_ref[to, 0:PAIR] = q.astype(BF16)
        k = rotate(qkv_ref[rows, PAIR : 2 * PAIR], cos, sa, sb).astype(BF16)
        k_s[to, :] = k
        sorted_ref[to, PAIR : 2 * PAIR] = k
        sorted_ref[to, 2 * PAIR : 3 * PAIR] = qkv_ref[rows, 2 * PAIR : 3 * PAIR].astype(BF16)
    q = sorted_ref[:, 0:PAIR].astype(F32)
    for h in range(2):
        qtm[h] = keep_head(q, h).astype(BF16).T
    vt_s[...] = sorted_ref[:, 2 * PAIR : 3 * PAIR].T.reshape(2, HD, length)
    prefix = prefix_ref[0]
    for first, reach, clear in spans(length, qblock, most):
        cols = slice(first, first + qblock)

        def head(h, _):
            s = masked_scores(k_s, qtm[h, :, cols], prefix, first, reach, clear)
            top = jnp.max(s, axis=0, keepdims=True)
            e = jnp.exp2(s - top)
            scale = 1.0 / jnp.sum(e, axis=0, keepdims=True)
            stat_ref[0, h, 0:1, cols] = top
            stat_ref[0, h, 1:2, cols] = scale
            low = (e * scale).astype(BF16)
            ot[h, :, cols] = jnp.dot(vt_s[h, :, 0:reach], low, preferred_element_type=F32)
            return 0

        lax.fori_loop(0, 2, head, 0)
    for p in range(length // glen):
        rows = pl.ds(pl.multiple_of(offs_ref[p], glen), glen)
        to = slice(p * glen, (p + 1) * glen)
        ctx_ref[rows, :] = ot[:, :, to].reshape(PAIR, glen).T.astype(BF16)


def attend_back_kernel(
    glen, qblock, most,
    offs_ref, prefix_ref,
    sorted_ref, stat_ref, do_ref, cos_ref, sa_ref, sb_ref,
    dqkv_ref,
    qm, qtm, k_s, kt_s, v_s, dom, dotm, dqt, dk_acc, dv_acc,
):
    length = cos_ref.shape[0]
    k_s[...] = sorted_ref[:, PAIR : 2 * PAIR]
    v_s[...] = sorted_ref[:, 2 * PAIR : 3 * PAIR]
    q = sorted_ref[:, 0:PAIR].astype(F32)
    for p in range(length // glen):
        rows = pl.ds(pl.multiple_of(offs_ref[p], glen), glen)
        to = slice(p * glen, (p + 1) * glen)
        do = do_ref[rows, :].astype(F32)
        for h in range(2):
            dom[h, to, :] = keep_head(do, h).astype(BF16)
    for h in range(2):
        qm[h] = keep_head(q, h).astype(BF16)
        qtm[h] = qm[h].T
        dotm[h] = dom[h].T
    kt_s[...] = k_s[...].T.reshape(2, HD, length)
    dk_acc[...] = jnp.zeros_like(dk_acc)
    dv_acc[...] = jnp.zeros_like(dv_acc)
    prefix = prefix_ref[0]
    dot = functools.partial(jnp.dot, preferred_element_type=F32)
    for first, reach, clear in spans(length, qblock, most):
        cols = slice(first, first + qblock)

        def head(h, _):
            s = masked_scores(k_s, qtm[h, :, cols], prefix, first, reach, clear)
            prob = jnp.exp2(s - stat_ref[0, h, 0:1, cols]) * stat_ref[0, h, 1:2, cols]
            dv_acc[0:reach, :] += dot(prob.astype(BF16), dom[h, cols, :])
            dp = dot(v_s[0:reach, :], dotm[h, :, cols])
            delta = jnp.sum(prob * dp, axis=0, keepdims=True)
            ds = (prob * (dp - delta)).astype(BF16)
            dqt[h, :, cols] = dot(kt_s[h, :, 0:reach], ds)
            dk_acc[0:reach, :] += dot(ds, qm[h, cols, :])
            return 0

        lax.fori_loop(0, 2, head, 0)
    for p in range(length // glen):
        rows = pl.ds(pl.multiple_of(offs_ref[p], glen), glen)
        to = slice(p * glen, (p + 1) * glen)
        cos, sa, sb = cos_ref[to, :], -sa_ref[to, :], -sb_ref[to, :]
        dq = dqt[:, :, to].reshape(PAIR, glen).T * (HD**-0.5)
        dqkv_ref[rows, 0:PAIR] = rotate(dq, cos, sa, sb).astype(BF16)
        dqkv_ref[rows, PAIR : 2 * PAIR] = rotate(dk_acc[to, :], cos, sa, sb).astype(BF16)
        dqkv_ref[rows, 2 * PAIR : 3 * PAIR] = dv_acc[to, :].astype(BF16)


def attention_specs(length):
    whole = pl.BlockSpec((length, PAIR), lambda p, *_: (0, 0))
    wide = pl.BlockSpec((length, 3 * PAIR), lambda p, *_: (0, p))
    narrow = pl.BlockSpec((length, PAIR), lambda p, *_: (0, p))
    stat = pl.BlockSpec((1, 2, 2, length), lambda p, *_: (p, 0, 0, 0))
    return whole, wide, narrow, stat


def attend(qkv, offs, prefix, tables):
    length, inner = qkv.shape[0], qkv.shape[1] // 3
    whole, wide, narrow, stat = attention_specs(length)
    vm = pltpu.VMEM
    return pl.pallas_call(
        functools.partial(attend_kernel, length // offs.shape[0], min(256, length), length // 2),
        out_shape=(
            jax.ShapeDtypeStruct((length, inner), BF16),
            jax.ShapeDtypeStruct((length, 3 * inner), BF16),
            jax.ShapeDtypeStruct((inner // PAIR, 2, 2, length), F32),
        ),
        grid_spec=pltpu.PrefetchScalarGridSpec(
            num_scalar_prefetch=2,
            grid=(inner // PAIR,),
            in_specs=[wide, whole, whole, whole],
            out_specs=(narrow, wide, stat),
            scratch_shapes=[
                vm((2, PAIR, length), BF16),
                vm((length, PAIR), BF16),
                vm((2, HD, length), BF16),
                vm((2, HD, length), F32),
            ],
        ),
        compiler_params=pltpu.CompilerParams(vmem_limit_bytes=40 << 20),
        cost_estimate=FREE,
        name="attend",
    )(offs, prefix, qkv, *tables)


def attend_back(ordered, stats, grad_context, offs, prefix, tables):
    length, inner = grad_context.shape
    whole, wide, narrow, stat = attention_specs(length)
    vm = pltpu.VMEM
    return pl.pallas_call(
        functools.partial(
            attend_back_kernel, length // offs.shape[0], min(256, length), length // 2
        ),
        out_shape=jax.ShapeDtypeStruct((length, 3 * inner), BF16),
        grid_spec=pltpu.PrefetchScalarGridSpec(
            num_scalar_prefetch=2,
            grid=(inner // PAIR,),
            in_specs=[wide, stat, narrow, whole, whole, whole],
            out_specs=wide,
            scratch_shapes=[
                vm((2, length, PAIR), BF16),
                vm((2, PAIR, length), BF16),
                vm((length, PAIR), BF16),
                vm((2, HD, length), BF16),
                vm((length, PAIR), BF16),
                vm((2, length, PAIR), BF16),
                vm((2, PAIR, length), BF16),
                vm((2, HD, length), F32),
                vm((length, PAIR), F32),
                vm((length, PAIR), F32),
            ],
        ),
        compiler_params=pltpu.CompilerParams(vmem_limit_bytes=40 << 20),
        cost_estimate=FREE,
        name="attend_back",
    )(offs, prefix, ordered, stats, grad_context, *tables)


def pair_kernel(split, a_ref, b_ref, w_ref, o_ref):
    nt = (((1,), (1,)), ((), ()))
    o = lax.dot_general(a_ref[...], w_ref[:, :split], nt, preferred_element_type=F32)
    o += lax.dot_general(b_ref[...], w_ref[:, split:], nt, preferred_element_type=F32)
    o_ref[...] = o.astype(o_ref.dtype)


def pair_product(a, b, w):
    n, depth = w.shape
    m = a.shape[0]
    bn = min(512, n)
    return pl.pallas_call(
        functools.partial(pair_kernel, a.shape[1]),
        out_shape=jax.ShapeDtypeStruct((m, n), BF16),
        grid=(n // bn,),
        in_specs=[
            pl.BlockSpec((m, a.shape[1]), lambda j: (0, 0), pipeline_mode=pl.Buffered(1)),
            pl.BlockSpec((m, b.shape[1]), lambda j: (0, 0), pipeline_mode=pl.Buffered(1)),
            pl.BlockSpec((bn, depth), lambda j: (j, 0)),
        ],
        out_specs=pl.BlockSpec((m, bn), lambda j: (0, j)),
        compiler_params=pltpu.CompilerParams(vmem_limit_bytes=48 << 20),
        cost_estimate=FREE,
        name="pair_product",
    )(a, b, w)


def pack_kernel(pieces, here_ref, *refs):
    o_ref = refs[-1]
    at = 0
    for n, start, size in pieces:
        o_ref[0, :, at : at + size] = refs[n][:, start : start + size]
        at += size


def pack_columns(weights, pieces, here, places, copies):
    rows = weights[0].shape[0]
    span = sum(size for _, _, size in pieces)
    return pl.pallas_call(
        functools.partial(pack_kernel, pieces),
        out_shape=jax.ShapeDtypeStruct((copies, rows, span), weights[0].dtype),
        grid_spec=pltpu.PrefetchScalarGridSpec(
            num_scalar_prefetch=1,
            grid=(copies,),
            in_specs=[
                pl.BlockSpec((rows, w.shape[1] // places), lambda i, h: (0, h[0])) for w in weights
            ],
            out_specs=pl.BlockSpec((1, rows, span), lambda i, h: (i, 0, 0)),
        ),
        compiler_params=pltpu.CompilerParams(vmem_limit_bytes=40 << 20),
        cost_estimate=FREE,
        name="pack_columns",
    )(here.reshape(1), *weights)


def rows_kernel(counts, *refs):
    o_ref = refs[-1]
    tn = (((0,), (0,)), ((), ()))
    at, col = 0, 0
    for count in counts:
        o = 0.0
        for n in range(count):
            o += lax.dot_general(
                refs[at + n][...], refs[at + count + n][...], tn, preferred_element_type=F32
            )
        o_ref[0, :, col : col + o.shape[1]] = o.astype(o_ref.dtype)
        at, col = at + 2 * count, col + o.shape[1]


def rows_product(products, owners):
    args, specs, columns = [], [], 0
    for a, b in products:
        bm = a[0].shape[1] // owners
        args += [*a, *b]
        specs += [pl.BlockSpec((x.shape[0], bm), lambda i: (0, i)) for x in a]
        specs += [
            pl.BlockSpec(x.shape, lambda i: (0, 0), pipeline_mode=pl.Buffered(1)) for x in b
        ]
        columns += b[0].shape[1]
    return pl.pallas_call(
        functools.partial(rows_kernel, [len(a) for a, _ in products]),
        out_shape=jax.ShapeDtypeStruct((owners, bm, columns), BF16),
        grid=(owners,),
        in_specs=specs,
        out_specs=pl.BlockSpec((1, bm, columns), lambda i: (i, 0, 0)),
        compiler_params=pltpu.CompilerParams(vmem_limit_bytes=56 << 20),
        cost_estimate=FREE,
        name="rows_product",
    )(*args)


def order_kernel(size, here_ref, *refs):
    blocks, o_ref = refs[:-1], refs[-1]
    m, here = pl.program_id(0), here_ref[0]

    def put(ref):
        o_ref[0] = ref[...]

    pl.when(m == 0)(lambda: put(blocks[0]))
    for k in range(1, size):
        pl.when((m == k) & (here >= k))(functools.partial(put, blocks[k]))
        pl.when((m == k) & (here < k))(functools.partial(put, blocks[2 * size - 1 - k]))


def in_order(blocks, here):
    size = len(blocks)
    rows, span = blocks[0].shape
    blocks = [blocks[0]] + [x[0] for x in blocks[1:]] + [x[1] for x in blocks[1:]]
    return pl.pallas_call(
        functools.partial(order_kernel, size),
        out_shape=jax.ShapeDtypeStruct((size, rows, span), blocks[0].dtype),
        grid_spec=pltpu.PrefetchScalarGridSpec(
            num_scalar_prefetch=1,
            grid=(size,),
            in_specs=[pl.BlockSpec((rows, span), lambda m, h: (0, 0), pipeline_mode=pl.Buffered(1))]
            * len(blocks),
            out_specs=pl.BlockSpec(
                (1, rows, span), lambda m, h: (lax.rem(h[0] - m + size, size), 0, 0)
            ),
        ),
        compiler_params=pltpu.CompilerParams(vmem_limit_bytes=48 << 20),
        cost_estimate=FREE,
        name="in_order",
    )(here.reshape(1), *blocks)


def place_kernel(size, pairs, here_ref, *refs):
    blocks, outs = refs[: 2 * size - 1], refs[2 * size - 1 :]
    m, here = pl.program_id(0), here_ref[0]
    spans = [[(p * 3 + n) * PAIR for p in range(pairs)] for n in range(3)]
    spans.append([(3 * pairs + p) * PAIR for p in range(pairs)])

    def put(block):
        for out, starts in zip(outs, spans):
            for p, at in enumerate(starts):
                out[:, p * PAIR : (p + 1) * PAIR] = block[:, at : at + PAIR].astype(F32)

    pl.when(m == 0)(lambda: put(blocks[0]))
    for k in range(1, size):
        pl.when((m == k) & (here >= k))(functools.partial(put, blocks[k]))
        pl.when((m == k) & (here < k))(functools.partial(put, blocks[2 * size - 1 - k]))


def place(blocks, here, pairs):
    size = len(blocks)
    rows, span = blocks[0].shape
    blocks = [blocks[0]] + [x[0] for x in blocks[1:]] + [x[1] for x in blocks[1:]]
    width = pairs * PAIR
    return pl.pallas_call(
        functools.partial(place_kernel, size, pairs),
        out_shape=(jax.ShapeDtypeStruct((rows, size * width), F32),) * 4,
        grid_spec=pltpu.PrefetchScalarGridSpec(
            num_scalar_prefetch=1,
            grid=(size,),
            in_specs=[pl.BlockSpec((rows, span), lambda m, h: (0, 0), pipeline_mode=pl.Buffered(1))]
            * len(blocks),
            out_specs=(
                pl.BlockSpec((rows, width), lambda m, h: (0, lax.rem(h[0] - m + size, size))),
            )
            * 4,
        ),
        compiler_params=pltpu.CompilerParams(vmem_limit_bytes=48 << 20),
        cost_estimate=FREE,
        name="place",
    )(here.reshape(1), *blocks)


def widen_kernel(a_ref, o_ref):
    o_ref[...] = a_ref[0].astype(F32)


def widen(blocks):
    n, rows, span = blocks.shape
    return pl.pallas_call(
        widen_kernel,
        out_shape=jax.ShapeDtypeStruct((rows, n * span), F32),
        grid=(n,),
        in_specs=[pl.BlockSpec((1, rows, span), lambda c: (c, 0, 0))],
        out_specs=pl.BlockSpec((rows, span), lambda c: (0, c)),
        compiler_params=pltpu.CompilerParams(vmem_limit_bytes=40 << 20),
        cost_estimate=FREE,
        name="widen",
    )(blocks)


def up_kernel(step, h_ref, w_ref, b_ref, act_ref, slope_ref):
    for c in range(0, act_ref.shape[1], step):
        up = jnp.dot(h_ref[...], w_ref[:, c : c + step], preferred_element_type=F32)
        act, slope = gelu_parts(up + b_ref[:, c : c + step])
        act_ref[:, c : c + step] = act.astype(BF16)
        slope_ref[:, c : c + step] = slope.astype(BF16)


def up_product(hidden, weight, bias):
    m, k = hidden.shape
    n = bias.shape[0]
    bm = min(512, m)
    return pl.pallas_call(
        functools.partial(up_kernel, min(256, n)),
        out_shape=(jax.ShapeDtypeStruct((m, n), BF16),) * 2,
        grid=(m // bm,),
        in_specs=[
            pl.BlockSpec((bm, k), lambda i: (i, 0)),
            pl.BlockSpec((k, n), lambda i: (0, 0), pipeline_mode=pl.Buffered(1)),
            pl.BlockSpec((1, n), lambda i: (0, 0)),
        ],
        out_specs=(pl.BlockSpec((bm, n), lambda i: (i, 0)),) * 2,
        compiler_params=pltpu.CompilerParams(vmem_limit_bytes=56 << 20),
        cost_estimate=FREE,
        name="up_product",
    )(hidden, weight, bias.reshape(1, n))


def down_kernel(units, g_ref, w_ref, s_ref, d_ref, c_ref):
    g = g_ref[...]
    d = jnp.dot(g, w_ref[:, :units], preferred_element_type=F32)
    d_ref[...] = (d * s_ref[...].astype(F32)).astype(BF16)
    c_ref[...] = jnp.dot(g, w_ref[:, units:], preferred_element_type=F32).astype(BF16)


def down_product(grad, weight, slope):
    m, k = grad.shape
    units, n = slope.shape[1], weight.shape[1]
    bm = min(512, m)
    return pl.pallas_call(
        functools.partial(down_kernel, units),
        out_shape=(
            jax.ShapeDtypeStruct((m, units), BF16),
            jax.ShapeDtypeStruct((m, n - units), BF16),
        ),
        grid=(m // bm,),
        in_specs=[
            pl.BlockSpec((bm, k), lambda i: (i, 0)),
            pl.BlockSpec((k, n), lambda i: (0, 0), pipeline_mode=pl.Buffered(1)),
            pl.BlockSpec((bm, units), lambda i: (i, 0)),
        ],
        out_specs=(
            pl.BlockSpec((bm, units), lambda i: (i, 0)),
            pl.BlockSpec((bm, n - units), lambda i: (i, 0)),
        ),
        compiler_params=pltpu.CompilerParams(vmem_limit_bytes=56 << 20),
        cost_estimate=FREE,
        name="down_product",
    )(grad, weight, slope)


def line_kernel(pieces, h_ref, *refs):
    b_ref, o_ref = refs[pieces], refs[-1]
    span = o_ref.shape[1] // pieces
    for n in range(pieces):
        to = slice(n * span, (n + 1) * span)
        o = jnp.dot(h_ref[...], refs[n][...], preferred_element_type=F32)
        o_ref[:, to] = o + b_ref[:, to]


def line_product(hidden, weight, bias, start, pieces):
    m, k = hidden.shape
    n = bias.shape[0]
    span = n // pieces
    bm = min(512, m)
    piece = lambda p: pl.BlockSpec(
        (k, span), lambda i: (0, start // span + p), pipeline_mode=pl.Buffered(1)
    )
    return pl.pallas_call(
        functools.partial(line_kernel, pieces),
        out_shape=jax.ShapeDtypeStruct((m, n), F32),
        grid=(m // bm,),
        in_specs=[pl.BlockSpec((bm, k), lambda i: (i, 0))]
        + [piece(p) for p in range(pieces)]
        + [pl.BlockSpec((1, n), lambda i: (0, 0))],
        out_specs=pl.BlockSpec((bm, n), lambda i: (i, 0)),
        compiler_params=pltpu.CompilerParams(vmem_limit_bytes=56 << 20),
        cost_estimate=FREE,
        name="line_product",
    )(hidden, *[weight] * pieces, bias.reshape(1, n))


def gelu_parts(up):
    square = up * up
    t = jnp.tanh(GELU_C * up * (1.0 + GELU_A * square))
    half = 0.5 * (1.0 + t)
    slope = half + 0.5 * up * (1.0 - t * t) * (GELU_C * (1.0 + 3.0 * GELU_A * square))
    return up * half, slope


def local(
    tokens, cotangent, prefix_len, group_order, ln_gain, ln_bias,
    query_weight, query_bias, key_weight, key_bias, value_weight, value_bias,
    out_weight, out_bias, up_weight, up_bias, down_weight, down_bias,
):
    nf, nc, nt = lax.axis_size("fsdp"), lax.axis_size("ctx"), lax.axis_size("tp")
    ci, ti = lax.axis_index("ctx").astype(jnp.int32), lax.axis_index("tp").astype(jnp.int32)
    seqs, rows, width = tokens.shape
    own_seqs = seqs // nt
    length = rows * nc
    own = own_seqs * rows
    db = width // nf
    inner = query_weight.shape[1] // nc
    units = up_weight.shape[1] // nc
    pairs = inner // PAIR

    def columns(w):
        return lax.dynamic_slice_in_dim(w, ci * (w.shape[-1] // nc), w.shape[-1] // nc, axis=-1)

    def by_pairs(arrays):
        return jnp.concatenate(
            [a[..., p * PAIR : (p + 1) * PAIR] for p in range(pairs) for a in arrays], axis=-1
        )

    x = lax.dynamic_slice_in_dim(tokens, ti * own_seqs, own_seqs, axis=0).reshape(own, width)
    g_own = lax.dynamic_slice_in_dim(cotangent, ti * own_seqs, own_seqs, axis=0).reshape(own, width)
    x = x.astype(F32)
    gain, shift = ln_gain.astype(F32), ln_bias.astype(F32)
    centred = x - jnp.mean(x, axis=-1, keepdims=True)
    inv_std = lax.rsqrt(jnp.mean(centred * centred, axis=-1, keepdims=True) + EPS)
    normed = centred * inv_std
    h_own = (normed * gain + shift).astype(BF16)

    h_in = [h_own]

    def side(blocks):
        return blocks[-1] if len(blocks) > 1 else (blocks[0], blocks[0])

    def gather_on(blocks):
        return blocks + [gather_step(side(blocks), len(blocks), nc)]

    cut = [
        (1 + n, p * PAIR, PAIR) for p in range(pairs) for n in range(3)
    ]
    h_own, early = meet(
        (h_own, (up_weight, query_weight, key_weight, value_weight, down_weight, out_weight))
    )
    first = pack_columns(early[:4], [(0, 0, units)] + cut, ci, nc, nf)
    second = pack_columns(early[4:], [(0, 0, units), (1, 0, inner)], ci, nc, nf)
    b_qkv = by_pairs([columns(query_bias), columns(key_bias), columns(value_bias)]).astype(F32)
    b_up = columns(up_bias).astype(F32)

    lane = jnp.arange(PAIR, dtype=jnp.int32)[None, :] % HD
    freq = jnp.power(10000.0, -2.0 * (lane % HALF).astype(F32) / ROT)
    angle = jnp.arange(length, dtype=jnp.int32).astype(F32)[:, None] * freq
    cos = jnp.where(lane < ROT, jnp.cos(angle), 1.0)
    sin = jnp.sin(angle)
    sa = jnp.where(lane < HALF, -sin, 0.0)
    sb = jnp.where((lane >= HALF) & (lane < ROT), sin, 0.0)
    groups = group_order.shape[0]
    glen = length // groups
    places = jnp.arange(groups, dtype=jnp.int32)
    slot = jnp.sum(
        jnp.where(group_order[None, :] == places[:, None], places[None, :], 0), axis=1
    ) * glen
    offs = slot
    seq_ids = jnp.arange(seqs, dtype=jnp.int32)
    seq_of = ((seq_ids // own_seqs) ^ ti) * own_seqs + seq_ids % own_seqs
    prefix = jnp.sum(
        jnp.where(seq_of[:, None] == seq_ids[None, :], prefix_len[None, :], 0), axis=1
    )
    offs, prefix = offs.astype(jnp.int32), prefix.astype(jnp.int32)

    tables = (cos, sa, sb)
    first_all = lax.all_to_all(first, "fsdp", 0, 0, tiled=True)
    h_in, second, tables = meet((gather_on(h_in), second, tables))
    while len(h_in) < nc:
        h_in = meet(gather_on(h_in))
    g_own, h_in = meet((g_own, h_in))
    g_all = lax.all_gather(g_own.reshape(own_seqs, rows, width), "ctx", axis=1, tiled=True)

    def halves(mine):
        mine = mine.reshape(own_seqs * length, width)
        return [mine] + [xor_swap(mine, "tp", nt, k) for k in range(1, nt)]

    def send_rows(full):
        return lax.all_to_all(full, "fsdp", 0, 0, tiled=True)

    def sum_rows(got):
        return total([got[k] for k in range(nf)]).astype(BF16)

    def gather_cols(mine):
        return lax.all_gather(mine, "ctx", axis=0, tiled=False)

    h_mine = jnp.moveaxis(in_order(h_in, ci).reshape(nc, own_seqs, rows, width), 1, 0)
    hidden = halves(h_mine)
    hidden, first_all = meet((hidden, first_all))
    w_first = first_all.reshape(width, units + 3 * inner)
    second_all = lax.all_to_all(second, "fsdp", 0, 0, tiled=True)
    ups, qkv = [], []
    for n in range(nt):
        ups.append(up_product(hidden[n], w_first, b_up))
        ups, hidden = meet((ups, hidden))
    for n in range(nt):
        qkv.append(line_product(hidden[n], w_first, b_qkv, units, 3))
        qkv, hidden = meet((qkv, hidden))
    act, slope = [u[0] for u in ups], [u[1] for u in ups]
    done = []
    for n in range(seqs):
        at = slice((n % own_seqs) * length, (n % own_seqs + 1) * length)
        done.append(attend(qkv[n // own_seqs][at], offs, prefix[n : n + 1], tables))
        done, qkv = meet((done, qkv))
    context = [
        jnp.concatenate([d[0] for d in done[n * own_seqs : (n + 1) * own_seqs]]) for n in range(nt)
    ]

    def parts_of(mine, got):
        grid = lambda a: a.reshape(own_seqs, nc, rows, width)
        mine, got = grid(mine), [grid(g) for g in got]

        def parts(m):
            at = (ci - m + nc) % nc
            pick = lambda a: lax.dynamic_index_in_dim(a, at, 1, keepdims=False).reshape(own, width)
            return [pick(mine)] + [pick(g) for g in got]

        return parts

    act, context, second_all, g_all = meet((act, context, second_all, g_all))
    w_second = second_all.reshape(width, units + inner)
    grad = halves(g_all)
    theirs, act, context = meet(
        ([pair_product(act[k], context[k], w_second) for k in range(1, nt)], act, context)
    )
    full_down = rows_product([(grad, act)], nf)
    grad, full_down, slope, theirs, act = meet((grad, full_down, slope, theirs, act))
    d_rows = send_rows(full_down)
    o_got = [xor_swap(t, "tp", nt, k) for k, t in zip(range(1, nt), theirs)]
    o_got, o_mine = meet((o_got, pair_product(act[0], context[0], w_second)))
    o_parts = parts_of(o_mine, o_got)
    o_sum = sum_step(None, o_parts, 1, nc)
    downs, step = [], 2
    for n in range(nt):
        downs.append(down_product(grad[n], w_second, slope[n]))
        downs, grad, hidden, o_sum = meet((downs, grad, hidden, o_sum))
        if step < nc:
            o_sum = sum_step(o_sum, o_parts, step, nc)
            step += 1
    dup, grad_context = [d[0] for d in downs], [d[1] for d in downs]
    full_up = rows_product([(hidden, dup)], nf)
    full_up, d_sum, done, grad_context, o_sum = meet(
        (full_up, sum_rows(d_rows), done, grad_context, o_sum)
    )
    for k in range(step, nc):
        o_sum = meet(sum_step(o_sum, o_parts, k, nc))
    d_cols = gather_cols(d_sum)
    u_rows = send_rows(full_up)
    back = []
    for n in range(seqs):
        at = slice((n % own_seqs) * length, (n % own_seqs + 1) * length)
        back.append(
            attend_back(
                done[n][1], done[n][2], grad_context[n // own_seqs][at],
                offs, prefix[n : n + 1], tables,
            )
        )
        back, done, grad_context = meet((back, done, grad_context))
    dqkv = [jnp.concatenate(back[n * own_seqs : (n + 1) * own_seqs]) for n in range(nt)]
    u_sum, dqkv, hidden, grad = meet((sum_rows(u_rows), dqkv, hidden, grad))
    qo_full = rows_product([(hidden, dqkv), (grad, context)], nf)
    qo_full, dqkv, dup, u_sum, d_cols = meet((qo_full, dqkv, dup, u_sum, d_cols))
    u_cols = gather_cols(u_sum)
    qo = send_rows(qo_full)
    theirs, dup, dqkv = meet(
        ([pair_product(dup[k], dqkv[k], w_first) for k in range(1, nt)], dup, dqkv)
    )
    h_got = [xor_swap(t, "tp", nt, k) for k, t in zip(range(1, nt), theirs)]
    h_got, h_mine = meet((h_got, pair_product(dup[0], dqkv[0], w_first)))
    h_parts = parts_of(h_mine, h_got)
    col_sum = lambda a: jnp.sum(a.astype(F32), axis=0)
    bias_sums = jnp.concatenate(
        [total([col_sum(a) for a in array]) for array in (dqkv, dup, grad)]
    )[None]
    bias_sums = jnp.sum(to_all(bias_sums, "fsdp", nf).reshape(nf, -1), axis=0)
    h_sum = meet(sum_step(None, h_parts, 1, nc))
    qo = [sum_rows(qo)]
    for k in range(2, nc + 1):
        if k < nc:
            h_sum = sum_step(h_sum, h_parts, k, nc)
        qo = gather_on(qo)
        qo, h_sum = meet((qo, h_sum))
        if k == nc - 1:
            grad_hidden = total(h_parts(0) + list(h_sum))

    gs = grad_hidden * gain
    grad_normed = inv_std * (
        gs - jnp.mean(gs, axis=-1, keepdims=True)
        - normed * jnp.mean(gs * normed, axis=-1, keepdims=True)
    )
    in_own = g_own.astype(F32) + grad_normed
    norm_sums = jnp.concatenate([col_sum(grad_hidden * normed), col_sum(grad_hidden)])
    out_own = total([x] + o_parts(0) + list(o_sum) + [out_bias, down_bias])

    def whole_tokens(own_rows):
        mine = own_rows.astype(BF16).reshape(1, own_seqs, rows, width)
        pieces = [mine] + [xor_swap(mine, "tp", nt, k) for k in range(1, nt)]
        full = jnp.zeros((nt, own_seqs, rows, width), BF16)
        for k in range(nt):
            full = lax.dynamic_update_slice_in_dim(full, pieces[k], ti ^ k, axis=0)
        return full.reshape(seqs, rows, width)

    output = whole_tokens(out_own)
    input_grad = whole_tokens(in_own)

    dw_down = widen(d_cols)
    dw_up = widen(u_cols)
    dw_qkv = place(qo, ci, pairs)

    small = 3 * inner + units
    obias = bias_sums[small:]
    got = to_all(jnp.concatenate([bias_sums[:small], norm_sums])[None], "ctx", nc).reshape(nc, -1)
    qkv_sums = got[:, : 3 * inner].reshape(nc, pairs, 3, PAIR)
    qb, kb, vb = (qkv_sums[:, :, n].reshape(nc * inner) for n in range(3))
    ub = got[:, 3 * inner : small].reshape(nc * units)
    norm_sums = jnp.sum(got[:, small:], axis=0)[None]
    norm_sums = jnp.sum(to_all(norm_sums, "fsdp", nf).reshape(nf, -1), axis=0)
    norm_sums = total([norm_sums] + [xor_swap(norm_sums, "tp", nt, k) for k in range(1, nt)])
    norm_sums = norm_sums.reshape(2, width)

    return (
        output, input_grad, norm_sums[0], norm_sums[1],
        dw_qkv[0], qb, dw_qkv[1], kb, dw_qkv[2], vb,
        dw_qkv[3], dw_up, ub, dw_down, obias,
    )


def solution(mesh):
    rows, flat, cols, one = P("fsdp", "ctx", None), P("fsdp", "tp"), P("tp"), P()
    return jax.shard_map(
        local,
        mesh=mesh,
        in_specs=(
            rows, rows, P("fsdp"), one, one, one,
            flat, cols, flat, cols, flat, cols, flat, one, flat, cols, flat, one,
        ),
        out_specs=(
            rows, rows, one, one, flat, cols, flat, cols, flat, cols, flat, flat, cols, flat, one,
        ),
        check_vma=False,
    )
```

```python
import functools

import jax
import jax.numpy as jnp
from jax import lax
from jax.experimental import pallas as pl
from jax.experimental.pallas import tpu as pltpu
from jax.sharding import PartitionSpec as P

HD = 64
ROT = 32
HALF = ROT // 2
PAIR = 2 * HD
NEG = -1e30
EPS = 1e-05
LOG2E = 1.4426950408889634
GELU_C = 0.7978845608028654
GELU_A = 0.044715
F32 = jnp.float32
BF16 = jnp.bfloat16


def meet(tree):
    return lax.optimization_barrier(tree)


def total(addends):
    out = addends[0].astype(F32)
    for one in addends[1:]:
        out = out + one.astype(F32)
    return out


def xor_swap(value, axis, size, step):
    return lax.ppermute(value, axis, [(j, j ^ step) for j in range(size)])


def to_all(value, axis, size):
    return lax.all_to_all(jnp.broadcast_to(value[None], (size,) + value.shape), axis, 0, 0, tiled=True)


def gather_step(sides, step, size, axis="ctx"):
    left, right = sides
    return (
        lax.ppermute(left, axis, [(j, j + 1) for j in range(step - 1, size - 1)]),
        lax.ppermute(right, axis, [(j, j - 1) for j in range(1, size - step + 1)]),
    )


def sum_step(sides, parts, step, size, axis="ctx"):
    a, b = parts(step), parts(size - step)
    if sides is not None:
        a, b = a + [sides[0]], b + [sides[1]]
    return (
        lax.ppermute(
            total(a).astype(BF16), axis, [(j, j + 1) for j in range(min(step, size - 1))]
        ),
        lax.ppermute(
            total(b).astype(BF16), axis, [(j, j - 1) for j in range(max(size - step, 1), size)]
        ),
    )


def by_distance(blocks, here):
    n = len(blocks)
    return [blocks[0]] + [
        jnp.where(here >= m, blocks[m][0], blocks[n - m][1]) for m in range(1, n)
    ]


FREE = pl.CostEstimate(flops=1, transcendentals=0, bytes_accessed=1)


def rotate(x, cos, sa, sb):
    return (
        x * cos + pltpu.roll(x, PAIR - HALF, axis=1) * sa + pltpu.roll(x, HALF, axis=1) * sb
    )


def masked_scores(k_s, qt, prefix, first, reach, clear):
    s = jnp.dot(k_s[0:reach, :], qt, preferred_element_type=F32) * LOG2E
    count = qt.shape[1]
    kpos = clear + lax.broadcasted_iota(jnp.int32, (reach - clear, count), 0)
    qpos = first + lax.broadcasted_iota(jnp.int32, (1, count), 1)
    tail = jnp.where(kpos < jnp.maximum(qpos + 1, prefix), s[clear:reach], NEG)
    return jnp.concatenate([s[:clear], tail], axis=0) if clear else tail


def spans(length, qblock, most):
    for first in range(0, length, qblock):
        yield first, max(first + qblock, most), first if first >= most else 0


def keep_head(x, h):
    lane = lax.broadcasted_iota(jnp.int32, x.shape, 1)
    return jnp.where((lane >= h * HD) & (lane < (h + 1) * HD), x, 0.0)


def attend_kernel(
    glen, qblock, most,
    offs_ref, prefix_ref,
    qkv_ref, cos_ref, sa_ref, sb_ref,
    ctx_ref, sorted_ref, stat_ref,
    qtm, k_s, vt_s, ot,
):
    length = cos_ref.shape[0]
    for p in range(length // glen):
        rows = pl.ds(pl.multiple_of(offs_ref[p], glen), glen)
        to = slice(p * glen, (p + 1) * glen)
        cos, sa, sb = cos_ref[to, :], sa_ref[to, :], sb_ref[to, :]
        q = rotate(qkv_ref[rows, 0:PAIR], cos, sa, sb).astype(BF16).astype(F32) * (HD**-0.5)
        sorted_ref[to, 0:PAIR] = q.astype(BF16)
        k = rotate(qkv_ref[rows, PAIR : 2 * PAIR], cos, sa, sb).astype(BF16)
        k_s[to, :] = k
        sorted_ref[to, PAIR : 2 * PAIR] = k
        sorted_ref[to, 2 * PAIR : 3 * PAIR] = qkv_ref[rows, 2 * PAIR : 3 * PAIR].astype(BF16)
    q = sorted_ref[:, 0:PAIR].astype(F32)
    for h in range(2):
        qtm[h] = keep_head(q, h).astype(BF16).T
    vt_s[...] = sorted_ref[:, 2 * PAIR : 3 * PAIR].T.reshape(2, HD, length)
    prefix = prefix_ref[0]
    for first, reach, clear in spans(length, qblock, most):
        cols = slice(first, first + qblock)

        def head(h, _):
            s = masked_scores(k_s, qtm[h, :, cols], prefix, first, reach, clear)
            top = jnp.max(s, axis=0, keepdims=True)
            e = jnp.exp2(s - top)
            scale = 1.0 / jnp.sum(e, axis=0, keepdims=True)
            stat_ref[0, h, 0:1, cols] = top
            stat_ref[0, h, 1:2, cols] = scale
            low = (e * scale).astype(BF16)
            ot[h, :, cols] = jnp.dot(vt_s[h, :, 0:reach], low, preferred_element_type=F32)
            return 0

        lax.fori_loop(0, 2, head, 0)
    for p in range(length // glen):
        rows = pl.ds(pl.multiple_of(offs_ref[p], glen), glen)
        to = slice(p * glen, (p + 1) * glen)
        ctx_ref[rows, :] = ot[:, :, to].reshape(PAIR, glen).T.astype(BF16)


def attend_back_kernel(
    glen, qblock, most,
    offs_ref, prefix_ref,
    sorted_ref, stat_ref, do_ref, cos_ref, sa_ref, sb_ref,
    dqkv_ref,
    qm, qtm, k_s, kt_s, v_s, dom, dotm, dqt, dk_acc, dv_acc,
):
    length = cos_ref.shape[0]
    k_s[...] = sorted_ref[:, PAIR : 2 * PAIR]
    v_s[...] = sorted_ref[:, 2 * PAIR : 3 * PAIR]
    q = sorted_ref[:, 0:PAIR].astype(F32)
    for p in range(length // glen):
        rows = pl.ds(pl.multiple_of(offs_ref[p], glen), glen)
        to = slice(p * glen, (p + 1) * glen)
        do = do_ref[rows, :].astype(F32)
        for h in range(2):
            dom[h, to, :] = keep_head(do, h).astype(BF16)
    for h in range(2):
        qm[h] = keep_head(q, h).astype(BF16)
        qtm[h] = qm[h].T
        dotm[h] = dom[h].T
    kt_s[...] = k_s[...].T.reshape(2, HD, length)
    dk_acc[...] = jnp.zeros_like(dk_acc)
    dv_acc[...] = jnp.zeros_like(dv_acc)
    prefix = prefix_ref[0]
    dot = functools.partial(jnp.dot, preferred_element_type=F32)
    for first, reach, clear in spans(length, qblock, most):
        cols = slice(first, first + qblock)

        def head(h, _):
            s = masked_scores(k_s, qtm[h, :, cols], prefix, first, reach, clear)
            prob = jnp.exp2(s - stat_ref[0, h, 0:1, cols]) * stat_ref[0, h, 1:2, cols]
            dv_acc[0:reach, :] += dot(prob.astype(BF16), dom[h, cols, :])
            dp = dot(v_s[0:reach, :], dotm[h, :, cols])
            delta = jnp.sum(prob * dp, axis=0, keepdims=True)
            ds = (prob * (dp - delta)).astype(BF16)
            dqt[h, :, cols] = dot(kt_s[h, :, 0:reach], ds)
            dk_acc[0:reach, :] += dot(ds, qm[h, cols, :])
            return 0

        lax.fori_loop(0, 2, head, 0)
    for p in range(length // glen):
        rows = pl.ds(pl.multiple_of(offs_ref[p], glen), glen)
        to = slice(p * glen, (p + 1) * glen)
        cos, sa, sb = cos_ref[to, :], -sa_ref[to, :], -sb_ref[to, :]
        dq = dqt[:, :, to].reshape(PAIR, glen).T * (HD**-0.5)
        dqkv_ref[rows, 0:PAIR] = rotate(dq, cos, sa, sb).astype(BF16)
        dqkv_ref[rows, PAIR : 2 * PAIR] = rotate(dk_acc[to, :], cos, sa, sb).astype(BF16)
        dqkv_ref[rows, 2 * PAIR : 3 * PAIR] = dv_acc[to, :].astype(BF16)


def attention_specs(length):
    whole = pl.BlockSpec((length, PAIR), lambda p, *_: (0, 0))
    wide = pl.BlockSpec((length, 3 * PAIR), lambda p, *_: (0, p))
    narrow = pl.BlockSpec((length, PAIR), lambda p, *_: (0, p))
    stat = pl.BlockSpec((1, 2, 2, length), lambda p, *_: (p, 0, 0, 0))
    return whole, wide, narrow, stat


def attend(qkv, offs, prefix, tables):
    length, inner = qkv.shape[0], qkv.shape[1] // 3
    whole, wide, narrow, stat = attention_specs(length)
    vm = pltpu.VMEM
    return pl.pallas_call(
        functools.partial(attend_kernel, length // offs.shape[0], min(256, length), length // 2),
        out_shape=(
            jax.ShapeDtypeStruct((length, inner), BF16),
            jax.ShapeDtypeStruct((length, 3 * inner), BF16),
            jax.ShapeDtypeStruct((inner // PAIR, 2, 2, length), F32),
        ),
        grid_spec=pltpu.PrefetchScalarGridSpec(
            num_scalar_prefetch=2,
            grid=(inner // PAIR,),
            in_specs=[wide, whole, whole, whole],
            out_specs=(narrow, wide, stat),
            scratch_shapes=[
                vm((2, PAIR, length), BF16),
                vm((length, PAIR), BF16),
                vm((2, HD, length), BF16),
                vm((2, HD, length), F32),
            ],
        ),
        compiler_params=pltpu.CompilerParams(vmem_limit_bytes=40 << 20),
        cost_estimate=FREE,
        name="attend",
    )(offs, prefix, qkv, *tables)


def attend_back(ordered, stats, grad_context, offs, prefix, tables):
    length, inner = grad_context.shape
    whole, wide, narrow, stat = attention_specs(length)
    vm = pltpu.VMEM
    return pl.pallas_call(
        functools.partial(
            attend_back_kernel, length // offs.shape[0], min(256, length), length // 2
        ),
        out_shape=jax.ShapeDtypeStruct((length, 3 * inner), BF16),
        grid_spec=pltpu.PrefetchScalarGridSpec(
            num_scalar_prefetch=2,
            grid=(inner // PAIR,),
            in_specs=[wide, stat, narrow, whole, whole, whole],
            out_specs=wide,
            scratch_shapes=[
                vm((2, length, PAIR), BF16),
                vm((2, PAIR, length), BF16),
                vm((length, PAIR), BF16),
                vm((2, HD, length), BF16),
                vm((length, PAIR), BF16),
                vm((2, length, PAIR), BF16),
                vm((2, PAIR, length), BF16),
                vm((2, HD, length), F32),
                vm((length, PAIR), F32),
                vm((length, PAIR), F32),
            ],
        ),
        compiler_params=pltpu.CompilerParams(vmem_limit_bytes=40 << 20),
        cost_estimate=FREE,
        name="attend_back",
    )(offs, prefix, ordered, stats, grad_context, *tables)


def pair_kernel(split, a_ref, b_ref, w_ref, *refs):
    nt = (((1,), (1,)), ((), ()))
    o = lax.dot_general(a_ref[...], w_ref[:, :split], nt, preferred_element_type=F32)
    o += lax.dot_general(b_ref[...], w_ref[:, split:], nt, preferred_element_type=F32)
    for more in refs[:-1]:
        o += more[...].astype(F32)
    refs[-1][...] = o.astype(refs[-1].dtype)


def pair_product(a, b, w, more=()):
    n, depth = w.shape
    m = a.shape[0]
    bn = min(512, n)
    out = pl.BlockSpec((m, bn), lambda j: (0, j))
    return pl.pallas_call(
        functools.partial(pair_kernel, a.shape[1]),
        out_shape=jax.ShapeDtypeStruct((m, n), BF16),
        grid=(n // bn,),
        in_specs=[
            pl.BlockSpec((m, a.shape[1]), lambda j: (0, 0), pipeline_mode=pl.Buffered(1)),
            pl.BlockSpec((m, b.shape[1]), lambda j: (0, 0), pipeline_mode=pl.Buffered(1)),
            pl.BlockSpec((bn, depth), lambda j: (j, 0)),
        ]
        + [out] * len(more),
        out_specs=out,
        compiler_params=pltpu.CompilerParams(vmem_limit_bytes=48 << 20),
        cost_estimate=FREE,
        name="pair_product",
    )(a, b, w, *more)


def pack_kernel(pieces, here_ref, *refs):
    o_ref = refs[-1]
    at = 0
    for n, start, size in pieces:
        o_ref[0, :, at : at + size] = refs[n][:, start : start + size]
        at += size


def pack_columns(weights, pieces, here, places, copies):
    rows = weights[0].shape[0]
    span = sum(size for _, _, size in pieces)
    return pl.pallas_call(
        functools.partial(pack_kernel, pieces),
        out_shape=jax.ShapeDtypeStruct((copies, rows, span), weights[0].dtype),
        grid_spec=pltpu.PrefetchScalarGridSpec(
            num_scalar_prefetch=1,
            grid=(copies,),
            in_specs=[
                pl.BlockSpec((rows, w.shape[1] // places), lambda i, h: (0, h[0])) for w in weights
            ],
            out_specs=pl.BlockSpec((1, rows, span), lambda i, h: (i, 0, 0)),
        ),
        compiler_params=pltpu.CompilerParams(vmem_limit_bytes=40 << 20),
        cost_estimate=FREE,
        name="pack_columns",
    )(here.reshape(1), *weights)


def rows_kernel(counts, *refs):
    o_ref = refs[-1]
    tn = (((0,), (0,)), ((), ()))
    at, col = 0, 0
    for count in counts:
        o = 0.0
        for n in range(count):
            o += lax.dot_general(
                refs[at + n][...], refs[at + count + n][...], tn, preferred_element_type=F32
            )
        o_ref[0, :, col : col + o.shape[1]] = o.astype(o_ref.dtype)
        at, col = at + 2 * count, col + o.shape[1]


def rows_product(products, owners):
    args, specs, columns = [], [], 0
    for a, b in products:
        bm = a[0].shape[1] // owners
        args += [*a, *b]
        specs += [pl.BlockSpec((x.shape[0], bm), lambda i: (0, i)) for x in a]
        specs += [
            pl.BlockSpec(x.shape, lambda i: (0, 0), pipeline_mode=pl.Buffered(1)) for x in b
        ]
        columns += b[0].shape[1]
    return pl.pallas_call(
        functools.partial(rows_kernel, [len(a) for a, _ in products]),
        out_shape=jax.ShapeDtypeStruct((owners, bm, columns), BF16),
        grid=(owners,),
        in_specs=specs,
        out_specs=pl.BlockSpec((1, bm, columns), lambda i: (i, 0, 0)),
        compiler_params=pltpu.CompilerParams(vmem_limit_bytes=56 << 20),
        cost_estimate=FREE,
        name="rows_product",
    )(*args)


def order_kernel(size, here_ref, *refs):
    blocks, o_ref = refs[:-1], refs[-1]
    m, here = pl.program_id(0), here_ref[0]

    def put(ref):
        o_ref[0] = ref[...]

    pl.when(m == 0)(lambda: put(blocks[0]))
    for k in range(1, size):
        pl.when((m == k) & (here >= k))(functools.partial(put, blocks[k]))
        pl.when((m == k) & (here < k))(functools.partial(put, blocks[2 * size - 1 - k]))


def in_order(blocks, here):
    size = len(blocks)
    rows, span = blocks[0].shape
    blocks = [blocks[0]] + [x[0] for x in blocks[1:]] + [x[1] for x in blocks[1:]]
    return pl.pallas_call(
        functools.partial(order_kernel, size),
        out_shape=jax.ShapeDtypeStruct((size, rows, span), blocks[0].dtype),
        grid_spec=pltpu.PrefetchScalarGridSpec(
            num_scalar_prefetch=1,
            grid=(size,),
            in_specs=[pl.BlockSpec((rows, span), lambda m, h: (0, 0), pipeline_mode=pl.Buffered(1))]
            * len(blocks),
            out_specs=pl.BlockSpec(
                (1, rows, span), lambda m, h: (lax.rem(h[0] - m + size, size), 0, 0)
            ),
        ),
        compiler_params=pltpu.CompilerParams(vmem_limit_bytes=48 << 20),
        cost_estimate=FREE,
        name="in_order",
    )(here.reshape(1), *blocks)


def place_kernel(pairs, a_ref, *outs):
    starts = [[(p * 3 + n) * PAIR for p in range(pairs)] for n in range(3)]
    starts.append([(3 * pairs + p) * PAIR for p in range(pairs)])
    for out, at in zip(outs, starts):
        for p in range(pairs):
            out[:, p * PAIR : (p + 1) * PAIR] = a_ref[0, :, at[p] : at[p] + PAIR].astype(F32)


def place(blocks, pairs):
    n, rows, span = blocks.shape
    width = pairs * PAIR
    return pl.pallas_call(
        functools.partial(place_kernel, pairs),
        out_shape=(jax.ShapeDtypeStruct((rows, n * width), F32),) * 4,
        grid=(n,),
        in_specs=[pl.BlockSpec((1, rows, span), lambda c: (c, 0, 0))],
        out_specs=(pl.BlockSpec((rows, width), lambda c: (0, c)),) * 4,
        compiler_params=pltpu.CompilerParams(vmem_limit_bytes=48 << 20),
        cost_estimate=FREE,
        name="place",
    )(blocks)


def widen_kernel(a_ref, o_ref):
    o_ref[...] = a_ref[0].astype(F32)


def widen(blocks):
    n, rows, span = blocks.shape
    return pl.pallas_call(
        widen_kernel,
        out_shape=jax.ShapeDtypeStruct((rows, n * span), F32),
        grid=(n,),
        in_specs=[pl.BlockSpec((1, rows, span), lambda c: (c, 0, 0))],
        out_specs=pl.BlockSpec((rows, span), lambda c: (0, c)),
        compiler_params=pltpu.CompilerParams(vmem_limit_bytes=40 << 20),
        cost_estimate=FREE,
        name="widen",
    )(blocks)


def up_kernel(step, h_ref, w_ref, b_ref, act_ref, slope_ref):
    for c in range(0, act_ref.shape[1], step):
        up = jnp.dot(h_ref[...], w_ref[:, c : c + step], preferred_element_type=F32)
        act, slope = gelu_parts(up + b_ref[:, c : c + step])
        act_ref[:, c : c + step] = act.astype(BF16)
        slope_ref[:, c : c + step] = slope.astype(BF16)


def up_product(hidden, weight, bias):
    m, k = hidden.shape
    n = bias.shape[0]
    bm = min(512, m)
    return pl.pallas_call(
        functools.partial(up_kernel, min(256, n)),
        out_shape=(jax.ShapeDtypeStruct((m, n), BF16),) * 2,
        grid=(m // bm,),
        in_specs=[
            pl.BlockSpec((bm, k), lambda i: (i, 0)),
            pl.BlockSpec((k, n), lambda i: (0, 0), pipeline_mode=pl.Buffered(1)),
            pl.BlockSpec((1, n), lambda i: (0, 0)),
        ],
        out_specs=(pl.BlockSpec((bm, n), lambda i: (i, 0)),) * 2,
        compiler_params=pltpu.CompilerParams(vmem_limit_bytes=56 << 20),
        cost_estimate=FREE,
        name="up_product",
    )(hidden, weight, bias.reshape(1, n))


def down_kernel(units, g_ref, w_ref, s_ref, d_ref, c_ref):
    g = g_ref[...]
    d = jnp.dot(g, w_ref[:, :units], preferred_element_type=F32)
    d_ref[...] = (d * s_ref[...].astype(F32)).astype(BF16)
    c_ref[...] = jnp.dot(g, w_ref[:, units:], preferred_element_type=F32).astype(BF16)


def down_product(grad, weight, slope):
    m, k = grad.shape
    units, n = slope.shape[1], weight.shape[1]
    bm = min(512, m)
    return pl.pallas_call(
        functools.partial(down_kernel, units),
        out_shape=(
            jax.ShapeDtypeStruct((m, units), BF16),
            jax.ShapeDtypeStruct((m, n - units), BF16),
        ),
        grid=(m // bm,),
        in_specs=[
            pl.BlockSpec((bm, k), lambda i: (i, 0)),
            pl.BlockSpec((k, n), lambda i: (0, 0), pipeline_mode=pl.Buffered(1)),
            pl.BlockSpec((bm, units), lambda i: (i, 0)),
        ],
        out_specs=(
            pl.BlockSpec((bm, units), lambda i: (i, 0)),
            pl.BlockSpec((bm, n - units), lambda i: (i, 0)),
        ),
        compiler_params=pltpu.CompilerParams(vmem_limit_bytes=56 << 20),
        cost_estimate=FREE,
        name="down_product",
    )(grad, weight, slope)


def line_kernel(pieces, h_ref, *refs):
    b_ref, o_ref = refs[pieces], refs[-1]
    span = o_ref.shape[1] // pieces
    for n in range(pieces):
        to = slice(n * span, (n + 1) * span)
        o = jnp.dot(h_ref[...], refs[n][...], preferred_element_type=F32)
        o_ref[:, to] = o + b_ref[:, to]


def line_product(hidden, weight, bias, start, pieces):
    m, k = hidden.shape
    n = bias.shape[0]
    span = n // pieces
    bm = min(512, m)
    piece = lambda p: pl.BlockSpec(
        (k, span), lambda i: (0, start // span + p), pipeline_mode=pl.Buffered(1)
    )
    return pl.pallas_call(
        functools.partial(line_kernel, pieces),
        out_shape=jax.ShapeDtypeStruct((m, n), F32),
        grid=(m // bm,),
        in_specs=[pl.BlockSpec((bm, k), lambda i: (i, 0))]
        + [piece(p) for p in range(pieces)]
        + [pl.BlockSpec((1, n), lambda i: (0, 0))],
        out_specs=pl.BlockSpec((bm, n), lambda i: (i, 0)),
        compiler_params=pltpu.CompilerParams(vmem_limit_bytes=56 << 20),
        cost_estimate=FREE,
        name="line_product",
    )(hidden, *[weight] * pieces, bias.reshape(1, n))


def gelu_parts(up):
    square = up * up
    t = jnp.tanh(GELU_C * up * (1.0 + GELU_A * square))
    half = 0.5 * (1.0 + t)
    slope = half + 0.5 * up * (1.0 - t * t) * (GELU_C * (1.0 + 3.0 * GELU_A * square))
    return up * half, slope


def local(
    tokens, cotangent, prefix_len, group_order, ln_gain, ln_bias,
    query_weight, query_bias, key_weight, key_bias, value_weight, value_bias,
    out_weight, out_bias, up_weight, up_bias, down_weight, down_bias,
):
    nf, nc, nt = lax.axis_size("fsdp"), lax.axis_size("ctx"), lax.axis_size("tp")
    ci, ti = lax.axis_index("ctx").astype(jnp.int32), lax.axis_index("tp").astype(jnp.int32)
    seqs, rows, width = tokens.shape
    own_seqs = seqs // nt
    length = rows * nc
    own = own_seqs * rows
    db = width // nf
    inner = query_weight.shape[1] // nc
    units = up_weight.shape[1] // nc
    pairs = inner // PAIR

    def columns(w):
        return lax.dynamic_slice_in_dim(w, ci * (w.shape[-1] // nc), w.shape[-1] // nc, axis=-1)

    def by_pairs(arrays):
        return jnp.concatenate(
            [a[..., p * PAIR : (p + 1) * PAIR] for p in range(pairs) for a in arrays], axis=-1
        )

    x = lax.dynamic_slice_in_dim(tokens, ti * own_seqs, own_seqs, axis=0).reshape(own, width)
    g_own = lax.dynamic_slice_in_dim(cotangent, ti * own_seqs, own_seqs, axis=0).reshape(own, width)
    x = x.astype(F32)
    gain, shift = ln_gain.astype(F32), ln_bias.astype(F32)
    centred = x - jnp.mean(x, axis=-1, keepdims=True)
    inv_std = lax.rsqrt(jnp.mean(centred * centred, axis=-1, keepdims=True) + EPS)
    normed = centred * inv_std
    h_own = (normed * gain + shift).astype(BF16)

    h_in = [h_own]

    def side(blocks):
        return blocks[-1] if len(blocks) > 1 else (blocks[0], blocks[0])

    def gather_on(blocks):
        return blocks + [gather_step(side(blocks), len(blocks), nc)]

    cut = [
        (1 + n, p * PAIR, PAIR) for p in range(pairs) for n in range(3)
    ]
    h_own, early = meet(
        (h_own, (up_weight, query_weight, key_weight, value_weight, down_weight, out_weight))
    )
    first = pack_columns(early[:4], [(0, 0, units)] + cut, ci, nc, nf)
    second = pack_columns(early[4:], [(0, 0, units), (1, 0, inner)], ci, nc, nf)
    b_qkv = by_pairs([columns(query_bias), columns(key_bias), columns(value_bias)]).astype(F32)
    b_up = columns(up_bias).astype(F32)

    lane = jnp.arange(PAIR, dtype=jnp.int32)[None, :] % HD
    freq = jnp.power(10000.0, -2.0 * (lane % HALF).astype(F32) / ROT)
    angle = jnp.arange(length, dtype=jnp.int32).astype(F32)[:, None] * freq
    cos = jnp.where(lane < ROT, jnp.cos(angle), 1.0)
    sin = jnp.sin(angle)
    sa = jnp.where(lane < HALF, -sin, 0.0)
    sb = jnp.where((lane >= HALF) & (lane < ROT), sin, 0.0)
    groups = group_order.shape[0]
    glen = length // groups
    places = jnp.arange(groups, dtype=jnp.int32)
    slot = jnp.sum(
        jnp.where(group_order[None, :] == places[:, None], places[None, :], 0), axis=1
    ) * glen
    offs = slot
    seq_ids = jnp.arange(seqs, dtype=jnp.int32)
    seq_of = ((seq_ids // own_seqs) ^ ti) * own_seqs + seq_ids % own_seqs
    prefix = jnp.sum(
        jnp.where(seq_of[:, None] == seq_ids[None, :], prefix_len[None, :], 0), axis=1
    )
    offs, prefix = offs.astype(jnp.int32), prefix.astype(jnp.int32)

    tables = (cos, sa, sb)
    first_all = lax.all_to_all(first, "fsdp", 0, 0, tiled=True)
    h_in, second, tables, b_up, b_qkv, offs, prefix = meet(
        (gather_on(h_in), second, tables, b_up, b_qkv, offs, prefix)
    )
    while len(h_in) < nc:
        h_in = meet(gather_on(h_in))
    g_own, h_in = meet((g_own, h_in))
    g_all = lax.all_gather(g_own.reshape(own_seqs, rows, width), "ctx", axis=1, tiled=True)

    def halves(mine):
        mine = mine.reshape(own_seqs * length, width)
        return [mine] + [xor_swap(mine, "tp", nt, k) for k in range(1, nt)]

    def send_rows(full):
        return lax.all_to_all(full, "fsdp", 0, 0, tiled=True)

    def sum_rows(got):
        return total([got[k] for k in range(nf)]).astype(BF16)

    def gather_cols(mine):
        return lax.all_gather(mine, "ctx", axis=0, tiled=False)

    h_mine = jnp.moveaxis(in_order(h_in, ci).reshape(nc, own_seqs, rows, width), 1, 0)
    hidden = halves(h_mine)
    hidden, first_all = meet((hidden, first_all))
    w_first = first_all.reshape(width, units + 3 * inner)
    second_all = lax.all_to_all(second, "fsdp", 0, 0, tiled=True)
    ups, qkv = [], []
    for n in range(nt):
        ups.append(up_product(hidden[n], w_first, b_up))
        ups, hidden = meet((ups, hidden))
    for n in range(nt):
        qkv.append(line_product(hidden[n], w_first, b_qkv, units, 3))
        qkv, hidden = meet((qkv, hidden))
    act, slope = [u[0] for u in ups], [u[1] for u in ups]
    done = []
    for n in range(seqs):
        at = slice((n % own_seqs) * length, (n % own_seqs + 1) * length)
        done.append(attend(qkv[n // own_seqs][at], offs, prefix[n : n + 1], tables))
        done, qkv = meet((done, qkv))
    context = [
        jnp.concatenate([d[0] for d in done[n * own_seqs : (n + 1) * own_seqs]]) for n in range(nt)
    ]

    def parts_of(mine, got):
        grid = lambda a: a.reshape(own_seqs, nc, rows, width)
        mine, got = grid(mine), [grid(g) for g in got]

        def parts(m):
            at = (ci - m + nc) % nc
            pick = lambda a: lax.dynamic_index_in_dim(a, at, 1, keepdims=False).reshape(own, width)
            return [pick(mine)] + [pick(g) for g in got]

        return parts

    act, context, second_all, g_all = meet((act, context, second_all, g_all))
    w_second = second_all.reshape(width, units + inner)
    grad = halves(g_all)
    theirs, act, context = meet(
        ([pair_product(act[k], context[k], w_second) for k in range(1, nt)], act, context)
    )
    o_got = [xor_swap(t, "tp", nt, k) for k, t in zip(range(1, nt), theirs)]
    full_down = rows_product([(grad, act)], nf)
    grad, full_down, slope, o_got, act = meet((grad, full_down, slope, o_got, act))
    d_rows = send_rows(full_down)
    both = pair_product(act[0], context[0], w_second, o_got)
    both = jnp.moveaxis(both.reshape(own_seqs, nc, rows, width), 1, 0).reshape(nc, own, width)
    both, grad, slope = meet((both, grad, slope))
    o_sum = lax.psum_scatter(both, "ctx", scatter_dimension=0, tiled=True)
    downs = []
    for n in range(nt):
        downs.append(down_product(grad[n], w_second, slope[n]))
        downs, grad, hidden = meet((downs, grad, hidden))
    dup, grad_context = [d[0] for d in downs], [d[1] for d in downs]
    full_up = rows_product([(hidden, dup)], nf)
    full_up, d_rows = meet((full_up, d_rows))
    d_sum, done, grad_context = meet((sum_rows(d_rows), done, grad_context))
    u_rows = send_rows(full_up)
    back = []
    for n in range(seqs):
        at = slice((n % own_seqs) * length, (n % own_seqs + 1) * length)
        back.append(
            attend_back(
                done[n][1], done[n][2], grad_context[n // own_seqs][at],
                offs, prefix[n : n + 1], tables,
            )
        )
        back, done, grad_context, o_sum = meet((back, done, grad_context, o_sum))
        if n == 0:
            d_cols = gather_cols(d_sum)
    dqkv = [jnp.concatenate(back[n * own_seqs : (n + 1) * own_seqs]) for n in range(nt)]
    u_rows, dqkv, hidden, grad, dup = meet((u_rows, dqkv, hidden, grad, dup))

    theirs, dup, dqkv, hidden = meet(
        ([pair_product(dup[k], dqkv[k], w_first) for k in range(1, nt)], dup, dqkv, hidden)
    )
    h_got = [xor_swap(t, "tp", nt, k) for k, t in zip(range(1, nt), theirs)]
    u_sum = sum_rows(u_rows)
    qo_full = rows_product([(hidden, dqkv), (grad, context)], nf)
    qo_full, dqkv, dup, h_got, u_sum = meet((qo_full, dqkv, dup, h_got, u_sum))
    qo = send_rows(qo_full)
    h_both, d_cols, u_sum = meet((pair_product(dup[0], dqkv[0], w_first, h_got), d_cols, u_sum))
    u_cols = gather_cols(u_sum)
    h_parts = parts_of(h_both, [])
    dw_down = widen(d_cols)
    h_sum, qo, dw_down = meet((sum_step(None, h_parts, 1, nc), qo, dw_down))
    qo_sum = sum_rows(qo)
    for k in range(2, nc):
        h_sum = sum_step(h_sum, h_parts, k, nc)
        if k == 2:
            h_sum, qo_sum = meet((h_sum, qo_sum))
        h_sum = meet(h_sum)
    grad_hidden = total(h_parts(0) + list(h_sum))
    u_cols, h_sum = meet((u_cols, h_sum))
    dw_up = widen(u_cols)
    qo_cols = gather_cols(qo_sum)
    col_sum = lambda a: jnp.sum(a.astype(F32), axis=0)
    out_own = total([x, o_sum.reshape(own, width), out_bias, down_bias])

    gs = grad_hidden * gain
    grad_normed = inv_std * (
        gs - jnp.mean(gs, axis=-1, keepdims=True)
        - normed * jnp.mean(gs * normed, axis=-1, keepdims=True)
    )
    in_own = g_own.astype(F32) + grad_normed
    norm_sums = jnp.concatenate([col_sum(grad_hidden * normed), col_sum(grad_hidden)])

    def whole_tokens(own_rows):
        mine = own_rows.astype(BF16).reshape(1, own_seqs, rows, width)
        pieces = [mine] + [xor_swap(mine, "tp", nt, k) for k in range(1, nt)]
        full = jnp.zeros((nt, own_seqs, rows, width), BF16)
        for k in range(nt):
            full = lax.dynamic_update_slice_in_dim(full, pieces[k], ti ^ k, axis=0)
        return full.reshape(seqs, rows, width)

    output = whole_tokens(out_own)
    input_grad = whole_tokens(in_own)

    dw_qkv = place(qo_cols, pairs)

    bias_sums = jnp.concatenate(
        [total([col_sum(a) for a in array]) for array in (dqkv, dup, grad)]
    )[None]
    bias_sums = jnp.sum(to_all(bias_sums, "fsdp", nf).reshape(nf, -1), axis=0)
    small = 3 * inner + units
    obias = bias_sums[small:]
    got = to_all(jnp.concatenate([bias_sums[:small], norm_sums])[None], "ctx", nc).reshape(nc, -1)
    qkv_sums = got[:, : 3 * inner].reshape(nc, pairs, 3, PAIR)
    qb, kb, vb = (qkv_sums[:, :, n].reshape(nc * inner) for n in range(3))
    ub = got[:, 3 * inner : small].reshape(nc * units)
    norm_sums = jnp.sum(got[:, small:], axis=0)[None]
    norm_sums = jnp.sum(to_all(norm_sums, "fsdp", nf).reshape(nf, -1), axis=0)
    norm_sums = total([norm_sums] + [xor_swap(norm_sums, "tp", nt, k) for k in range(1, nt)])
    norm_sums = norm_sums.reshape(2, width)

    return (
        output, input_grad, norm_sums[0], norm_sums[1],
        dw_qkv[0], qb, dw_qkv[1], kb, dw_qkv[2], vb,
        dw_qkv[3], dw_up, ub, dw_down, obias,
    )


def solution(mesh):
    rows, flat, cols, one = P("fsdp", "ctx", None), P("fsdp", "tp"), P("tp"), P()
    return jax.shard_map(
        local,
        mesh=mesh,
        in_specs=(
            rows, rows, P("fsdp"), one, one, one,
            flat, cols, flat, cols, flat, cols, flat, one, flat, cols, flat, one,
        ),
        out_specs=(
            rows, rows, one, one, flat, cols, flat, cols, flat, cols, flat, flat, cols, flat, one,
        ),
        check_vma=False,
    )
```

```python
import functools

import jax
import jax.numpy as jnp
from jax import lax
from jax.experimental import pallas as pl
from jax.experimental.pallas import tpu as pltpu
from jax.sharding import PartitionSpec as P

HD = 64
ROT = 32
HALF = ROT // 2
PAIR = 2 * HD
NEG = -1e30
EPS = 1e-05
LOG2E = 1.4426950408889634
GELU_C = 0.7978845608028654
GELU_A = 0.044715
F32 = jnp.float32
BF16 = jnp.bfloat16


def meet(tree):
    return lax.optimization_barrier(tree)


def total(addends):
    out = addends[0].astype(F32)
    for one in addends[1:]:
        out = out + one.astype(F32)
    return out


def xor_swap(value, axis, size, step):
    return lax.ppermute(value, axis, [(j, j ^ step) for j in range(size)])


def to_all(value, axis, size):
    return lax.all_to_all(jnp.broadcast_to(value[None], (size,) + value.shape), axis, 0, 0, tiled=True)


def gather_step(sides, step, size, axis="ctx"):
    left, right = sides
    return (
        lax.ppermute(left, axis, [(j, j + 1) for j in range(step - 1, size - 1)]),
        lax.ppermute(right, axis, [(j, j - 1) for j in range(1, size - step + 1)]),
    )


def sum_step(sides, parts, step, size, axis="ctx"):
    a, b = parts(step), parts(size - step)
    if sides is not None:
        a, b = a + [sides[0]], b + [sides[1]]
    return (
        lax.ppermute(
            total(a).astype(BF16), axis, [(j, j + 1) for j in range(min(step, size - 1))]
        ),
        lax.ppermute(
            total(b).astype(BF16), axis, [(j, j - 1) for j in range(max(size - step, 1), size)]
        ),
    )


def by_distance(blocks, here):
    n = len(blocks)
    return [blocks[0]] + [
        jnp.where(here >= m, blocks[m][0], blocks[n - m][1]) for m in range(1, n)
    ]


def in_hbm(arrays):
    return [pltpu.with_memory_space_constraint(a, pltpu.HBM) for a in arrays]


FREE = pl.CostEstimate(flops=1, transcendentals=0, bytes_accessed=1)


def rotate(x, cos, sa, sb):
    return (
        x * cos + pltpu.roll(x, PAIR - HALF, axis=1) * sa + pltpu.roll(x, HALF, axis=1) * sb
    )


def masked_scores(k_s, qt, prefix, first, reach, clear):
    s = jnp.dot(k_s[0:reach, :], qt, preferred_element_type=F32) * LOG2E
    count = qt.shape[1]
    kpos = clear + lax.broadcasted_iota(jnp.int32, (reach - clear, count), 0)
    qpos = first + lax.broadcasted_iota(jnp.int32, (1, count), 1)
    tail = jnp.where(kpos < jnp.maximum(qpos + 1, prefix), s[clear:reach], NEG)
    return jnp.concatenate([s[:clear], tail], axis=0) if clear else tail


def spans(length, qblock, most):
    for first in range(0, length, qblock):
        yield first, max(first + qblock, most), first if first >= most else 0


def keep_head(x, h):
    lane = lax.broadcasted_iota(jnp.int32, x.shape, 1)
    return jnp.where((lane >= h * HD) & (lane < (h + 1) * HD), x, 0.0)


def attend_kernel(
    glen, qblock, most,
    offs_ref, prefix_ref,
    qkv_ref, cos_ref, sa_ref, sb_ref,
    ctx_ref, sorted_ref, stat_ref,
    qtm, k_s, vt_s, ot,
):
    length = cos_ref.shape[0]
    for p in range(length // glen):
        rows = pl.ds(pl.multiple_of(offs_ref[p], glen), glen)
        to = slice(p * glen, (p + 1) * glen)
        cos, sa, sb = cos_ref[to, :], sa_ref[to, :], sb_ref[to, :]
        q = rotate(qkv_ref[rows, 0:PAIR], cos, sa, sb).astype(BF16).astype(F32) * (HD**-0.5)
        sorted_ref[to, 0:PAIR] = q.astype(BF16)
        k = rotate(qkv_ref[rows, PAIR : 2 * PAIR], cos, sa, sb).astype(BF16)
        k_s[to, :] = k
        sorted_ref[to, PAIR : 2 * PAIR] = k
        sorted_ref[to, 2 * PAIR : 3 * PAIR] = qkv_ref[rows, 2 * PAIR : 3 * PAIR].astype(BF16)
    q = sorted_ref[:, 0:PAIR].astype(F32)
    for h in range(2):
        qtm[h] = keep_head(q, h).astype(BF16).T
    vt_s[...] = sorted_ref[:, 2 * PAIR : 3 * PAIR].T.reshape(2, HD, length)
    prefix = prefix_ref[0]
    for first, reach, clear in spans(length, qblock, most):
        cols = slice(first, first + qblock)

        def head(h, _):
            s = masked_scores(k_s, qtm[h, :, cols], prefix, first, reach, clear)
            top = jnp.max(s, axis=0, keepdims=True)
            e = jnp.exp2(s - top)
            scale = 1.0 / jnp.sum(e, axis=0, keepdims=True)
            stat_ref[0, h, 0:1, cols] = top
            stat_ref[0, h, 1:2, cols] = scale
            low = (e * scale).astype(BF16)
            ot[h, :, cols] = jnp.dot(vt_s[h, :, 0:reach], low, preferred_element_type=F32)
            return 0

        lax.fori_loop(0, 2, head, 0)
    for p in range(length // glen):
        rows = pl.ds(pl.multiple_of(offs_ref[p], glen), glen)
        to = slice(p * glen, (p + 1) * glen)
        ctx_ref[rows, :] = ot[:, :, to].reshape(PAIR, glen).T.astype(BF16)


def attend_back_kernel(
    glen, qblock, most,
    offs_ref, prefix_ref,
    sorted_ref, stat_ref, do_ref, cos_ref, sa_ref, sb_ref,
    dqkv_ref,
    qm, qtm, k_s, kt_s, v_s, dom, dotm, dqt, dk_acc, dv_acc,
):
    length = cos_ref.shape[0]
    k_s[...] = sorted_ref[:, PAIR : 2 * PAIR]
    v_s[...] = sorted_ref[:, 2 * PAIR : 3 * PAIR]
    q = sorted_ref[:, 0:PAIR].astype(F32)
    for p in range(length // glen):
        rows = pl.ds(pl.multiple_of(offs_ref[p], glen), glen)
        to = slice(p * glen, (p + 1) * glen)
        do = do_ref[rows, :].astype(F32)
        for h in range(2):
            dom[h, to, :] = keep_head(do, h).astype(BF16)
    for h in range(2):
        qm[h] = keep_head(q, h).astype(BF16)
        qtm[h] = qm[h].T
        dotm[h] = dom[h].T
    kt_s[...] = k_s[...].T.reshape(2, HD, length)
    dk_acc[...] = jnp.zeros_like(dk_acc)
    dv_acc[...] = jnp.zeros_like(dv_acc)
    prefix = prefix_ref[0]
    dot = functools.partial(jnp.dot, preferred_element_type=F32)
    for first, reach, clear in spans(length, qblock, most):
        cols = slice(first, first + qblock)

        def head(h, _):
            s = masked_scores(k_s, qtm[h, :, cols], prefix, first, reach, clear)
            prob = jnp.exp2(s - stat_ref[0, h, 0:1, cols]) * stat_ref[0, h, 1:2, cols]
            dv_acc[0:reach, :] += dot(prob.astype(BF16), dom[h, cols, :])
            dp = dot(v_s[0:reach, :], dotm[h, :, cols])
            delta = jnp.sum(prob * dp, axis=0, keepdims=True)
            ds = (prob * (dp - delta)).astype(BF16)
            dqt[h, :, cols] = dot(kt_s[h, :, 0:reach], ds)
            dk_acc[0:reach, :] += dot(ds, qm[h, cols, :])
            return 0

        lax.fori_loop(0, 2, head, 0)
    for p in range(length // glen):
        rows = pl.ds(pl.multiple_of(offs_ref[p], glen), glen)
        to = slice(p * glen, (p + 1) * glen)
        cos, sa, sb = cos_ref[to, :], -sa_ref[to, :], -sb_ref[to, :]
        dq = dqt[:, :, to].reshape(PAIR, glen).T * (HD**-0.5)
        dqkv_ref[rows, 0:PAIR] = rotate(dq, cos, sa, sb).astype(BF16)
        dqkv_ref[rows, PAIR : 2 * PAIR] = rotate(dk_acc[to, :], cos, sa, sb).astype(BF16)
        dqkv_ref[rows, 2 * PAIR : 3 * PAIR] = dv_acc[to, :].astype(BF16)


def attention_specs(length):
    whole = pl.BlockSpec((length, PAIR), lambda p, *_: (0, 0))
    wide = pl.BlockSpec((length, 3 * PAIR), lambda p, *_: (0, p))
    narrow = pl.BlockSpec((length, PAIR), lambda p, *_: (0, p))
    stat = pl.BlockSpec((1, 2, 2, length), lambda p, *_: (p, 0, 0, 0))
    return whole, wide, narrow, stat


def attend(qkv, offs, prefix, tables):
    length, inner = qkv.shape[0], qkv.shape[1] // 3
    whole, wide, narrow, stat = attention_specs(length)
    vm = pltpu.VMEM
    return pl.pallas_call(
        functools.partial(attend_kernel, length // offs.shape[0], min(256, length), length // 2),
        out_shape=(
            jax.ShapeDtypeStruct((length, inner), BF16),
            jax.ShapeDtypeStruct((length, 3 * inner), BF16),
            jax.ShapeDtypeStruct((inner // PAIR, 2, 2, length), F32),
        ),
        grid_spec=pltpu.PrefetchScalarGridSpec(
            num_scalar_prefetch=2,
            grid=(inner // PAIR,),
            in_specs=[wide, whole, whole, whole],
            out_specs=(narrow, wide, stat),
            scratch_shapes=[
                vm((2, PAIR, length), BF16),
                vm((length, PAIR), BF16),
                vm((2, HD, length), BF16),
                vm((2, HD, length), F32),
            ],
        ),
        compiler_params=pltpu.CompilerParams(vmem_limit_bytes=40 << 20),
        cost_estimate=FREE,
        name="attend",
    )(offs, prefix, qkv, *tables)


def attend_back(ordered, stats, grad_context, offs, prefix, tables):
    length, inner = grad_context.shape
    whole, wide, narrow, stat = attention_specs(length)
    vm = pltpu.VMEM
    return pl.pallas_call(
        functools.partial(
            attend_back_kernel, length // offs.shape[0], min(256, length), length // 2
        ),
        out_shape=jax.ShapeDtypeStruct((length, 3 * inner), BF16),
        grid_spec=pltpu.PrefetchScalarGridSpec(
            num_scalar_prefetch=2,
            grid=(inner // PAIR,),
            in_specs=[wide, stat, narrow, whole, whole, whole],
            out_specs=wide,
            scratch_shapes=[
                vm((2, length, PAIR), BF16),
                vm((2, PAIR, length), BF16),
                vm((length, PAIR), BF16),
                vm((2, HD, length), BF16),
                vm((length, PAIR), BF16),
                vm((2, length, PAIR), BF16),
                vm((2, PAIR, length), BF16),
                vm((2, HD, length), F32),
                vm((length, PAIR), F32),
                vm((length, PAIR), F32),
            ],
        ),
        compiler_params=pltpu.CompilerParams(vmem_limit_bytes=40 << 20),
        cost_estimate=FREE,
        name="attend_back",
    )(offs, prefix, ordered, stats, grad_context, *tables)


def pair_kernel(split, a_ref, b_ref, w_ref, *refs):
    nt = (((1,), (1,)), ((), ()))
    o = lax.dot_general(a_ref[...], w_ref[:, :split], nt, preferred_element_type=F32)
    o += lax.dot_general(b_ref[...], w_ref[:, split:], nt, preferred_element_type=F32)
    for more in refs[:-1]:
        o += more[...].astype(F32)
    refs[-1][...] = o.astype(refs[-1].dtype)


def pair_product(a, b, w, more=()):
    n, depth = w.shape
    m = a.shape[0]
    bn = min(512, n)
    out = pl.BlockSpec((m, bn), lambda j: (0, j))
    return pl.pallas_call(
        functools.partial(pair_kernel, a.shape[1]),
        out_shape=jax.ShapeDtypeStruct((m, n), BF16),
        grid=(n // bn,),
        in_specs=[
            pl.BlockSpec((m, a.shape[1]), lambda j: (0, 0), pipeline_mode=pl.Buffered(1)),
            pl.BlockSpec((m, b.shape[1]), lambda j: (0, 0), pipeline_mode=pl.Buffered(1)),
            pl.BlockSpec((bn, depth), lambda j: (j, 0)),
        ]
        + [out] * len(more),
        out_specs=out,
        compiler_params=pltpu.CompilerParams(vmem_limit_bytes=48 << 20),
        cost_estimate=FREE,
        name="pair_product",
    )(a, b, w, *more)


def pack_kernel(pieces, here_ref, *refs):
    o_ref = refs[-1]
    at = 0
    for n, start, size in pieces:
        o_ref[0, :, at : at + size] = refs[n][:, start : start + size]
        at += size


def pack_columns(weights, pieces, here, places, copies):
    rows = weights[0].shape[0]
    span = sum(size for _, _, size in pieces)
    return pl.pallas_call(
        functools.partial(pack_kernel, pieces),
        out_shape=jax.ShapeDtypeStruct((copies, rows, span), weights[0].dtype),
        grid_spec=pltpu.PrefetchScalarGridSpec(
            num_scalar_prefetch=1,
            grid=(copies,),
            in_specs=[
                pl.BlockSpec((rows, w.shape[1] // places), lambda i, h: (0, h[0])) for w in weights
            ],
            out_specs=pl.BlockSpec((1, rows, span), lambda i, h: (i, 0, 0)),
        ),
        compiler_params=pltpu.CompilerParams(vmem_limit_bytes=40 << 20),
        cost_estimate=FREE,
        name="pack_columns",
    )(here.reshape(1), *in_hbm(weights))


def rows_kernel(counts, *refs):
    o_ref = refs[-1]
    tn = (((0,), (0,)), ((), ()))
    at, col = 0, 0
    for count in counts:
        o = 0.0
        for n in range(count):
            o += lax.dot_general(
                refs[at + n][...], refs[at + count + n][...], tn, preferred_element_type=F32
            )
        o_ref[0, :, col : col + o.shape[1]] = o.astype(o_ref.dtype)
        at, col = at + 2 * count, col + o.shape[1]


def rows_product(products, owners):
    args, specs, columns = [], [], 0
    for a, b in products:
        bm = a[0].shape[1] // owners
        args += [*a, *b]
        specs += [pl.BlockSpec((x.shape[0], bm), lambda i: (0, i)) for x in a]
        specs += [
            pl.BlockSpec(x.shape, lambda i: (0, 0), pipeline_mode=pl.Buffered(1)) for x in b
        ]
        columns += b[0].shape[1]
    return pl.pallas_call(
        functools.partial(rows_kernel, [len(a) for a, _ in products]),
        out_shape=jax.ShapeDtypeStruct((owners, bm, columns), BF16),
        grid=(owners,),
        in_specs=specs,
        out_specs=pl.BlockSpec((1, bm, columns), lambda i: (i, 0, 0)),
        compiler_params=pltpu.CompilerParams(vmem_limit_bytes=56 << 20),
        cost_estimate=FREE,
        name="rows_product",
    )(*args)


def order_kernel(size, pieces, here_ref, *refs):
    blocks, o_ref = refs[:-1], refs[-1]
    m, piece, here = pl.program_id(0), pl.program_id(1), here_ref[0]

    def put(ref):
        o_ref[0] = ref[...]

    for p in range(pieces):
        mine = blocks[p * (2 * size - 1) : (p + 1) * (2 * size - 1)]
        pl.when((piece == p) & (m == 0))(functools.partial(put, mine[0]))
        for k in range(1, size):
            at = (piece == p) & (m == k)
            pl.when(at & (here >= k))(functools.partial(put, mine[k]))
            pl.when(at & (here < k))(functools.partial(put, mine[2 * size - 1 - k]))


def in_order(pieces, here):
    size = len(pieces[0])
    rows, span = pieces[0][0].shape
    flat = []
    for one in pieces:
        flat += [one[0]] + [x[0] for x in one[1:]] + [x[1] for x in one[1:]]
    return pl.pallas_call(
        functools.partial(order_kernel, size, len(pieces)),
        out_shape=jax.ShapeDtypeStruct((size, len(pieces) * rows, span), flat[0].dtype),
        grid_spec=pltpu.PrefetchScalarGridSpec(
            num_scalar_prefetch=1,
            grid=(size, len(pieces)),
            in_specs=[
                pl.BlockSpec((rows, span), lambda m, p, h: (0, 0), pipeline_mode=pl.Buffered(1))
            ]
            * len(flat),
            out_specs=pl.BlockSpec(
                (1, rows, span), lambda m, p, h: (lax.rem(h[0] - m + size, size), p, 0)
            ),
        ),
        compiler_params=pltpu.CompilerParams(vmem_limit_bytes=48 << 20),
        cost_estimate=FREE,
        name="in_order",
    )(here.reshape(1), *in_hbm(flat))


def place_kernel(pairs, a_ref, *outs):
    starts = [[(p * 3 + n) * PAIR for p in range(pairs)] for n in range(3)]
    starts.append([(3 * pairs + p) * PAIR for p in range(pairs)])
    for out, at in zip(outs, starts):
        for p in range(pairs):
            out[:, p * PAIR : (p + 1) * PAIR] = a_ref[0, :, at[p] : at[p] + PAIR].astype(F32)


def place(blocks, pairs):
    n, rows, span = blocks.shape
    width = pairs * PAIR
    return pl.pallas_call(
        functools.partial(place_kernel, pairs),
        out_shape=(jax.ShapeDtypeStruct((rows, n * width), F32),) * 4,
        grid=(n,),
        in_specs=[pl.BlockSpec((1, rows, span), lambda c: (c, 0, 0))],
        out_specs=(pl.BlockSpec((rows, width), lambda c: (0, c)),) * 4,
        compiler_params=pltpu.CompilerParams(vmem_limit_bytes=48 << 20),
        cost_estimate=FREE,
        name="place",
    )(*in_hbm([blocks]))


def widen_kernel(a_ref, o_ref):
    o_ref[...] = a_ref[0].astype(F32)


def widen(blocks):
    n, rows, span = blocks.shape
    return pl.pallas_call(
        widen_kernel,
        out_shape=jax.ShapeDtypeStruct((rows, n * span), F32),
        grid=(n,),
        in_specs=[pl.BlockSpec((1, rows, span), lambda c: (c, 0, 0))],
        out_specs=pl.BlockSpec((rows, span), lambda c: (0, c)),
        compiler_params=pltpu.CompilerParams(vmem_limit_bytes=40 << 20),
        cost_estimate=FREE,
        name="widen",
    )(*in_hbm([blocks]))


def up_kernel(step, h_ref, w_ref, b_ref, act_ref, slope_ref):
    for c in range(0, act_ref.shape[1], step):
        up = jnp.dot(h_ref[...], w_ref[:, c : c + step], preferred_element_type=F32)
        act, slope = gelu_parts(up + b_ref[:, c : c + step])
        act_ref[:, c : c + step] = act.astype(BF16)
        slope_ref[:, c : c + step] = slope.astype(BF16)


def up_product(hidden, weight, bias):
    m, k = hidden.shape
    n = bias.shape[0]
    bm = min(512, m)
    return pl.pallas_call(
        functools.partial(up_kernel, min(256, n)),
        out_shape=(jax.ShapeDtypeStruct((m, n), BF16),) * 2,
        grid=(m // bm,),
        in_specs=[
            pl.BlockSpec((bm, k), lambda i: (i, 0)),
            pl.BlockSpec((k, n), lambda i: (0, 0), pipeline_mode=pl.Buffered(1)),
            pl.BlockSpec((1, n), lambda i: (0, 0)),
        ],
        out_specs=(pl.BlockSpec((bm, n), lambda i: (i, 0)),) * 2,
        compiler_params=pltpu.CompilerParams(vmem_limit_bytes=56 << 20),
        cost_estimate=FREE,
        name="up_product",
    )(hidden, weight, bias.reshape(1, n))


def down_kernel(units, g_ref, w_ref, s_ref, d_ref, c_ref):
    g = g_ref[...]
    d = jnp.dot(g, w_ref[:, :units], preferred_element_type=F32)
    d_ref[...] = (d * s_ref[...].astype(F32)).astype(BF16)
    c_ref[...] = jnp.dot(g, w_ref[:, units:], preferred_element_type=F32).astype(BF16)


def down_product(grad, weight, slope):
    m, k = grad.shape
    units, n = slope.shape[1], weight.shape[1]
    bm = min(512, m)
    return pl.pallas_call(
        functools.partial(down_kernel, units),
        out_shape=(
            jax.ShapeDtypeStruct((m, units), BF16),
            jax.ShapeDtypeStruct((m, n - units), BF16),
        ),
        grid=(m // bm,),
        in_specs=[
            pl.BlockSpec((bm, k), lambda i: (i, 0)),
            pl.BlockSpec((k, n), lambda i: (0, 0), pipeline_mode=pl.Buffered(1)),
            pl.BlockSpec((bm, units), lambda i: (i, 0)),
        ],
        out_specs=(
            pl.BlockSpec((bm, units), lambda i: (i, 0)),
            pl.BlockSpec((bm, n - units), lambda i: (i, 0)),
        ),
        compiler_params=pltpu.CompilerParams(vmem_limit_bytes=56 << 20),
        cost_estimate=FREE,
        name="down_product",
    )(grad, weight, slope)


def line_kernel(pieces, h_ref, *refs):
    b_ref, o_ref = refs[pieces], refs[-1]
    span = o_ref.shape[1] // pieces
    for n in range(pieces):
        to = slice(n * span, (n + 1) * span)
        o = jnp.dot(h_ref[...], refs[n][...], preferred_element_type=F32)
        o_ref[:, to] = o + b_ref[:, to]


def line_product(hidden, weight, bias, start, pieces):
    m, k = hidden.shape
    n = bias.shape[0]
    span = n // pieces
    bm = min(512, m)
    piece = lambda p: pl.BlockSpec(
        (k, span), lambda i: (0, start // span + p), pipeline_mode=pl.Buffered(1)
    )
    return pl.pallas_call(
        functools.partial(line_kernel, pieces),
        out_shape=jax.ShapeDtypeStruct((m, n), F32),
        grid=(m // bm,),
        in_specs=[pl.BlockSpec((bm, k), lambda i: (i, 0))]
        + [piece(p) for p in range(pieces)]
        + [pl.BlockSpec((1, n), lambda i: (0, 0))],
        out_specs=pl.BlockSpec((bm, n), lambda i: (i, 0)),
        compiler_params=pltpu.CompilerParams(vmem_limit_bytes=56 << 20),
        cost_estimate=FREE,
        name="line_product",
    )(hidden, *[weight] * pieces, bias.reshape(1, n))


def gelu_parts(up):
    square = up * up
    t = jnp.tanh(GELU_C * up * (1.0 + GELU_A * square))
    half = 0.5 * (1.0 + t)
    slope = half + 0.5 * up * (1.0 - t * t) * (GELU_C * (1.0 + 3.0 * GELU_A * square))
    return up * half, slope


def local(
    tokens, cotangent, prefix_len, group_order, ln_gain, ln_bias,
    query_weight, query_bias, key_weight, key_bias, value_weight, value_bias,
    out_weight, out_bias, up_weight, up_bias, down_weight, down_bias,
):
    nf, nc, nt = lax.axis_size("fsdp"), lax.axis_size("ctx"), lax.axis_size("tp")
    ci, ti = lax.axis_index("ctx").astype(jnp.int32), lax.axis_index("tp").astype(jnp.int32)
    seqs, rows, width = tokens.shape
    own_seqs = seqs // nt
    length = rows * nc
    own = own_seqs * rows
    db = width // nf
    inner = query_weight.shape[1] // nc
    units = up_weight.shape[1] // nc
    pairs = inner // PAIR

    def columns(w):
        return lax.dynamic_slice_in_dim(w, ci * (w.shape[-1] // nc), w.shape[-1] // nc, axis=-1)

    def by_pairs(arrays):
        return jnp.concatenate(
            [a[..., p * PAIR : (p + 1) * PAIR] for p in range(pairs) for a in arrays], axis=-1
        )

    x = lax.dynamic_slice_in_dim(tokens, ti * own_seqs, own_seqs, axis=0).reshape(own, width)
    g_own = lax.dynamic_slice_in_dim(cotangent, ti * own_seqs, own_seqs, axis=0).reshape(own, width)
    x = x.astype(F32)
    gain, shift = ln_gain.astype(F32), ln_bias.astype(F32)
    centred = x - jnp.mean(x, axis=-1, keepdims=True)
    inv_std = lax.rsqrt(jnp.mean(centred * centred, axis=-1, keepdims=True) + EPS)
    normed = centred * inv_std
    h_own = (normed * gain + shift).astype(BF16)

    def side(blocks):
        return blocks[-1] if len(blocks) > 1 else (blocks[0], blocks[0])

    def gather_on(blocks):
        return blocks + [gather_step(side(blocks), len(blocks), nc)]

    cut = [
        (1 + n, p * PAIR, PAIR) for p in range(pairs) for n in range(3)
    ]
    col_sum = lambda a: jnp.sum(a.astype(F32), axis=0)
    h_own, g_cols = meet((h_own, col_sum(g_own)))
    h_in = [[piece] for piece in jnp.split(h_own, 2)]
    g_cols = total([g_cols] + [xor_swap(g_cols, "tp", nt, k) for k in range(1, nt)])
    g_cols, early = meet(
        (g_cols, (up_weight, query_weight, key_weight, value_weight, down_weight, out_weight))
    )
    first = pack_columns(early[:4], [(0, 0, units)] + cut, ci, nc, nf)
    second = pack_columns(early[4:], [(0, 0, units), (1, 0, inner)], ci, nc, nf)
    b_qkv = by_pairs([columns(query_bias), columns(key_bias), columns(value_bias)]).astype(F32)
    b_up = columns(up_bias).astype(F32)

    lane = jnp.arange(PAIR, dtype=jnp.int32)[None, :] % HD
    freq = jnp.power(10000.0, -2.0 * (lane % HALF).astype(F32) / ROT)
    angle = jnp.arange(length, dtype=jnp.int32).astype(F32)[:, None] * freq
    cos = jnp.where(lane < ROT, jnp.cos(angle), 1.0)
    sin = jnp.sin(angle)
    sa = jnp.where(lane < HALF, -sin, 0.0)
    sb = jnp.where((lane >= HALF) & (lane < ROT), sin, 0.0)
    groups = group_order.shape[0]
    glen = length // groups
    places = jnp.arange(groups, dtype=jnp.int32)
    slot = jnp.sum(
        jnp.where(group_order[None, :] == places[:, None], places[None, :], 0), axis=1
    ) * glen
    offs = slot
    seq_ids = jnp.arange(seqs, dtype=jnp.int32)
    seq_of = ((seq_ids // own_seqs) ^ ti) * own_seqs + seq_ids % own_seqs
    prefix = jnp.sum(
        jnp.where(seq_of[:, None] == seq_ids[None, :], prefix_len[None, :], 0), axis=1
    )
    offs, prefix = offs.astype(jnp.int32), prefix.astype(jnp.int32)

    tables = (cos, sa, sb)
    first_all = lax.all_to_all(first, "fsdp", 0, 0, tiled=True)
    h_in = [gather_on(h) for h in h_in]
    h_in[0], second, tables, b_up, b_qkv, offs, prefix = meet(
        (h_in[0], second, tables, b_up, b_qkv, offs, prefix)
    )
    while len(h_in[0]) < nc:
        h_in = [gather_on(h) for h in h_in]
    g_own, h_in = meet((g_own, h_in))
    g_all = lax.all_gather(g_own.reshape(own_seqs, rows, width), "ctx", axis=1, tiled=True)

    def halves(mine):
        mine = mine.reshape(own_seqs * length, width)
        return [mine] + [xor_swap(mine, "tp", nt, k) for k in range(1, nt)]

    def send_rows(full):
        return lax.all_to_all(full, "fsdp", 0, 0, tiled=True)

    def sum_rows(got):
        return total([got[k] for k in range(nf)]).astype(BF16)

    def gather_cols(mine):
        return lax.all_gather(mine, "ctx", axis=0, tiled=False)

    h_mine = jnp.moveaxis(in_order(h_in, ci).reshape(nc, own_seqs, rows, width), 1, 0)
    hidden = halves(h_mine)
    hidden, first_all = meet((hidden, first_all))
    w_first = first_all.reshape(width, units + 3 * inner)
    second_all = lax.all_to_all(second, "fsdp", 0, 0, tiled=True)
    ups, qkv = [], []
    for n in range(nt):
        ups.append(up_product(hidden[n], w_first, b_up))
        ups, hidden = meet((ups, hidden))
    for n in range(nt):
        qkv.append(line_product(hidden[n], w_first, b_qkv, units, 3))
        qkv, hidden = meet((qkv, hidden))
    act, slope = [u[0] for u in ups], [u[1] for u in ups]

    def attend_half(n, qkv):
        out = []
        for i in range(own_seqs):
            at = slice(i * length, (i + 1) * length)
            m = n * own_seqs + i
            out.append(attend(qkv[at], offs, prefix[m : m + 1], tables))
        return out

    def back_half(n, kept, grad_context):
        out = []
        for i in range(own_seqs):
            at = slice(i * length, (i + 1) * length)
            m = n * own_seqs + i
            out.append(
                attend_back(
                    kept[i][1], kept[i][2], grad_context[at], offs, prefix[m : m + 1], tables
                )
            )
        return jnp.concatenate(out)

    def parts_of(mine, got):
        grid = lambda a: a.reshape(own_seqs, nc, rows, width)
        mine, got = grid(mine), [grid(g) for g in got]

        def parts(m):
            at = (ci - m + nc) % nc
            pick = lambda a: lax.dynamic_index_in_dim(a, at, 1, keepdims=False).reshape(own, width)
            return [pick(mine)] + [pick(g) for g in got]

        return parts

    others = range(1, nt)
    kept = [None] * nt
    for n in others:
        kept[n] = attend_half(n, qkv[n])
    kept[1:], qkv, act, second_all = meet((kept[1:], qkv, act, second_all))
    w_second = second_all.reshape(width, units + inner)
    context = [None] + [jnp.concatenate([c[0] for c in kept[n]]) for n in others]
    theirs, qkv = meet(([pair_product(act[n], context[n], w_second) for n in others], qkv))
    o_got = [xor_swap(t, "tp", nt, n) for n, t in zip(others, theirs)]
    kept[0], act, o_got, g_all = meet((attend_half(0, qkv[0]), act, o_got, g_all))
    grad = halves(g_all)
    context[0] = jnp.concatenate([c[0] for c in kept[0]])
    both = pair_product(act[0], context[0], w_second, o_got)
    both = jnp.moveaxis(both.reshape(own_seqs, nc, rows, width), 1, 0).reshape(nc, own, width)
    grad, act, both = meet((grad, act, both))
    o_sum = lax.psum_scatter(both, "ctx", scatter_dimension=0, tiled=True)

    full_down = rows_product([(grad, act)], nf)
    grad, full_down, slope = meet((grad, full_down, slope))
    d_rows = send_rows(full_down)
    downs = []
    for n in range(nt):
        downs.append(down_product(grad[n], w_second, slope[n]))
        downs, grad, hidden = meet((downs, grad, hidden))
    dup, grad_context = [d[0] for d in downs], [d[1] for d in downs]
    full_up = rows_product([(hidden, dup)], nf)
    full_up, kept, grad_context = meet((full_up, kept, grad_context))
    dqkv = [None] + [back_half(n, kept[n], grad_context[n]) for n in others]
    dqkv[1:], d_rows, dup = meet((dqkv[1:], d_rows, dup))
    d_sum, dup = meet((sum_rows(d_rows), dup))
    d_cols = gather_cols(d_sum)
    u_rows = send_rows(full_up)

    theirs, kept, grad_context = meet(
        ([pair_product(dup[n], dqkv[n], w_first) for n in others], kept, grad_context)
    )
    h_got = [xor_swap(t, "tp", nt, n) for n, t in zip(others, theirs)]
    dqkv[0], o_sum, h_got = meet((back_half(0, kept[0], grad_context[0]), o_sum, h_got))
    h_both, dqkv, hidden = meet(
        (pair_product(dup[0], dqkv[0], w_first, h_got), dqkv, hidden)
    )
    qo_full = rows_product([(hidden, dqkv), (grad, context)], nf)
    qo_full, u_rows = meet((qo_full, u_rows))
    u_sum, d_cols = meet((sum_rows(u_rows), d_cols))
    qo = send_rows(qo_full)
    u_cols = gather_cols(u_sum)
    h_parts = parts_of(h_both, [])
    dw_down = widen(d_cols)
    h_sum, qo, dw_down = meet((sum_step(None, h_parts, 1, nc), qo, dw_down))
    qo_sum = sum_rows(qo)
    for k in range(2, nc):
        h_sum = sum_step(h_sum, h_parts, k, nc)
        if k == 2:
            h_sum, qo_sum = meet((h_sum, qo_sum))
        h_sum = meet(h_sum)
    grad_hidden = total(h_parts(0) + list(h_sum))
    u_cols, h_sum = meet((u_cols, h_sum))
    dw_up = widen(u_cols)
    grad_hidden, dw_up = meet((grad_hidden, dw_up))
    qo_cols = gather_cols(qo_sum)
    col_sum = lambda a: jnp.sum(a.astype(F32), axis=0)
    out_own = total([x, o_sum.reshape(own, width), out_bias, down_bias])

    gs = grad_hidden * gain
    grad_normed = inv_std * (
        gs - jnp.mean(gs, axis=-1, keepdims=True)
        - normed * jnp.mean(gs * normed, axis=-1, keepdims=True)
    )
    in_own = g_own.astype(F32) + grad_normed
    norm_sums = jnp.concatenate([col_sum(grad_hidden * normed), col_sum(grad_hidden)])

    def whole_tokens(own_rows):
        mine = own_rows.astype(BF16).reshape(1, own_seqs, rows, width)
        pieces = [mine] + [xor_swap(mine, "tp", nt, k) for k in range(1, nt)]
        full = jnp.zeros((nt, own_seqs, rows, width), BF16)
        for k in range(nt):
            full = lax.dynamic_update_slice_in_dim(full, pieces[k], ti ^ k, axis=0)
        return full.reshape(seqs, rows, width)

    output = whole_tokens(out_own)
    input_grad = whole_tokens(in_own)

    dw_qkv = place(qo_cols, pairs)

    bias_sums = jnp.concatenate(
        [total([col_sum(a) for a in array]) for array in (dqkv, dup)]
    )[None]
    bias_sums = jnp.sum(to_all(bias_sums, "fsdp", nf).reshape(nf, -1), axis=0)
    small = 3 * inner + units
    got = to_all(jnp.concatenate([bias_sums, norm_sums, g_cols])[None], "ctx", nc).reshape(nc, -1)
    qkv_sums = got[:, : 3 * inner].reshape(nc, pairs, 3, PAIR)
    qb, kb, vb = (qkv_sums[:, :, n].reshape(nc * inner) for n in range(3))
    ub = got[:, 3 * inner : small].reshape(nc * units)
    sums = jnp.sum(got[:, small:], axis=0)[None]
    sums = jnp.sum(to_all(sums, "fsdp", nf).reshape(nf, -1), axis=0)
    norm_sums, obias = sums[: 2 * width], sums[2 * width :]
    norm_sums = total([norm_sums] + [xor_swap(norm_sums, "tp", nt, k) for k in range(1, nt)])
    norm_sums = norm_sums.reshape(2, width)

    return (
        output, input_grad, norm_sums[0], norm_sums[1],
        dw_qkv[0], qb, dw_qkv[1], kb, dw_qkv[2], vb,
        dw_qkv[3], dw_up, ub, dw_down, obias,
    )


def solution(mesh):
    rows, flat, cols, one = P("fsdp", "ctx", None), P("fsdp", "tp"), P("tp"), P()
    return jax.shard_map(
        local,
        mesh=mesh,
        in_specs=(
            rows, rows, P("fsdp"), one, one, one,
            flat, cols, flat, cols, flat, cols, flat, one, flat, cols, flat, one,
        ),
        out_specs=(
            rows, rows, one, one, flat, cols, flat, cols, flat, cols, flat, flat, cols, flat, one,
        ),
        check_vma=False,
    )
```

```python
import functools

import jax
import jax.numpy as jnp
from jax import lax
from jax.experimental import pallas as pl
from jax.experimental.pallas import tpu as pltpu
from jax.sharding import PartitionSpec as P

HD = 64
ROT = 32
HALF = ROT // 2
PAIR = 2 * HD
NEG = -1e30
EPS = 1e-05
LOG2E = 1.4426950408889634
GELU_C = 0.7978845608028654
GELU_A = 0.044715
F32 = jnp.float32
BF16 = jnp.bfloat16


def meet(tree):
    return lax.optimization_barrier(tree)


def total(addends):
    out = addends[0].astype(F32)
    for one in addends[1:]:
        out = out + one.astype(F32)
    return out


def xor_swap(value, axis, size, step):
    return lax.ppermute(value, axis, [(j, j ^ step) for j in range(size)])


def to_all(value, axis, size):
    return lax.all_to_all(jnp.broadcast_to(value[None], (size,) + value.shape), axis, 0, 0, tiled=True)


def gather_step(sides, step, size, axis="ctx"):
    left, right = sides
    return (
        lax.ppermute(left, axis, [(j, j + 1) for j in range(step - 1, size - 1)]),
        lax.ppermute(right, axis, [(j, j - 1) for j in range(1, size - step + 1)]),
    )


def sum_step(sides, parts, step, size, axis="ctx"):
    a, b = parts(step), parts(size - step)
    if sides is not None:
        a, b = a + [sides[0]], b + [sides[1]]
    return (
        lax.ppermute(
            total(a).astype(BF16), axis, [(j, j + 1) for j in range(min(step, size - 1))]
        ),
        lax.ppermute(
            total(b).astype(BF16), axis, [(j, j - 1) for j in range(max(size - step, 1), size)]
        ),
    )


def by_distance(blocks, here):
    n = len(blocks)
    return [blocks[0]] + [
        jnp.where(here >= m, blocks[m][0], blocks[n - m][1]) for m in range(1, n)
    ]


def in_hbm(arrays):
    return [pltpu.with_memory_space_constraint(a, pltpu.HBM) for a in arrays]


FREE = pl.CostEstimate(flops=1, transcendentals=0, bytes_accessed=1)


def rotate(x, cos, sa, sb):
    return (
        x * cos + pltpu.roll(x, PAIR - HALF, axis=1) * sa + pltpu.roll(x, HALF, axis=1) * sb
    )


def masked_scores(k_s, qt, prefix, first, reach, clear):
    s = jnp.dot(k_s[0:reach, :], qt, preferred_element_type=F32) * LOG2E
    count = qt.shape[1]
    kpos = clear + lax.broadcasted_iota(jnp.int32, (reach - clear, count), 0)
    qpos = first + lax.broadcasted_iota(jnp.int32, (1, count), 1)
    tail = jnp.where(kpos < jnp.maximum(qpos + 1, prefix), s[clear:reach], NEG)
    return jnp.concatenate([s[:clear], tail], axis=0) if clear else tail


def spans(length, qblock, most):
    for first in range(0, length, qblock):
        yield first, max(first + qblock, most), first if first >= most else 0


def keep_head(x, h):
    lane = lax.broadcasted_iota(jnp.int32, x.shape, 1)
    return jnp.where((lane >= h * HD) & (lane < (h + 1) * HD), x, 0.0)


def attend_kernel(
    glen, qblock, most,
    offs_ref, prefix_ref,
    qkv_ref, cos_ref, sa_ref, sb_ref,
    ctx_ref, sorted_ref, stat_ref,
    qtm, k_s, vt_s, ot,
):
    length = cos_ref.shape[0]
    for p in range(length // glen):
        rows = pl.ds(pl.multiple_of(offs_ref[p], glen), glen)
        to = slice(p * glen, (p + 1) * glen)
        cos, sa, sb = cos_ref[to, :], sa_ref[to, :], sb_ref[to, :]
        q = rotate(qkv_ref[rows, 0:PAIR], cos, sa, sb).astype(BF16).astype(F32) * (HD**-0.5)
        sorted_ref[to, 0:PAIR] = q.astype(BF16)
        k = rotate(qkv_ref[rows, PAIR : 2 * PAIR], cos, sa, sb).astype(BF16)
        k_s[to, :] = k
        sorted_ref[to, PAIR : 2 * PAIR] = k
        sorted_ref[to, 2 * PAIR : 3 * PAIR] = qkv_ref[rows, 2 * PAIR : 3 * PAIR].astype(BF16)
    q = sorted_ref[:, 0:PAIR].astype(F32)
    for h in range(2):
        qtm[h] = keep_head(q, h).astype(BF16).T
    vt_s[...] = sorted_ref[:, 2 * PAIR : 3 * PAIR].T.reshape(2, HD, length)
    prefix = prefix_ref[0]
    for first, reach, clear in spans(length, qblock, most):
        cols = slice(first, first + qblock)

        def head(h, _):
            s = masked_scores(k_s, qtm[h, :, cols], prefix, first, reach, clear)
            top = jnp.max(s, axis=0, keepdims=True)
            e = jnp.exp2(s - top)
            scale = 1.0 / jnp.sum(e, axis=0, keepdims=True)
            stat_ref[0, h, 0:1, cols] = top
            stat_ref[0, h, 1:2, cols] = scale
            low = (e * scale).astype(BF16)
            ot[h, :, cols] = jnp.dot(vt_s[h, :, 0:reach], low, preferred_element_type=F32)
            return 0

        lax.fori_loop(0, 2, head, 0, unroll=True)
    for p in range(length // glen):
        rows = pl.ds(pl.multiple_of(offs_ref[p], glen), glen)
        to = slice(p * glen, (p + 1) * glen)
        ctx_ref[rows, :] = ot[:, :, to].reshape(PAIR, glen).T.astype(BF16)


def attend_back_kernel(
    glen, qblock, most,
    offs_ref, prefix_ref,
    sorted_ref, stat_ref, do_ref, cos_ref, sa_ref, sb_ref,
    dqkv_ref,
    qm, qtm, k_s, kt_s, v_s, dom, dotm, dqt, dk_acc, dv_acc,
):
    length = cos_ref.shape[0]
    k_s[...] = sorted_ref[:, PAIR : 2 * PAIR]
    v_s[...] = sorted_ref[:, 2 * PAIR : 3 * PAIR]
    q = sorted_ref[:, 0:PAIR].astype(F32)
    for p in range(length // glen):
        rows = pl.ds(pl.multiple_of(offs_ref[p], glen), glen)
        to = slice(p * glen, (p + 1) * glen)
        do = do_ref[rows, :].astype(F32)
        for h in range(2):
            dom[h, to, :] = keep_head(do, h).astype(BF16)
    for h in range(2):
        qm[h] = keep_head(q, h).astype(BF16)
        qtm[h] = qm[h].T
        dotm[h] = dom[h].T
    kt_s[...] = k_s[...].T.reshape(2, HD, length)
    dk_acc[...] = jnp.zeros_like(dk_acc)
    dv_acc[...] = jnp.zeros_like(dv_acc)
    prefix = prefix_ref[0]
    dot = functools.partial(jnp.dot, preferred_element_type=F32)
    for first, reach, clear in spans(length, qblock, most):
        cols = slice(first, first + qblock)

        def head(h, _):
            s = masked_scores(k_s, qtm[h, :, cols], prefix, first, reach, clear)
            prob = jnp.exp2(s - stat_ref[0, h, 0:1, cols]) * stat_ref[0, h, 1:2, cols]
            dv_acc[0:reach, :] += dot(prob.astype(BF16), dom[h, cols, :])
            dp = dot(v_s[0:reach, :], dotm[h, :, cols])
            delta = jnp.sum(prob * dp, axis=0, keepdims=True)
            ds = (prob * (dp - delta)).astype(BF16)
            dqt[h, :, cols] = dot(kt_s[h, :, 0:reach], ds)
            dk_acc[0:reach, :] += dot(ds, qm[h, cols, :])
            return 0

        lax.fori_loop(0, 2, head, 0, unroll=True)
    for p in range(length // glen):
        rows = pl.ds(pl.multiple_of(offs_ref[p], glen), glen)
        to = slice(p * glen, (p + 1) * glen)
        cos, sa, sb = cos_ref[to, :], -sa_ref[to, :], -sb_ref[to, :]
        dq = dqt[:, :, to].reshape(PAIR, glen).T * (HD**-0.5)
        dqkv_ref[rows, 0:PAIR] = rotate(dq, cos, sa, sb).astype(BF16)
        dqkv_ref[rows, PAIR : 2 * PAIR] = rotate(dk_acc[to, :], cos, sa, sb).astype(BF16)
        dqkv_ref[rows, 2 * PAIR : 3 * PAIR] = dv_acc[to, :].astype(BF16)


def attention_specs(length):
    whole = pl.BlockSpec((length, PAIR), lambda p, *_: (0, 0))
    wide = pl.BlockSpec((length, 3 * PAIR), lambda p, *_: (0, p))
    narrow = pl.BlockSpec((length, PAIR), lambda p, *_: (0, p))
    stat = pl.BlockSpec((1, 2, 2, length), lambda p, *_: (p, 0, 0, 0))
    return whole, wide, narrow, stat


def attend(qkv, offs, prefix, tables):
    length, inner = qkv.shape[0], qkv.shape[1] // 3
    whole, wide, narrow, stat = attention_specs(length)
    vm = pltpu.VMEM
    return pl.pallas_call(
        functools.partial(attend_kernel, length // offs.shape[0], min(256, length), length // 2),
        out_shape=(
            jax.ShapeDtypeStruct((length, inner), BF16),
            jax.ShapeDtypeStruct((length, 3 * inner), BF16),
            jax.ShapeDtypeStruct((inner // PAIR, 2, 2, length), F32),
        ),
        grid_spec=pltpu.PrefetchScalarGridSpec(
            num_scalar_prefetch=2,
            grid=(inner // PAIR,),
            in_specs=[wide, whole, whole, whole],
            out_specs=(narrow, wide, stat),
            scratch_shapes=[
                vm((2, PAIR, length), BF16),
                vm((length, PAIR), BF16),
                vm((2, HD, length), BF16),
                vm((2, HD, length), F32),
            ],
        ),
        compiler_params=pltpu.CompilerParams(vmem_limit_bytes=40 << 20),
        cost_estimate=FREE,
        name="attend",
    )(offs, prefix, qkv, *tables)


def attend_back(ordered, stats, grad_context, offs, prefix, tables):
    length, inner = grad_context.shape
    whole, wide, narrow, stat = attention_specs(length)
    vm = pltpu.VMEM
    return pl.pallas_call(
        functools.partial(
            attend_back_kernel, length // offs.shape[0], min(256, length), length // 2
        ),
        out_shape=jax.ShapeDtypeStruct((length, 3 * inner), BF16),
        grid_spec=pltpu.PrefetchScalarGridSpec(
            num_scalar_prefetch=2,
            grid=(inner // PAIR,),
            in_specs=[wide, stat, narrow, whole, whole, whole],
            out_specs=wide,
            scratch_shapes=[
                vm((2, length, PAIR), BF16),
                vm((2, PAIR, length), BF16),
                vm((length, PAIR), BF16),
                vm((2, HD, length), BF16),
                vm((length, PAIR), BF16),
                vm((2, length, PAIR), BF16),
                vm((2, PAIR, length), BF16),
                vm((2, HD, length), F32),
                vm((length, PAIR), F32),
                vm((length, PAIR), F32),
            ],
        ),
        compiler_params=pltpu.CompilerParams(vmem_limit_bytes=40 << 20),
        cost_estimate=FREE,
        name="attend_back",
    )(offs, prefix, ordered, stats, grad_context, *tables)


def pair_kernel(split, a_ref, b_ref, w_ref, *refs):
    nt = (((1,), (1,)), ((), ()))
    o = lax.dot_general(a_ref[...], w_ref[:, :split], nt, preferred_element_type=F32)
    o += lax.dot_general(b_ref[...], w_ref[:, split:], nt, preferred_element_type=F32)
    for more in refs[:-1]:
        o += more[...].astype(F32)
    refs[-1][...] = o.astype(refs[-1].dtype)


def pair_product(a, b, w, more=()):
    n, depth = w.shape
    m = a.shape[0]
    bn = min(512, n)
    out = pl.BlockSpec((m, bn), lambda j: (0, j))
    return pl.pallas_call(
        functools.partial(pair_kernel, a.shape[1]),
        out_shape=jax.ShapeDtypeStruct((m, n), BF16),
        grid=(n // bn,),
        in_specs=[
            pl.BlockSpec((m, a.shape[1]), lambda j: (0, 0), pipeline_mode=pl.Buffered(1)),
            pl.BlockSpec((m, b.shape[1]), lambda j: (0, 0), pipeline_mode=pl.Buffered(1)),
            pl.BlockSpec((bn, depth), lambda j: (j, 0)),
        ]
        + [out] * len(more),
        out_specs=out,
        compiler_params=pltpu.CompilerParams(vmem_limit_bytes=48 << 20),
        cost_estimate=FREE,
        name="pair_product",
    )(a, b, w, *more)


def pack_kernel(pieces, here_ref, *refs):
    o_ref = refs[-1]
    at = 0
    for n, start, size in pieces:
        o_ref[0, :, at : at + size] = refs[n][:, start : start + size]
        at += size


def pack_columns(weights, pieces, here, places, copies):
    rows = weights[0].shape[0]
    span = sum(size for _, _, size in pieces)
    return pl.pallas_call(
        functools.partial(pack_kernel, pieces),
        out_shape=jax.ShapeDtypeStruct((copies, rows, span), weights[0].dtype),
        grid_spec=pltpu.PrefetchScalarGridSpec(
            num_scalar_prefetch=1,
            grid=(copies,),
            in_specs=[
                pl.BlockSpec((rows, w.shape[1] // places), lambda i, h: (0, h[0])) for w in weights
            ],
            out_specs=pl.BlockSpec((1, rows, span), lambda i, h: (i, 0, 0)),
        ),
        compiler_params=pltpu.CompilerParams(vmem_limit_bytes=40 << 20),
        cost_estimate=FREE,
        name="pack_columns",
    )(here.reshape(1), *in_hbm(weights))


def rows_kernel(counts, *refs):
    o_ref = refs[-1]
    tn = (((0,), (0,)), ((), ()))
    at, col = 0, 0
    for count in counts:
        o = 0.0
        for n in range(count):
            o += lax.dot_general(
                refs[at + n][...], refs[at + count + n][...], tn, preferred_element_type=F32
            )
        o_ref[0, :, col : col + o.shape[1]] = o.astype(o_ref.dtype)
        at, col = at + 2 * count, col + o.shape[1]


def rows_product(products, owners):
    args, specs, columns = [], [], 0
    for a, b in products:
        bm = a[0].shape[1] // owners
        args += [*a, *b]
        specs += [pl.BlockSpec((x.shape[0], bm), lambda i: (0, i)) for x in a]
        specs += [
            pl.BlockSpec(x.shape, lambda i: (0, 0), pipeline_mode=pl.Buffered(1)) for x in b
        ]
        columns += b[0].shape[1]
    return pl.pallas_call(
        functools.partial(rows_kernel, [len(a) for a, _ in products]),
        out_shape=jax.ShapeDtypeStruct((owners, bm, columns), BF16),
        grid=(owners,),
        in_specs=specs,
        out_specs=pl.BlockSpec((1, bm, columns), lambda i: (i, 0, 0)),
        compiler_params=pltpu.CompilerParams(vmem_limit_bytes=56 << 20),
        cost_estimate=FREE,
        name="rows_product",
    )(*args)


def order_kernel(size, pieces, here_ref, *refs):
    blocks, o_ref = refs[:-1], refs[-1]
    m, piece, here = pl.program_id(0), pl.program_id(1), here_ref[0]

    def put(ref):
        o_ref[0] = ref[...]

    for p in range(pieces):
        mine = blocks[p * (2 * size - 1) : (p + 1) * (2 * size - 1)]
        pl.when((piece == p) & (m == 0))(functools.partial(put, mine[0]))
        for k in range(1, size):
            at = (piece == p) & (m == k)
            pl.when(at & (here >= k))(functools.partial(put, mine[k]))
            pl.when(at & (here < k))(functools.partial(put, mine[2 * size - 1 - k]))


def in_order(pieces, here):
    size = len(pieces[0])
    rows, span = pieces[0][0].shape
    flat = []
    for one in pieces:
        flat += [one[0]] + [x[0] for x in one[1:]] + [x[1] for x in one[1:]]
    return pl.pallas_call(
        functools.partial(order_kernel, size, len(pieces)),
        out_shape=jax.ShapeDtypeStruct((size, len(pieces) * rows, span), flat[0].dtype),
        grid_spec=pltpu.PrefetchScalarGridSpec(
            num_scalar_prefetch=1,
            grid=(size, len(pieces)),
            in_specs=[
                pl.BlockSpec((rows, span), lambda m, p, h: (0, 0), pipeline_mode=pl.Buffered(1))
            ]
            * len(flat),
            out_specs=pl.BlockSpec(
                (1, rows, span), lambda m, p, h: (lax.rem(h[0] - m + size, size), p, 0)
            ),
        ),
        compiler_params=pltpu.CompilerParams(vmem_limit_bytes=48 << 20),
        cost_estimate=FREE,
        name="in_order",
    )(here.reshape(1), *in_hbm(flat))


def place_kernel(pairs, a_ref, *outs):
    starts = [[(p * 3 + n) * PAIR for p in range(pairs)] for n in range(3)]
    starts.append([(3 * pairs + p) * PAIR for p in range(pairs)])
    for out, at in zip(outs, starts):
        for p in range(pairs):
            out[:, p * PAIR : (p + 1) * PAIR] = a_ref[0, :, at[p] : at[p] + PAIR].astype(F32)


def place(blocks, pairs):
    n, rows, span = blocks.shape
    width = pairs * PAIR
    return pl.pallas_call(
        functools.partial(place_kernel, pairs),
        out_shape=(jax.ShapeDtypeStruct((rows, n * width), F32),) * 4,
        grid=(n,),
        in_specs=[pl.BlockSpec((1, rows, span), lambda c: (c, 0, 0))],
        out_specs=(pl.BlockSpec((rows, width), lambda c: (0, c)),) * 4,
        compiler_params=pltpu.CompilerParams(vmem_limit_bytes=48 << 20),
        cost_estimate=FREE,
        name="place",
    )(*in_hbm([blocks]))


def widen_kernel(a_ref, o_ref):
    o_ref[...] = a_ref[0].astype(F32)


def widen(blocks):
    n, rows, span = blocks.shape
    return pl.pallas_call(
        widen_kernel,
        out_shape=jax.ShapeDtypeStruct((rows, n * span), F32),
        grid=(n,),
        in_specs=[pl.BlockSpec((1, rows, span), lambda c: (c, 0, 0))],
        out_specs=pl.BlockSpec((rows, span), lambda c: (0, c)),
        compiler_params=pltpu.CompilerParams(vmem_limit_bytes=40 << 20),
        cost_estimate=FREE,
        name="widen",
    )(*in_hbm([blocks]))


def up_kernel(step, h_ref, w_ref, b_ref, act_ref, slope_ref):
    for c in range(0, act_ref.shape[1], step):
        up = jnp.dot(h_ref[...], w_ref[:, c : c + step], preferred_element_type=F32)
        act, slope = gelu_parts(up + b_ref[:, c : c + step])
        act_ref[:, c : c + step] = act.astype(BF16)
        slope_ref[:, c : c + step] = slope.astype(BF16)


def up_product(hidden, weight, bias):
    m, k = hidden.shape
    n = bias.shape[0]
    bm = min(512, m)
    return pl.pallas_call(
        functools.partial(up_kernel, min(256, n)),
        out_shape=(jax.ShapeDtypeStruct((m, n), BF16),) * 2,
        grid=(m // bm,),
        in_specs=[
            pl.BlockSpec((bm, k), lambda i: (i, 0)),
            pl.BlockSpec((k, n), lambda i: (0, 0), pipeline_mode=pl.Buffered(1)),
            pl.BlockSpec((1, n), lambda i: (0, 0)),
        ],
        out_specs=(pl.BlockSpec((bm, n), lambda i: (i, 0)),) * 2,
        compiler_params=pltpu.CompilerParams(vmem_limit_bytes=56 << 20),
        cost_estimate=FREE,
        name="up_product",
    )(hidden, weight, bias.reshape(1, n))


def down_kernel(units, g_ref, w_ref, s_ref, d_ref, c_ref):
    g = g_ref[...]
    d = jnp.dot(g, w_ref[:, :units], preferred_element_type=F32)
    d_ref[...] = (d * s_ref[...].astype(F32)).astype(BF16)
    c_ref[...] = jnp.dot(g, w_ref[:, units:], preferred_element_type=F32).astype(BF16)


def down_product(grad, weight, slope):
    m, k = grad.shape
    units, n = slope.shape[1], weight.shape[1]
    bm = min(512, m)
    return pl.pallas_call(
        functools.partial(down_kernel, units),
        out_shape=(
            jax.ShapeDtypeStruct((m, units), BF16),
            jax.ShapeDtypeStruct((m, n - units), BF16),
        ),
        grid=(m // bm,),
        in_specs=[
            pl.BlockSpec((bm, k), lambda i: (i, 0)),
            pl.BlockSpec((k, n), lambda i: (0, 0), pipeline_mode=pl.Buffered(1)),
            pl.BlockSpec((bm, units), lambda i: (i, 0)),
        ],
        out_specs=(
            pl.BlockSpec((bm, units), lambda i: (i, 0)),
            pl.BlockSpec((bm, n - units), lambda i: (i, 0)),
        ),
        compiler_params=pltpu.CompilerParams(vmem_limit_bytes=56 << 20),
        cost_estimate=FREE,
        name="down_product",
    )(grad, weight, slope)


def line_kernel(pieces, h_ref, *refs):
    b_ref, o_ref = refs[pieces], refs[-1]
    span = o_ref.shape[1] // pieces
    for n in range(pieces):
        to = slice(n * span, (n + 1) * span)
        o = jnp.dot(h_ref[...], refs[n][...], preferred_element_type=F32)
        o_ref[:, to] = o + b_ref[:, to]


def line_product(hidden, weight, bias, start, pieces):
    m, k = hidden.shape
    n = bias.shape[0]
    span = n // pieces
    bm = min(512, m)
    piece = lambda p: pl.BlockSpec(
        (k, span), lambda i: (0, start // span + p), pipeline_mode=pl.Buffered(1)
    )
    return pl.pallas_call(
        functools.partial(line_kernel, pieces),
        out_shape=jax.ShapeDtypeStruct((m, n), F32),
        grid=(m // bm,),
        in_specs=[pl.BlockSpec((bm, k), lambda i: (i, 0))]
        + [piece(p) for p in range(pieces)]
        + [pl.BlockSpec((1, n), lambda i: (0, 0))],
        out_specs=pl.BlockSpec((bm, n), lambda i: (i, 0)),
        compiler_params=pltpu.CompilerParams(vmem_limit_bytes=56 << 20),
        cost_estimate=FREE,
        name="line_product",
    )(hidden, *[weight] * pieces, bias.reshape(1, n))


def gelu_parts(up):
    square = up * up
    t = jnp.tanh(GELU_C * up * (1.0 + GELU_A * square))
    half = 0.5 * (1.0 + t)
    slope = half + 0.5 * up * (1.0 - t * t) * (GELU_C * (1.0 + 3.0 * GELU_A * square))
    return up * half, slope


def local(
    tokens, cotangent, prefix_len, group_order, ln_gain, ln_bias,
    query_weight, query_bias, key_weight, key_bias, value_weight, value_bias,
    out_weight, out_bias, up_weight, up_bias, down_weight, down_bias,
):
    nf, nc, nt = lax.axis_size("fsdp"), lax.axis_size("ctx"), lax.axis_size("tp")
    ci, ti = lax.axis_index("ctx").astype(jnp.int32), lax.axis_index("tp").astype(jnp.int32)
    seqs, rows, width = tokens.shape
    own_seqs = seqs // nt
    length = rows * nc
    own = own_seqs * rows
    db = width // nf
    inner = query_weight.shape[1] // nc
    units = up_weight.shape[1] // nc
    pairs = inner // PAIR

    def columns(w):
        return lax.dynamic_slice_in_dim(w, ci * (w.shape[-1] // nc), w.shape[-1] // nc, axis=-1)

    def by_pairs(arrays):
        return jnp.concatenate(
            [a[..., p * PAIR : (p + 1) * PAIR] for p in range(pairs) for a in arrays], axis=-1
        )

    x = lax.dynamic_slice_in_dim(tokens, ti * own_seqs, own_seqs, axis=0).reshape(own, width)
    g_own = lax.dynamic_slice_in_dim(cotangent, ti * own_seqs, own_seqs, axis=0).reshape(own, width)
    x = x.astype(F32)
    gain, shift = ln_gain.astype(F32), ln_bias.astype(F32)
    centred = x - jnp.mean(x, axis=-1, keepdims=True)
    inv_std = lax.rsqrt(jnp.mean(centred * centred, axis=-1, keepdims=True) + EPS)
    normed = centred * inv_std
    h_own = (normed * gain + shift).astype(BF16)

    def side(blocks):
        return blocks[-1] if len(blocks) > 1 else (blocks[0], blocks[0])

    def gather_on(blocks):
        return blocks + [gather_step(side(blocks), len(blocks), nc)]

    cut = [
        (1 + n, p * PAIR, PAIR) for p in range(pairs) for n in range(3)
    ]
    col_sum = lambda a: jnp.sum(a.astype(F32), axis=0)
    h_own, g_cols = meet((h_own, col_sum(g_own)))
    h_in = [[piece] for piece in jnp.split(h_own, 2)]
    g_cols = total([g_cols] + [xor_swap(g_cols, "tp", nt, k) for k in range(1, nt)])
    g_cols, early = meet(
        (g_cols, (up_weight, query_weight, key_weight, value_weight, down_weight, out_weight))
    )
    first = pack_columns(early[:4], [(0, 0, units)] + cut, ci, nc, nf)
    second = pack_columns(early[4:], [(0, 0, units), (1, 0, inner)], ci, nc, nf)
    b_qkv = by_pairs([columns(query_bias), columns(key_bias), columns(value_bias)]).astype(F32)
    b_up = columns(up_bias).astype(F32)

    lane = jnp.arange(PAIR, dtype=jnp.int32)[None, :] % HD
    freq = jnp.power(10000.0, -2.0 * (lane % HALF).astype(F32) / ROT)
    angle = jnp.arange(length, dtype=jnp.int32).astype(F32)[:, None] * freq
    cos = jnp.where(lane < ROT, jnp.cos(angle), 1.0)
    sin = jnp.sin(angle)
    sa = jnp.where(lane < HALF, -sin, 0.0)
    sb = jnp.where((lane >= HALF) & (lane < ROT), sin, 0.0)
    groups = group_order.shape[0]
    glen = length // groups
    places = jnp.arange(groups, dtype=jnp.int32)
    slot = jnp.sum(
        jnp.where(group_order[None, :] == places[:, None], places[None, :], 0), axis=1
    ) * glen
    offs = slot
    seq_ids = jnp.arange(seqs, dtype=jnp.int32)
    seq_of = ((seq_ids // own_seqs) ^ ti) * own_seqs + seq_ids % own_seqs
    prefix = jnp.sum(
        jnp.where(seq_of[:, None] == seq_ids[None, :], prefix_len[None, :], 0), axis=1
    )
    offs, prefix = offs.astype(jnp.int32), prefix.astype(jnp.int32)

    tables = (cos, sa, sb)
    first_all = lax.all_to_all(first, "fsdp", 0, 0, tiled=True)
    h_in = [gather_on(h) for h in h_in]
    h_in[0], second, tables, b_up, b_qkv, offs, prefix = meet(
        (h_in[0], second, tables, b_up, b_qkv, offs, prefix)
    )
    while len(h_in[0]) < nc:
        h_in = [gather_on(h) for h in h_in]
    g_own, h_in = meet((g_own, h_in))
    g_all = lax.all_gather(g_own.reshape(own_seqs, rows, width), "ctx", axis=1, tiled=True)

    def halves(mine):
        mine = mine.reshape(own_seqs * length, width)
        return [mine] + [xor_swap(mine, "tp", nt, k) for k in range(1, nt)]

    def send_rows(full):
        return lax.all_to_all(full, "fsdp", 0, 0, tiled=True)

    def sum_rows(got):
        return total([got[k] for k in range(nf)]).astype(BF16)

    def gather_cols(mine):
        return lax.all_gather(mine, "ctx", axis=0, tiled=False)

    h_mine = jnp.moveaxis(in_order(h_in, ci).reshape(nc, own_seqs, rows, width), 1, 0)
    hidden = halves(h_mine)
    hidden, first_all = meet((hidden, first_all))
    w_first = first_all.reshape(width, units + 3 * inner)
    second_all = lax.all_to_all(second, "fsdp", 0, 0, tiled=True)
    ups, qkv = [], []
    for n in range(nt):
        ups.append(up_product(hidden[n], w_first, b_up))
        ups, hidden = meet((ups, hidden))
    for n in range(nt):
        qkv.append(line_product(hidden[n], w_first, b_qkv, units, 3))
        qkv, hidden = meet((qkv, hidden))
    act, slope = [u[0] for u in ups], [u[1] for u in ups]

    def attend_half(n, qkv):
        out = []
        for i in range(own_seqs):
            at = slice(i * length, (i + 1) * length)
            m = n * own_seqs + i
            out.append(attend(qkv[at], offs, prefix[m : m + 1], tables))
        return out

    def back_half(n, kept, grad_context):
        out = []
        for i in range(own_seqs):
            at = slice(i * length, (i + 1) * length)
            m = n * own_seqs + i
            out.append(
                attend_back(
                    kept[i][1], kept[i][2], grad_context[at], offs, prefix[m : m + 1], tables
                )
            )
        return jnp.concatenate(out)

    def parts_of(mine, got):
        grid = lambda a: a.reshape(own_seqs, nc, rows, width)
        mine, got = grid(mine), [grid(g) for g in got]

        def parts(m):
            at = (ci - m + nc) % nc
            pick = lambda a: lax.dynamic_index_in_dim(a, at, 1, keepdims=False).reshape(own, width)
            return [pick(mine)] + [pick(g) for g in got]

        return parts

    others = range(1, nt)
    kept = [None] * nt
    for n in others:
        kept[n] = attend_half(n, qkv[n])
    kept[1:], qkv, act, second_all = meet((kept[1:], qkv, act, second_all))
    w_second = second_all.reshape(width, units + inner)
    context = [None] + [jnp.concatenate([c[0] for c in kept[n]]) for n in others]
    theirs, qkv = meet(([pair_product(act[n], context[n], w_second) for n in others], qkv))
    o_got = [xor_swap(t, "tp", nt, n) for n, t in zip(others, theirs)]
    kept[0], act, o_got, g_all = meet((attend_half(0, qkv[0]), act, o_got, g_all))
    grad = halves(g_all)
    context[0] = jnp.concatenate([c[0] for c in kept[0]])
    both = pair_product(act[0], context[0], w_second, o_got)
    both = jnp.moveaxis(both.reshape(own_seqs, nc, rows, width), 1, 0).reshape(nc, own, width)
    grad, act, both = meet((grad, act, both))
    o_sum = lax.psum_scatter(both, "ctx", scatter_dimension=0, tiled=True)

    full_down = rows_product([(grad, act)], nf)
    grad, full_down, slope = meet((grad, full_down, slope))
    d_rows = send_rows(full_down)
    downs = []
    for n in range(nt):
        downs.append(down_product(grad[n], w_second, slope[n]))
        downs, grad, hidden = meet((downs, grad, hidden))
    dup, grad_context = [d[0] for d in downs], [d[1] for d in downs]
    full_up = rows_product([(hidden, dup)], nf)
    full_up, kept, grad_context = meet((full_up, kept, grad_context))
    dqkv = [None] + [back_half(n, kept[n], grad_context[n]) for n in others]
    dqkv[1:], d_rows, dup = meet((dqkv[1:], d_rows, dup))
    d_sum, dup = meet((sum_rows(d_rows), dup))
    d_cols = gather_cols(d_sum)
    u_rows = send_rows(full_up)

    theirs, kept, grad_context = meet(
        ([pair_product(dup[n], dqkv[n], w_first) for n in others], kept, grad_context)
    )
    h_got = [xor_swap(t, "tp", nt, n) for n, t in zip(others, theirs)]
    dqkv[0], o_sum, h_got = meet((back_half(0, kept[0], grad_context[0]), o_sum, h_got))
    h_both, dqkv, hidden = meet(
        (pair_product(dup[0], dqkv[0], w_first, h_got), dqkv, hidden)
    )
    qo_full = rows_product([(hidden, dqkv), (grad, context)], nf)
    qo_full, u_rows = meet((qo_full, u_rows))
    u_sum, d_cols = meet((sum_rows(u_rows), d_cols))
    qo = send_rows(qo_full)
    u_cols = gather_cols(u_sum)
    h_parts = parts_of(h_both, [])
    dw_down = widen(d_cols)
    h_sum, qo, dw_down = meet((sum_step(None, h_parts, 1, nc), qo, dw_down))
    qo_sum = sum_rows(qo)
    for k in range(2, nc):
        h_sum = sum_step(h_sum, h_parts, k, nc)
        if k == 2:
            h_sum, qo_sum = meet((h_sum, qo_sum))
        h_sum = meet(h_sum)
    grad_hidden = total(h_parts(0) + list(h_sum))
    u_cols, h_sum = meet((u_cols, h_sum))
    dw_up = widen(u_cols)
    grad_hidden, dw_up = meet((grad_hidden, dw_up))
    qo_cols = gather_cols(qo_sum)
    col_sum = lambda a: jnp.sum(a.astype(F32), axis=0)
    out_own = total([x, o_sum.reshape(own, width), out_bias, down_bias])

    gs = grad_hidden * gain
    grad_normed = inv_std * (
        gs - jnp.mean(gs, axis=-1, keepdims=True)
        - normed * jnp.mean(gs * normed, axis=-1, keepdims=True)
    )
    in_own = g_own.astype(F32) + grad_normed
    norm_sums = jnp.concatenate([col_sum(grad_hidden * normed), col_sum(grad_hidden)])

    def whole_tokens(own_rows):
        mine = own_rows.astype(BF16).reshape(1, own_seqs, rows, width)
        pieces = [mine] + [xor_swap(mine, "tp", nt, k) for k in range(1, nt)]
        full = jnp.zeros((nt, own_seqs, rows, width), BF16)
        for k in range(nt):
            full = lax.dynamic_update_slice_in_dim(full, pieces[k], ti ^ k, axis=0)
        return full.reshape(seqs, rows, width)

    output = whole_tokens(out_own)
    input_grad = whole_tokens(in_own)

    dw_qkv = place(qo_cols, pairs)

    bias_sums = jnp.concatenate(
        [total([col_sum(a) for a in array]) for array in (dqkv, dup)]
    )[None]
    bias_sums = jnp.sum(to_all(bias_sums, "fsdp", nf).reshape(nf, -1), axis=0)
    small = 3 * inner + units
    got = to_all(jnp.concatenate([bias_sums, norm_sums, g_cols])[None], "ctx", nc).reshape(nc, -1)
    qkv_sums = got[:, : 3 * inner].reshape(nc, pairs, 3, PAIR)
    qb, kb, vb = (qkv_sums[:, :, n].reshape(nc * inner) for n in range(3))
    ub = got[:, 3 * inner : small].reshape(nc * units)
    sums = jnp.sum(got[:, small:], axis=0)[None]
    sums = jnp.sum(to_all(sums, "fsdp", nf).reshape(nf, -1), axis=0)
    norm_sums, obias = sums[: 2 * width], sums[2 * width :]
    norm_sums = total([norm_sums] + [xor_swap(norm_sums, "tp", nt, k) for k in range(1, nt)])
    norm_sums = norm_sums.reshape(2, width)

    return (
        output, input_grad, norm_sums[0], norm_sums[1],
        dw_qkv[0], qb, dw_qkv[1], kb, dw_qkv[2], vb,
        dw_qkv[3], dw_up, ub, dw_down, obias,
    )


def solution(mesh):
    rows, flat, cols, one = P("fsdp", "ctx", None), P("fsdp", "tp"), P("tp"), P()
    return jax.shard_map(
        local,
        mesh=mesh,
        in_specs=(
            rows, rows, P("fsdp"), one, one, one,
            flat, cols, flat, cols, flat, cols, flat, one, flat, cols, flat, one,
        ),
        out_specs=(
            rows, rows, one, one, flat, cols, flat, cols, flat, cols, flat, flat, cols, flat, one,
        ),
        check_vma=False,
    )
```

```python
import functools

import jax
import jax.numpy as jnp
from jax import lax
from jax.experimental import pallas as pl
from jax.experimental.pallas import tpu as pltpu
from jax.sharding import PartitionSpec as P

HD = 64
ROT = 32
HALF = ROT // 2
PAIR = 2 * HD
NEG = -1e30
EPS = 1e-05
LOG2E = 1.4426950408889634
GELU_C = 0.7978845608028654
GELU_A = 0.044715
F32 = jnp.float32
BF16 = jnp.bfloat16


def meet(tree):
    return lax.optimization_barrier(tree)


def total(addends):
    out = addends[0].astype(F32)
    for one in addends[1:]:
        out = out + one.astype(F32)
    return out


def xor_swap(value, axis, size, step):
    return lax.ppermute(value, axis, [(j, j ^ step) for j in range(size)])


def to_all(value, axis, size):
    return lax.all_to_all(jnp.broadcast_to(value[None], (size,) + value.shape), axis, 0, 0, tiled=True)


def gather_step(sides, step, size, axis="ctx"):
    left, right = sides
    return (
        lax.ppermute(left, axis, [(j, j + 1) for j in range(step - 1, size - 1)]),
        lax.ppermute(right, axis, [(j, j - 1) for j in range(1, size - step + 1)]),
    )


def sum_step(sides, parts, step, size, axis="ctx"):
    a, b = parts(step), parts(size - step)
    if sides is not None:
        a, b = a + [sides[0]], b + [sides[1]]
    return (
        lax.ppermute(
            total(a).astype(BF16), axis, [(j, j + 1) for j in range(min(step, size - 1))]
        ),
        lax.ppermute(
            total(b).astype(BF16), axis, [(j, j - 1) for j in range(max(size - step, 1), size)]
        ),
    )


def by_distance(blocks, here):
    n = len(blocks)
    return [blocks[0]] + [
        jnp.where(here >= m, blocks[m][0], blocks[n - m][1]) for m in range(1, n)
    ]


def in_hbm(arrays):
    return [pltpu.with_memory_space_constraint(a, pltpu.HBM) for a in arrays]


FREE = pl.CostEstimate(flops=1, transcendentals=0, bytes_accessed=1)


def rotate(x, cos, sa, sb):
    return (
        x * cos + pltpu.roll(x, PAIR - HALF, axis=1) * sa + pltpu.roll(x, HALF, axis=1) * sb
    )


def masked_scores(k_s, qt, prefix, first, reach, clear):
    s = jnp.dot(k_s[0:reach, :], qt, preferred_element_type=F32) * LOG2E
    count = qt.shape[1]
    kpos = clear + lax.broadcasted_iota(jnp.int32, (reach - clear, count), 0)
    qpos = first + lax.broadcasted_iota(jnp.int32, (1, count), 1)
    tail = jnp.where(kpos < jnp.maximum(qpos + 1, prefix), s[clear:reach], NEG)
    return jnp.concatenate([s[:clear], tail], axis=0) if clear else tail


def spans(length, qblock, most):
    for first in range(0, length, qblock):
        yield first, max(first + qblock, most), first if first >= most else 0


def keep_head(x, h):
    lane = lax.broadcasted_iota(jnp.int32, x.shape, 1)
    return jnp.where((lane >= h * HD) & (lane < (h + 1) * HD), x, 0.0)


def attend_kernel(
    glen, qblock, most,
    offs_ref, prefix_ref,
    qkv_ref, cos_ref, sa_ref, sb_ref,
    ctx_ref, sorted_ref, stat_ref,
    qtm, k_s, vt_s, ot,
):
    length = cos_ref.shape[0]
    for p in range(length // glen):
        rows = pl.ds(pl.multiple_of(offs_ref[p], glen), glen)
        to = slice(p * glen, (p + 1) * glen)
        cos, sa, sb = cos_ref[to, :], sa_ref[to, :], sb_ref[to, :]
        q = rotate(qkv_ref[rows, 0:PAIR], cos, sa, sb).astype(BF16).astype(F32) * (HD**-0.5)
        sorted_ref[to, 0:PAIR] = q.astype(BF16)
        k = rotate(qkv_ref[rows, PAIR : 2 * PAIR], cos, sa, sb).astype(BF16)
        k_s[to, :] = k
        sorted_ref[to, PAIR : 2 * PAIR] = k
        sorted_ref[to, 2 * PAIR : 3 * PAIR] = qkv_ref[rows, 2 * PAIR : 3 * PAIR].astype(BF16)
    q = sorted_ref[:, 0:PAIR].astype(F32)
    for h in range(2):
        qtm[h] = keep_head(q, h).astype(BF16).T
    vt_s[...] = sorted_ref[:, 2 * PAIR : 3 * PAIR].T.reshape(2, HD, length)
    prefix = prefix_ref[0]
    for first, reach, clear in spans(length, qblock, most):
        cols = slice(first, first + qblock)

        def head(h, _):
            s = masked_scores(k_s, qtm[h, :, cols], prefix, first, reach, clear)
            top = jnp.max(s, axis=0, keepdims=True)
            e = jnp.exp2(s - top)
            scale = 1.0 / jnp.sum(e, axis=0, keepdims=True)
            stat_ref[0, h, 0:1, cols] = top
            stat_ref[0, h, 1:2, cols] = scale
            low = (e * scale).astype(BF16)
            ot[h, :, cols] = jnp.dot(vt_s[h, :, 0:reach], low, preferred_element_type=F32)
            return 0

        lax.fori_loop(0, 2, head, 0, unroll=True)
    for p in range(length // glen):
        rows = pl.ds(pl.multiple_of(offs_ref[p], glen), glen)
        to = slice(p * glen, (p + 1) * glen)
        ctx_ref[rows, :] = ot[:, :, to].reshape(PAIR, glen).T.astype(BF16)


def attend_back_kernel(
    glen, qblock, most,
    offs_ref, prefix_ref,
    sorted_ref, stat_ref, do_ref, cos_ref, sa_ref, sb_ref,
    dqkv_ref,
    qm, qtm, k_s, kt_s, v_s, dom, dotm, dqt, dk_acc, dv_acc,
):
    length = cos_ref.shape[0]
    k_s[...] = sorted_ref[:, PAIR : 2 * PAIR]
    v_s[...] = sorted_ref[:, 2 * PAIR : 3 * PAIR]
    q = sorted_ref[:, 0:PAIR].astype(F32)
    for p in range(length // glen):
        rows = pl.ds(pl.multiple_of(offs_ref[p], glen), glen)
        to = slice(p * glen, (p + 1) * glen)
        do = do_ref[rows, :].astype(F32)
        for h in range(2):
            dom[h, to, :] = keep_head(do, h).astype(BF16)
    for h in range(2):
        qm[h] = keep_head(q, h).astype(BF16)
        qtm[h] = qm[h].T
        dotm[h] = dom[h].T
    kt_s[...] = k_s[...].T.reshape(2, HD, length)
    dk_acc[...] = jnp.zeros_like(dk_acc)
    dv_acc[...] = jnp.zeros_like(dv_acc)
    prefix = prefix_ref[0]
    dot = functools.partial(jnp.dot, preferred_element_type=F32)
    for first, reach, clear in spans(length, qblock, most):
        cols = slice(first, first + qblock)

        def head(h, _):
            s = masked_scores(k_s, qtm[h, :, cols], prefix, first, reach, clear)
            prob = jnp.exp2(s - stat_ref[0, h, 0:1, cols]) * stat_ref[0, h, 1:2, cols]
            dv_acc[0:reach, :] += dot(prob.astype(BF16), dom[h, cols, :])
            dp = dot(v_s[0:reach, :], dotm[h, :, cols])
            delta = jnp.sum(prob * dp, axis=0, keepdims=True)
            ds = (prob * (dp - delta)).astype(BF16)
            dqt[h, :, cols] = dot(kt_s[h, :, 0:reach], ds)
            dk_acc[0:reach, :] += dot(ds, qm[h, cols, :])
            return 0

        lax.fori_loop(0, 2, head, 0, unroll=True)
    for p in range(length // glen):
        rows = pl.ds(pl.multiple_of(offs_ref[p], glen), glen)
        to = slice(p * glen, (p + 1) * glen)
        cos, sa, sb = cos_ref[to, :], -sa_ref[to, :], -sb_ref[to, :]
        dq = dqt[:, :, to].reshape(PAIR, glen).T * (HD**-0.5)
        dqkv_ref[rows, 0:PAIR] = rotate(dq, cos, sa, sb).astype(BF16)
        dqkv_ref[rows, PAIR : 2 * PAIR] = rotate(dk_acc[to, :], cos, sa, sb).astype(BF16)
        dqkv_ref[rows, 2 * PAIR : 3 * PAIR] = dv_acc[to, :].astype(BF16)


def attention_specs(length):
    whole = pl.BlockSpec((length, PAIR), lambda p, *_: (0, 0))
    wide = pl.BlockSpec((length, 3 * PAIR), lambda p, *_: (0, p))
    narrow = pl.BlockSpec((length, PAIR), lambda p, *_: (0, p))
    stat = pl.BlockSpec((1, 2, 2, length), lambda p, *_: (p, 0, 0, 0))
    return whole, wide, narrow, stat


def attend(qkv, offs, prefix, tables):
    length, inner = qkv.shape[0], qkv.shape[1] // 3
    whole, wide, narrow, stat = attention_specs(length)
    vm = pltpu.VMEM
    return pl.pallas_call(
        functools.partial(attend_kernel, length // offs.shape[0], min(512, length), length // 2),
        out_shape=(
            jax.ShapeDtypeStruct((length, inner), BF16),
            jax.ShapeDtypeStruct((length, 3 * inner), BF16),
            jax.ShapeDtypeStruct((inner // PAIR, 2, 2, length), F32),
        ),
        grid_spec=pltpu.PrefetchScalarGridSpec(
            num_scalar_prefetch=2,
            grid=(inner // PAIR,),
            in_specs=[wide, whole, whole, whole],
            out_specs=(narrow, wide, stat),
            scratch_shapes=[
                vm((2, PAIR, length), BF16),
                vm((length, PAIR), BF16),
                vm((2, HD, length), BF16),
                vm((2, HD, length), F32),
            ],
        ),
        compiler_params=pltpu.CompilerParams(vmem_limit_bytes=40 << 20),
        cost_estimate=FREE,
        name="attend",
    )(offs, prefix, qkv, *tables)


def attend_back(ordered, stats, grad_context, offs, prefix, tables):
    length, inner = grad_context.shape
    whole, wide, narrow, stat = attention_specs(length)
    vm = pltpu.VMEM
    return pl.pallas_call(
        functools.partial(
            attend_back_kernel, length // offs.shape[0], min(256, length), length // 2
        ),
        out_shape=jax.ShapeDtypeStruct((length, 3 * inner), BF16),
        grid_spec=pltpu.PrefetchScalarGridSpec(
            num_scalar_prefetch=2,
            grid=(inner // PAIR,),
            in_specs=[wide, stat, narrow, whole, whole, whole],
            out_specs=wide,
            scratch_shapes=[
                vm((2, length, PAIR), BF16),
                vm((2, PAIR, length), BF16),
                vm((length, PAIR), BF16),
                vm((2, HD, length), BF16),
                vm((length, PAIR), BF16),
                vm((2, length, PAIR), BF16),
                vm((2, PAIR, length), BF16),
                vm((2, HD, length), F32),
                vm((length, PAIR), F32),
                vm((length, PAIR), F32),
            ],
        ),
        compiler_params=pltpu.CompilerParams(vmem_limit_bytes=40 << 20),
        cost_estimate=FREE,
        name="attend_back",
    )(offs, prefix, ordered, stats, grad_context, *tables)


def pair_kernel(split, a_ref, b_ref, w_ref, *refs):
    nt = (((1,), (1,)), ((), ()))
    o = lax.dot_general(a_ref[...], w_ref[:, :split], nt, preferred_element_type=F32)
    o += lax.dot_general(b_ref[...], w_ref[:, split:], nt, preferred_element_type=F32)
    for more in refs[:-1]:
        o += more[...].astype(F32)
    refs[-1][...] = o.astype(refs[-1].dtype)


def pair_product(a, b, w, more=()):
    n, depth = w.shape
    m = a.shape[0]
    bn = min(512, n)
    out = pl.BlockSpec((m, bn), lambda j: (0, j))
    return pl.pallas_call(
        functools.partial(pair_kernel, a.shape[1]),
        out_shape=jax.ShapeDtypeStruct((m, n), BF16),
        grid=(n // bn,),
        in_specs=[
            pl.BlockSpec((m, a.shape[1]), lambda j: (0, 0), pipeline_mode=pl.Buffered(1)),
            pl.BlockSpec((m, b.shape[1]), lambda j: (0, 0), pipeline_mode=pl.Buffered(1)),
            pl.BlockSpec((bn, depth), lambda j: (j, 0)),
        ]
        + [out] * len(more),
        out_specs=out,
        compiler_params=pltpu.CompilerParams(vmem_limit_bytes=48 << 20),
        cost_estimate=FREE,
        name="pair_product",
    )(a, b, w, *more)


def pack_kernel(pieces, here_ref, *refs):
    o_ref = refs[-1]
    at = 0
    for n, start, size in pieces:
        o_ref[0, :, at : at + size] = refs[n][:, start : start + size]
        at += size


def pack_columns(weights, pieces, here, places, copies):
    rows = weights[0].shape[0]
    span = sum(size for _, _, size in pieces)
    return pl.pallas_call(
        functools.partial(pack_kernel, pieces),
        out_shape=jax.ShapeDtypeStruct((copies, rows, span), weights[0].dtype),
        grid_spec=pltpu.PrefetchScalarGridSpec(
            num_scalar_prefetch=1,
            grid=(copies,),
            in_specs=[
                pl.BlockSpec((rows, w.shape[1] // places), lambda i, h: (0, h[0])) for w in weights
            ],
            out_specs=pl.BlockSpec((1, rows, span), lambda i, h: (i, 0, 0)),
        ),
        compiler_params=pltpu.CompilerParams(vmem_limit_bytes=40 << 20),
        cost_estimate=FREE,
        name="pack_columns",
    )(here.reshape(1), *in_hbm(weights))


def rows_kernel(counts, *refs):
    o_ref = refs[-1]
    tn = (((0,), (0,)), ((), ()))
    at, col = 0, 0
    for count in counts:
        o = 0.0
        for n in range(count):
            o += lax.dot_general(
                refs[at + n][...], refs[at + count + n][...], tn, preferred_element_type=F32
            )
        o_ref[0, :, col : col + o.shape[1]] = o.astype(o_ref.dtype)
        at, col = at + 2 * count, col + o.shape[1]


def rows_product(products, owners):
    args, specs, columns = [], [], 0
    for a, b in products:
        bm = a[0].shape[1] // owners
        args += [*a, *b]
        specs += [pl.BlockSpec((x.shape[0], bm), lambda i: (0, i)) for x in a]
        specs += [
            pl.BlockSpec(x.shape, lambda i: (0, 0), pipeline_mode=pl.Buffered(1)) for x in b
        ]
        columns += b[0].shape[1]
    return pl.pallas_call(
        functools.partial(rows_kernel, [len(a) for a, _ in products]),
        out_shape=jax.ShapeDtypeStruct((owners, bm, columns), BF16),
        grid=(owners,),
        in_specs=specs,
        out_specs=pl.BlockSpec((1, bm, columns), lambda i: (i, 0, 0)),
        compiler_params=pltpu.CompilerParams(vmem_limit_bytes=56 << 20),
        cost_estimate=FREE,
        name="rows_product",
    )(*args)


def order_kernel(size, pieces, here_ref, *refs):
    blocks, o_ref = refs[:-1], refs[-1]
    m, piece, here = pl.program_id(0), pl.program_id(1), here_ref[0]

    def put(ref):
        o_ref[0] = ref[...]

    for p in range(pieces):
        mine = blocks[p * (2 * size - 1) : (p + 1) * (2 * size - 1)]
        pl.when((piece == p) & (m == 0))(functools.partial(put, mine[0]))
        for k in range(1, size):
            at = (piece == p) & (m == k)
            pl.when(at & (here >= k))(functools.partial(put, mine[k]))
            pl.when(at & (here < k))(functools.partial(put, mine[2 * size - 1 - k]))


def in_order(pieces, here):
    size = len(pieces[0])
    rows, span = pieces[0][0].shape
    flat = []
    for one in pieces:
        flat += [one[0]] + [x[0] for x in one[1:]] + [x[1] for x in one[1:]]
    return pl.pallas_call(
        functools.partial(order_kernel, size, len(pieces)),
        out_shape=jax.ShapeDtypeStruct((size, len(pieces) * rows, span), flat[0].dtype),
        grid_spec=pltpu.PrefetchScalarGridSpec(
            num_scalar_prefetch=1,
            grid=(size, len(pieces)),
            in_specs=[
                pl.BlockSpec((rows, span), lambda m, p, h: (0, 0), pipeline_mode=pl.Buffered(1))
            ]
            * len(flat),
            out_specs=pl.BlockSpec(
                (1, rows, span), lambda m, p, h: (lax.rem(h[0] - m + size, size), p, 0)
            ),
        ),
        compiler_params=pltpu.CompilerParams(vmem_limit_bytes=48 << 20),
        cost_estimate=FREE,
        name="in_order",
    )(here.reshape(1), *in_hbm(flat))


def place_kernel(pairs, a_ref, *outs):
    starts = [[(p * 3 + n) * PAIR for p in range(pairs)] for n in range(3)]
    starts.append([(3 * pairs + p) * PAIR for p in range(pairs)])
    for out, at in zip(outs, starts):
        for p in range(pairs):
            out[:, p * PAIR : (p + 1) * PAIR] = a_ref[0, :, at[p] : at[p] + PAIR].astype(F32)


def place(blocks, pairs):
    n, rows, span = blocks.shape
    width = pairs * PAIR
    return pl.pallas_call(
        functools.partial(place_kernel, pairs),
        out_shape=(jax.ShapeDtypeStruct((rows, n * width), F32),) * 4,
        grid=(n,),
        in_specs=[pl.BlockSpec((1, rows, span), lambda c: (c, 0, 0))],
        out_specs=(pl.BlockSpec((rows, width), lambda c: (0, c)),) * 4,
        compiler_params=pltpu.CompilerParams(vmem_limit_bytes=48 << 20),
        cost_estimate=FREE,
        name="place",
    )(*in_hbm([blocks]))


def widen_kernel(a_ref, o_ref):
    o_ref[...] = a_ref[0].astype(F32)


def widen(blocks):
    n, rows, span = blocks.shape
    return pl.pallas_call(
        widen_kernel,
        out_shape=jax.ShapeDtypeStruct((rows, n * span), F32),
        grid=(n,),
        in_specs=[pl.BlockSpec((1, rows, span), lambda c: (c, 0, 0))],
        out_specs=pl.BlockSpec((rows, span), lambda c: (0, c)),
        compiler_params=pltpu.CompilerParams(vmem_limit_bytes=40 << 20),
        cost_estimate=FREE,
        name="widen",
    )(*in_hbm([blocks]))


def up_kernel(step, h_ref, w_ref, b_ref, act_ref, slope_ref):
    for c in range(0, act_ref.shape[1], step):
        up = jnp.dot(h_ref[...], w_ref[:, c : c + step], preferred_element_type=F32)
        act, slope = gelu_parts(up + b_ref[:, c : c + step])
        act_ref[:, c : c + step] = act.astype(BF16)
        slope_ref[:, c : c + step] = slope.astype(BF16)


def up_product(hidden, weight, bias):
    m, k = hidden.shape
    n = bias.shape[0]
    bm = min(512, m)
    return pl.pallas_call(
        functools.partial(up_kernel, min(256, n)),
        out_shape=(jax.ShapeDtypeStruct((m, n), BF16),) * 2,
        grid=(m // bm,),
        in_specs=[
            pl.BlockSpec((bm, k), lambda i: (i, 0)),
            pl.BlockSpec((k, n), lambda i: (0, 0), pipeline_mode=pl.Buffered(1)),
            pl.BlockSpec((1, n), lambda i: (0, 0)),
        ],
        out_specs=(pl.BlockSpec((bm, n), lambda i: (i, 0)),) * 2,
        compiler_params=pltpu.CompilerParams(vmem_limit_bytes=56 << 20),
        cost_estimate=FREE,
        name="up_product",
    )(hidden, weight, bias.reshape(1, n))


def down_kernel(units, g_ref, w_ref, s_ref, d_ref, c_ref):
    g = g_ref[...]
    d = jnp.dot(g, w_ref[:, :units], preferred_element_type=F32)
    d_ref[...] = (d * s_ref[...].astype(F32)).astype(BF16)
    c_ref[...] = jnp.dot(g, w_ref[:, units:], preferred_element_type=F32).astype(BF16)


def down_product(grad, weight, slope):
    m, k = grad.shape
    units, n = slope.shape[1], weight.shape[1]
    bm = min(512, m)
    return pl.pallas_call(
        functools.partial(down_kernel, units),
        out_shape=(
            jax.ShapeDtypeStruct((m, units), BF16),
            jax.ShapeDtypeStruct((m, n - units), BF16),
        ),
        grid=(m // bm,),
        in_specs=[
            pl.BlockSpec((bm, k), lambda i: (i, 0)),
            pl.BlockSpec((k, n), lambda i: (0, 0), pipeline_mode=pl.Buffered(1)),
            pl.BlockSpec((bm, units), lambda i: (i, 0)),
        ],
        out_specs=(
            pl.BlockSpec((bm, units), lambda i: (i, 0)),
            pl.BlockSpec((bm, n - units), lambda i: (i, 0)),
        ),
        compiler_params=pltpu.CompilerParams(vmem_limit_bytes=56 << 20),
        cost_estimate=FREE,
        name="down_product",
    )(grad, weight, slope)


def line_kernel(pieces, h_ref, *refs):
    b_ref, o_ref = refs[pieces], refs[-1]
    span = o_ref.shape[1] // pieces
    for n in range(pieces):
        to = slice(n * span, (n + 1) * span)
        o = jnp.dot(h_ref[...], refs[n][...], preferred_element_type=F32)
        o_ref[:, to] = o + b_ref[:, to]


def line_product(hidden, weight, bias, start, pieces):
    m, k = hidden.shape
    n = bias.shape[0]
    span = n // pieces
    bm = min(512, m)
    piece = lambda p: pl.BlockSpec(
        (k, span), lambda i: (0, start // span + p), pipeline_mode=pl.Buffered(1)
    )
    return pl.pallas_call(
        functools.partial(line_kernel, pieces),
        out_shape=jax.ShapeDtypeStruct((m, n), F32),
        grid=(m // bm,),
        in_specs=[pl.BlockSpec((bm, k), lambda i: (i, 0))]
        + [piece(p) for p in range(pieces)]
        + [pl.BlockSpec((1, n), lambda i: (0, 0))],
        out_specs=pl.BlockSpec((bm, n), lambda i: (i, 0)),
        compiler_params=pltpu.CompilerParams(vmem_limit_bytes=56 << 20),
        cost_estimate=FREE,
        name="line_product",
    )(hidden, *[weight] * pieces, bias.reshape(1, n))


def gelu_parts(up):
    square = up * up
    t = jnp.tanh(GELU_C * up * (1.0 + GELU_A * square))
    half = 0.5 * (1.0 + t)
    slope = half + 0.5 * up * (1.0 - t * t) * (GELU_C * (1.0 + 3.0 * GELU_A * square))
    return up * half, slope


def local(
    tokens, cotangent, prefix_len, group_order, ln_gain, ln_bias,
    query_weight, query_bias, key_weight, key_bias, value_weight, value_bias,
    out_weight, out_bias, up_weight, up_bias, down_weight, down_bias,
):
    nf, nc, nt = lax.axis_size("fsdp"), lax.axis_size("ctx"), lax.axis_size("tp")
    ci, ti = lax.axis_index("ctx").astype(jnp.int32), lax.axis_index("tp").astype(jnp.int32)
    seqs, rows, width = tokens.shape
    own_seqs = seqs // nt
    length = rows * nc
    own = own_seqs * rows
    db = width // nf
    inner = query_weight.shape[1] // nc
    units = up_weight.shape[1] // nc
    pairs = inner // PAIR

    def columns(w):
        return lax.dynamic_slice_in_dim(w, ci * (w.shape[-1] // nc), w.shape[-1] // nc, axis=-1)

    def by_pairs(arrays):
        return jnp.concatenate(
            [a[..., p * PAIR : (p + 1) * PAIR] for p in range(pairs) for a in arrays], axis=-1
        )

    x = lax.dynamic_slice_in_dim(tokens, ti * own_seqs, own_seqs, axis=0).reshape(own, width)
    g_own = lax.dynamic_slice_in_dim(cotangent, ti * own_seqs, own_seqs, axis=0).reshape(own, width)
    x = x.astype(F32)
    gain, shift = ln_gain.astype(F32), ln_bias.astype(F32)
    centred = x - jnp.mean(x, axis=-1, keepdims=True)
    inv_std = lax.rsqrt(jnp.mean(centred * centred, axis=-1, keepdims=True) + EPS)
    normed = centred * inv_std
    h_own = (normed * gain + shift).astype(BF16)

    def side(blocks):
        return blocks[-1] if len(blocks) > 1 else (blocks[0], blocks[0])

    def gather_on(blocks):
        return blocks + [gather_step(side(blocks), len(blocks), nc)]

    cut = [
        (1 + n, p * PAIR, PAIR) for p in range(pairs) for n in range(3)
    ]
    col_sum = lambda a: jnp.sum(a.astype(F32), axis=0)
    h_own, g_cols = meet((h_own, col_sum(g_own)))
    h_in = [[piece] for piece in jnp.split(h_own, 2)]
    g_cols = total([g_cols] + [xor_swap(g_cols, "tp", nt, k) for k in range(1, nt)])
    g_cols, early = meet(
        (g_cols, (up_weight, query_weight, key_weight, value_weight, down_weight, out_weight))
    )
    first = pack_columns(early[:4], [(0, 0, units)] + cut, ci, nc, nf)
    second = pack_columns(early[4:], [(0, 0, units), (1, 0, inner)], ci, nc, nf)
    b_qkv = by_pairs([columns(query_bias), columns(key_bias), columns(value_bias)]).astype(F32)
    b_up = columns(up_bias).astype(F32)

    lane = jnp.arange(PAIR, dtype=jnp.int32)[None, :] % HD
    freq = jnp.power(10000.0, -2.0 * (lane % HALF).astype(F32) / ROT)
    angle = jnp.arange(length, dtype=jnp.int32).astype(F32)[:, None] * freq
    cos = jnp.where(lane < ROT, jnp.cos(angle), 1.0)
    sin = jnp.sin(angle)
    sa = jnp.where(lane < HALF, -sin, 0.0)
    sb = jnp.where((lane >= HALF) & (lane < ROT), sin, 0.0)
    groups = group_order.shape[0]
    glen = length // groups
    places = jnp.arange(groups, dtype=jnp.int32)
    slot = jnp.sum(
        jnp.where(group_order[None, :] == places[:, None], places[None, :], 0), axis=1
    ) * glen
    offs = slot
    seq_ids = jnp.arange(seqs, dtype=jnp.int32)
    seq_of = ((seq_ids // own_seqs) ^ ti) * own_seqs + seq_ids % own_seqs
    prefix = jnp.sum(
        jnp.where(seq_of[:, None] == seq_ids[None, :], prefix_len[None, :], 0), axis=1
    )
    offs, prefix = offs.astype(jnp.int32), prefix.astype(jnp.int32)

    tables = (cos, sa, sb)
    first_all = lax.all_to_all(first, "fsdp", 0, 0, tiled=True)
    h_in = [gather_on(h) for h in h_in]
    h_in[0], second, tables, b_up, b_qkv, offs, prefix = meet(
        (h_in[0], second, tables, b_up, b_qkv, offs, prefix)
    )
    while len(h_in[0]) < nc:
        h_in = [gather_on(h) for h in h_in]
    g_own, h_in = meet((g_own, h_in))
    g_all = lax.all_gather(g_own.reshape(own_seqs, rows, width), "ctx", axis=1, tiled=True)

    def halves(mine):
        mine = mine.reshape(own_seqs * length, width)
        return [mine] + [xor_swap(mine, "tp", nt, k) for k in range(1, nt)]

    def send_rows(full):
        return lax.all_to_all(full, "fsdp", 0, 0, tiled=True)

    def sum_rows(got):
        return total([got[k] for k in range(nf)]).astype(BF16)

    def gather_cols(mine):
        return lax.all_gather(mine, "ctx", axis=0, tiled=False)

    h_mine = jnp.moveaxis(in_order(h_in, ci).reshape(nc, own_seqs, rows, width), 1, 0)
    hidden = halves(h_mine)
    hidden, first_all = meet((hidden, first_all))
    w_first = first_all.reshape(width, units + 3 * inner)
    second_all = lax.all_to_all(second, "fsdp", 0, 0, tiled=True)
    ups, qkv = [], []
    for n in range(nt):
        ups.append(up_product(hidden[n], w_first, b_up))
        ups, hidden = meet((ups, hidden))
    for n in range(nt):
        qkv.append(line_product(hidden[n], w_first, b_qkv, units, 3))
        qkv, hidden = meet((qkv, hidden))
    act, slope = [u[0] for u in ups], [u[1] for u in ups]

    def attend_half(n, qkv):
        out = []
        for i in range(own_seqs):
            at = slice(i * length, (i + 1) * length)
            m = n * own_seqs + i
            out.append(attend(qkv[at], offs, prefix[m : m + 1], tables))
        return out

    def back_half(n, kept, grad_context):
        out = []
        for i in range(own_seqs):
            at = slice(i * length, (i + 1) * length)
            m = n * own_seqs + i
            out.append(
                attend_back(
                    kept[i][1], kept[i][2], grad_context[at], offs, prefix[m : m + 1], tables
                )
            )
        return jnp.concatenate(out)

    def parts_of(mine, got):
        grid = lambda a: a.reshape(own_seqs, nc, rows, width)
        mine, got = grid(mine), [grid(g) for g in got]

        def parts(m):
            at = (ci - m + nc) % nc
            pick = lambda a: lax.dynamic_index_in_dim(a, at, 1, keepdims=False).reshape(own, width)
            return [pick(mine)] + [pick(g) for g in got]

        return parts

    others = range(1, nt)
    kept = [None] * nt
    for n in others:
        kept[n] = attend_half(n, qkv[n])
    kept[1:], qkv, act, second_all = meet((kept[1:], qkv, act, second_all))
    w_second = second_all.reshape(width, units + inner)
    context = [None] + [jnp.concatenate([c[0] for c in kept[n]]) for n in others]
    theirs, qkv = meet(([pair_product(act[n], context[n], w_second) for n in others], qkv))
    o_got = [xor_swap(t, "tp", nt, n) for n, t in zip(others, theirs)]
    kept[0], act, o_got, g_all = meet((attend_half(0, qkv[0]), act, o_got, g_all))
    grad = halves(g_all)
    context[0] = jnp.concatenate([c[0] for c in kept[0]])
    both = pair_product(act[0], context[0], w_second, o_got)
    both = jnp.moveaxis(both.reshape(own_seqs, nc, rows, width), 1, 0).reshape(nc, own, width)
    grad, act, both = meet((grad, act, both))
    o_sum = lax.psum_scatter(both, "ctx", scatter_dimension=0, tiled=True)

    full_down = rows_product([(grad, act)], nf)
    grad, full_down, slope = meet((grad, full_down, slope))
    d_rows = send_rows(full_down)
    downs = []
    for n in range(nt):
        downs.append(down_product(grad[n], w_second, slope[n]))
        downs, grad, hidden = meet((downs, grad, hidden))
    dup, grad_context = [d[0] for d in downs], [d[1] for d in downs]
    full_up = rows_product([(hidden, dup)], nf)
    full_up, kept, grad_context = meet((full_up, kept, grad_context))
    dqkv = [None] + [back_half(n, kept[n], grad_context[n]) for n in others]
    dqkv[1:], d_rows, dup = meet((dqkv[1:], d_rows, dup))
    d_sum, dup = meet((sum_rows(d_rows), dup))
    d_cols = gather_cols(d_sum)
    u_rows = send_rows(full_up)

    theirs, kept, grad_context = meet(
        ([pair_product(dup[n], dqkv[n], w_first) for n in others], kept, grad_context)
    )
    h_got = [xor_swap(t, "tp", nt, n) for n, t in zip(others, theirs)]
    dqkv[0], o_sum, h_got = meet((back_half(0, kept[0], grad_context[0]), o_sum, h_got))
    h_both, dqkv, hidden = meet(
        (pair_product(dup[0], dqkv[0], w_first, h_got), dqkv, hidden)
    )
    qo_full = rows_product([(hidden, dqkv), (grad, context)], nf)
    qo_full, u_rows = meet((qo_full, u_rows))
    u_sum, d_cols = meet((sum_rows(u_rows), d_cols))
    qo = send_rows(qo_full)
    u_cols = gather_cols(u_sum)
    h_parts = parts_of(h_both, [])
    dw_down = widen(d_cols)
    h_sum, qo, dw_down = meet((sum_step(None, h_parts, 1, nc), qo, dw_down))
    qo_sum = sum_rows(qo)
    for k in range(2, nc):
        h_sum = sum_step(h_sum, h_parts, k, nc)
        if k == 2:
            h_sum, qo_sum = meet((h_sum, qo_sum))
        h_sum = meet(h_sum)
    grad_hidden = total(h_parts(0) + list(h_sum))
    u_cols, h_sum = meet((u_cols, h_sum))
    dw_up = widen(u_cols)
    grad_hidden, dw_up = meet((grad_hidden, dw_up))
    qo_cols = gather_cols(qo_sum)
    col_sum = lambda a: jnp.sum(a.astype(F32), axis=0)
    out_own = total([x, o_sum.reshape(own, width), out_bias, down_bias])

    gs = grad_hidden * gain
    grad_normed = inv_std * (
        gs - jnp.mean(gs, axis=-1, keepdims=True)
        - normed * jnp.mean(gs * normed, axis=-1, keepdims=True)
    )
    in_own = g_own.astype(F32) + grad_normed
    norm_sums = jnp.concatenate([col_sum(grad_hidden * normed), col_sum(grad_hidden)])

    def whole_tokens(own_rows):
        mine = own_rows.astype(BF16).reshape(1, own_seqs, rows, width)
        pieces = [mine] + [xor_swap(mine, "tp", nt, k) for k in range(1, nt)]
        full = jnp.zeros((nt, own_seqs, rows, width), BF16)
        for k in range(nt):
            full = lax.dynamic_update_slice_in_dim(full, pieces[k], ti ^ k, axis=0)
        return full.reshape(seqs, rows, width)

    output = whole_tokens(out_own)
    input_grad = whole_tokens(in_own)

    dw_qkv = place(qo_cols, pairs)

    bias_sums = jnp.concatenate(
        [total([col_sum(a) for a in array]) for array in (dqkv, dup)]
    )[None]
    bias_sums = jnp.sum(to_all(bias_sums, "fsdp", nf).reshape(nf, -1), axis=0)
    small = 3 * inner + units
    got = to_all(jnp.concatenate([bias_sums, norm_sums, g_cols])[None], "ctx", nc).reshape(nc, -1)
    qkv_sums = got[:, : 3 * inner].reshape(nc, pairs, 3, PAIR)
    qb, kb, vb = (qkv_sums[:, :, n].reshape(nc * inner) for n in range(3))
    ub = got[:, 3 * inner : small].reshape(nc * units)
    sums = jnp.sum(got[:, small:], axis=0)[None]
    sums = jnp.sum(to_all(sums, "fsdp", nf).reshape(nf, -1), axis=0)
    norm_sums, obias = sums[: 2 * width], sums[2 * width :]
    norm_sums = total([norm_sums] + [xor_swap(norm_sums, "tp", nt, k) for k in range(1, nt)])
    norm_sums = norm_sums.reshape(2, width)

    return (
        output, input_grad, norm_sums[0], norm_sums[1],
        dw_qkv[0], qb, dw_qkv[1], kb, dw_qkv[2], vb,
        dw_qkv[3], dw_up, ub, dw_down, obias,
    )


def solution(mesh):
    rows, flat, cols, one = P("fsdp", "ctx", None), P("fsdp", "tp"), P("tp"), P()
    return jax.shard_map(
        local,
        mesh=mesh,
        in_specs=(
            rows, rows, P("fsdp"), one, one, one,
            flat, cols, flat, cols, flat, cols, flat, one, flat, cols, flat, one,
        ),
        out_specs=(
            rows, rows, one, one, flat, cols, flat, cols, flat, cols, flat, flat, cols, flat, one,
        ),
        check_vma=False,
    )
```
